32 devices in a mesh: gx: 4 (over y, x), gz: 8 (over z, core).
Axes of the slice: x: 2, y: 2, z: 4, core: 2. Of those that a mesh axis runs over, the one named last changes fastest.
Arguments:
- pop_ratio: float32 [19, 16, 64, 512], P(None, None, 'gz', 'gx'), may hold values from 0.6 to 1.4
- solid_blocks: int32 [4, 16, 128], P(None, 'gz', 'gx'), may hold values 0 or 1
- shift_whole: int32 [2], replicated, may hold values from 0 to 511
- shift_frac: int32 [2], replicated, may hold values from 0 to 4095
Outputs:
- populations: float32 [19, 16, 64, 512], P(None, None, 'gz', 'gx')
- accumulated: float32 [2, 16, 64, 512], P(None, None, 'gz', 'gx')
- profiles: float32 [2, 16, 64], P(None, None, 'gz')
The draws below stay inside these ranges and needn't reach their ends.
Inputs may be any that keep to these rules, and one draw needn't show every extreme that they name: `shift_whole`: whole cells of the displacement, below 512.
All inputs are finite; a program needn't handle non-finite values. No bound on the sum of `solid_blocks` on one device may be relied on, other than what follows from the above.
Results may differ from the reference program's by a relative error of at most 0.00023.
Values sent between devices are 32-bit elements; how exact they have to be, the bound alone decides.
No kernel may reach another device: no remote copies, remote signals or barrier semaphores. Data moves between devices by JAX's collectives and lax.ppermute only.
A program may use at most 64 MiB of HBM per device.

```python
import jax
import jax.numpy as jnp
import numpy as np
from jax import lax

NY = 16
QDIR = 19
STEPS = 2
BLOCK = 4
NX = 512
NZ = 64


def plant(drawn, key, smallest, largest):
    place = [jax.random.randint(jax.random.fold_in(key, axis), (), 0, length) for axis, length in enumerate(drawn.shape)]
    widest = drawn.shape.index(max(drawn.shape))
    neighbour = place[:widest] + [(place[widest] + 1) % drawn.shape[widest]] + place[widest + 1:]
    return drawn.at[tuple(place)].set(smallest).at[tuple(neighbour)].set(largest)


def block_scale(key, dims, shards, least, top_value):
    def one(position, shards_of):
        steps = jax.random.uniform(jax.random.fold_in(jax.random.fold_in(key, 6), position), (shards_of,), jnp.float32, least / len(shards), top_value / len(shards))
        return jnp.repeat(jnp.exp(steps), dims[position] // shards_of).reshape((-1,) + (1,) * (len(dims) - position - 1))

    factor_of = one(*shards[0])
    for cut in shards[1:]:
        factor_of = factor_of * one(*cut)
    return factor_of


def setup_inputs(seed: int = 0) -> dict:
    key_list = jax.random.split(jax.random.key(seed), 5)
    pop_ratio = jnp.clip(0.6 + 0.79999995 * jax.random.uniform(key_list[0], (QDIR, NY, NZ, NX), jnp.float32) ** block_scale(key_list[0], (QDIR, NY, NZ, NX), ((2, 8), (3, 4)), -0.2, 0.2), 0.6, 1.4)
    solid_blocks = plant((jax.random.randint(key_list[1], (NY // BLOCK, NZ // BLOCK, NX // BLOCK), 0, 3) < 1).astype(jnp.int32), jax.random.fold_in(key_list[1], 1), 0, 1)
    shift_whole = jax.random.randint(key_list[2], (STEPS,), 0, NX).astype(jnp.int32)
    shift_frac = jax.random.randint(key_list[3], (STEPS,), 0, 4096).astype(jnp.int32)
    return {"pop_ratio": pop_ratio, "solid_blocks": solid_blocks, "shift_whole": shift_whole, "shift_frac": shift_frac}


velocity_list = [(0, 0, 0), (1, 0, 0), (-1, 0, 0), (0, 1, 0), (0, -1, 0), (0, 0, 1), (0, 0, -1), (1, 1, 0), (-1, -1, 0), (1, -1, 0), (-1, 1, 0), (1, 0, 1), (-1, 0, -1), (1, 0, -1), (-1, 0, 1), (0, 1, 1), (0, -1, -1), (0, 1, -1), (0, -1, 1)]
velocities = np.array(velocity_list)
lattice_weights = np.array([1.0 / 3.0] + [1.0 / 18.0] * 6 + [1.0 / 36.0] * 12)
opposite = np.array([velocity_list.index((-entry[0], -entry[1], -entry[2])) for entry in velocity_list])
rising = [index for index in range(19) if velocities[index, 1] == 1]
falling = [index for index in range(19) if velocities[index, 1] == -1]
wall_speed = 0.08
visc_rate = 1.25
fraction_unit = 4096.0
relax_rates = np.array([0.0, 1.19, 1.4, 0.0, 1.2, 0.0, 1.2, 0.0, 1.2, 1.25, 1.4, 1.25, 1.4, 1.25, 1.25, 1.25, 1.98, 1.98, 1.98])


def moment_rows():
    vel_x = velocities[:, 0] * 1.0
    vel_y = velocities[:, 1] * 1.0
    vel_z = velocities[:, 2] * 1.0
    speed_sq = vel_x * vel_x + vel_y * vel_y + vel_z * vel_z
    rows = [np.ones(19), 19 * speed_sq - 30, (21 * speed_sq * speed_sq - 53 * speed_sq + 24) / 2,
            vel_x, (5 * speed_sq - 9) * vel_x, vel_y, (5 * speed_sq - 9) * vel_y, vel_z, (5 * speed_sq - 9) * vel_z,
            3 * vel_x * vel_x - speed_sq, (3 * speed_sq - 5) * (3 * vel_x * vel_x - speed_sq),
            vel_y * vel_y - vel_z * vel_z, (3 * speed_sq - 5) * (vel_y * vel_y - vel_z * vel_z),
            vel_x * vel_y, vel_y * vel_z, vel_x * vel_z,
            (vel_y * vel_y - vel_z * vel_z) * vel_x, (vel_z * vel_z - vel_x * vel_x) * vel_y, (vel_x * vel_x - vel_y * vel_y) * vel_z]
    return np.stack(rows)


def relax_matrix():
    moments = moment_rows()
    scaled = moments.T / np.sum(moments * moments, axis=1)
    return (scaled @ (relax_rates[:, None] * moments)).astype(np.float32)


def column(values):
    return jnp.asarray(np.asarray(values, dtype=np.float32).reshape(-1, 1, 1, 1))


def plane_column(values):
    return jnp.asarray(np.asarray(values, dtype=np.float32).reshape(-1, 1, 1))


def expand(blocks):
    deep, tall, wide = blocks.shape
    big = jnp.broadcast_to(blocks[:, None, :, None, :, None], (deep, BLOCK, tall, BLOCK, wide, BLOCK))
    return big.reshape(deep * BLOCK, tall * BLOCK, wide * BLOCK).astype(jnp.float32)


def collide(popul, solid):
    rho = jnp.sum(popul, axis=0)
    mom_x = jnp.sum(column(velocities[:, 0]) * popul, axis=0)
    mom_y = jnp.sum(column(velocities[:, 1]) * popul, axis=0)
    mom_z = jnp.sum(column(velocities[:, 2]) * popul, axis=0)
    inverse = 1.0 / rho
    vel_x = mom_x * inverse
    vel_y = mom_y * inverse
    vel_z = mom_z * inverse
    along = column(velocities[:, 0]) * vel_x + column(velocities[:, 1]) * vel_y + column(velocities[:, 2]) * vel_z
    speed_sq = vel_x * vel_x + vel_y * vel_y + vel_z * vel_z
    equil = column(lattice_weights) * rho * (1.0 + 3.0 * along + 4.5 * along * along - 1.5 * speed_sq)
    noneq = popul - equil
    relaxed = jnp.dot(jnp.asarray(relax_matrix()), noneq.reshape(19, -1), precision=lax.Precision.HIGHEST).reshape(popul.shape)
    post = jnp.where(solid > 0, popul[opposite], popul - relaxed)
    fluid = 1.0 - solid
    stress = -(1.0 - 0.5 * visc_rate) * jnp.sum(column(velocities[:, 0] * velocities[:, 1]) * noneq, axis=0)
    return post, jnp.stack([fluid * mom_x, fluid * stress])


def assemble(shifted, le_top, le_bot):
    pieces = []
    for index in range(19):
        lift = velocities[index, 1]
        if lift == 0:
            pieces.append(shifted[index])
        elif lift > 0:
            pieces.append(jnp.concatenate([le_top[rising.index(index)][None], shifted[index, :-1]], axis=0))
        else:
            pieces.append(jnp.concatenate([shifted[index, 1:], le_bot[falling.index(index)][None]], axis=0))
    return jnp.stack(pieces)


def reference(pop_ratio, solid_blocks, shift_whole, shift_frac):
    popul = pop_ratio * column(lattice_weights)
    solid = expand(solid_blocks)
    accumulated = jnp.zeros((2,) + popul.shape[1:], jnp.float32)
    top_fix = plane_column(6.0 * lattice_weights[rising] * velocities[rising, 0] * wall_speed)
    bot_fix = plane_column(6.0 * lattice_weights[falling] * velocities[falling, 0] * wall_speed)
    for step in range(STEPS):
        post, fields = collide(popul, solid)
        accumulated = accumulated + fields
        shifted = jnp.stack([jnp.roll(post[index], (int(velocities[index, 2]), int(velocities[index, 0])), axis=(1, 2)) for index in range(19)])
        whole = shift_whole[step].astype(jnp.int32)
        weight = shift_frac[step].astype(jnp.float32) / fraction_unit
        top = shifted[np.array(rising), NY - 1]
        bot = shifted[np.array(falling), 0]
        le_top = (1.0 - weight) * jnp.roll(top, -whole, axis=2) + weight * jnp.roll(top, -whole - 1, axis=2) - top_fix
        le_bot = (1.0 - weight) * jnp.roll(bot, whole, axis=2) + weight * jnp.roll(bot, whole + 1, axis=2) + bot_fix
        popul = assemble(shifted, le_top, le_bot)
    return popul, accumulated, jnp.sum(accumulated, axis=3)
```

```python
import functools

import jax
import jax.numpy as jnp
import numpy as np
from jax import lax
from jax.experimental import pallas as pl
from jax.experimental.pallas import tpu as pltpu
from jax.sharding import PartitionSpec as P

BLOCK = 4
velocity_list = [
    (0, 0, 0),
    (1, 0, 0),
    (-1, 0, 0),
    (0, 1, 0),
    (0, -1, 0),
    (0, 0, 1),
    (0, 0, -1),
    (1, 1, 0),
    (-1, -1, 0),
    (1, -1, 0),
    (-1, 1, 0),
    (1, 0, 1),
    (-1, 0, -1),
    (1, 0, -1),
    (-1, 0, 1),
    (0, 1, 1),
    (0, -1, -1),
    (0, 1, -1),
    (0, -1, 1),
]
Q = len(velocity_list)
weights = [1.0 / 3.0] + [1.0 / 18.0] * 6 + [1.0 / 36.0] * 12
CX = [v[0] for v in velocity_list]
CY = [v[1] for v in velocity_list]
CZ = [v[2] for v in velocity_list]
opposite = [velocity_list.index((-x, -y, -z)) for x, y, z in velocity_list]
mirror = [velocity_list.index((x, y, -z)) for x, y, z in velocity_list]
rising = [i for i in range(Q) if CY[i] == 1]
falling = [i for i in range(Q) if CY[i] == -1]
eastward = [i for i in range(Q) if CX[i] == 1]
westward = [i for i in range(Q) if CX[i] == -1]
upward = [i for i in range(Q) if CZ[i] == 1]
level = [i for i in range(Q) if CZ[i] == 0]
near_list = level + upward
near_slot = {i: s for s, i in enumerate(near_list)}
far_slot = {i: len(near_list) + s for s, i in enumerate(upward)}
MASK_SLOT = Q
wall_speed = 0.08
visc_rate = 1.25
fraction_unit = 4096.0
relax_rates = [0.0, 1.19, 1.4, 0.0, 1.2, 0.0, 1.2, 0.0, 1.2, 1.25, 1.4, 1.25, 1.4]
relax_rates += [1.25, 1.25, 1.25, 1.98, 1.98, 1.98]


def row_norms():
    v = np.array(velocity_list, dtype=np.float64)
    x, y, z = v[:, 0], v[:, 1], v[:, 2]
    s = x * x + y * y + z * z
    rows = [
        np.ones(Q),
        19 * s - 30,
        (21 * s * s - 53 * s + 24) / 2,
        x,
        (5 * s - 9) * x,
        y,
        (5 * s - 9) * y,
        z,
        (5 * s - 9) * z,
        3 * x * x - s,
        (3 * s - 5) * (3 * x * x - s),
        y * y - z * z,
        (3 * s - 5) * (y * y - z * z),
        x * y,
        y * z,
        x * z,
        (y * y - z * z) * x,
        (z * z - x * x) * y,
        (x * x - y * y) * z,
    ]
    return [float(np.sum(row * row)) for row in rows]


RATE = [rate / norm for rate, norm in zip(relax_rates, row_norms())]


def collide(f, solid):
    sums = {i: f[i] + f[i + 1] for i in range(1, Q, 2)}
    difs = {i: f[i] - f[i + 1] for i in range(1, Q, 2)}
    p1, d1 = sums[7] + sums[9], sums[7] - sums[9]
    p2, d2 = sums[11] + sums[13], sums[11] - sums[13]
    p3, d3 = sums[15] + sums[17], sums[15] - sums[17]
    s23 = sums[3] + sums[5]
    axis = sums[1] + s23
    p12 = p1 + p2
    diag = p12 + p3
    rho = f[0] + axis + diag
    inverse = 1.0 / rho
    a, c = difs[7] + difs[9], difs[7] - difs[9]
    b, e = difs[11] + difs[13], difs[11] - difs[13]
    d, g = difs[15] + difs[17], difs[15] - difs[17]
    ab, cd, eg = a + b, c + d, e + g
    jx, jy, jz = difs[1] + ab, difs[3] + cd, difs[5] + eg
    ux, uy, uz = jx * inverse, jy * inverse, jz * inverse
    xx, yy, zz = jx * ux, jy * uy, jz * uz
    yz_sum, yz_dif = yy + zz, yy - zz
    square = xx + yz_sum

    even_e = RATE[1] * (8.0 * diag - 11.0 * axis - 30.0 * f[0] + 11.0 * rho - 19.0 * square)
    even_s = RATE[2] * (12.0 * f[0] - 4.0 * axis + diag - 3.0 * rho + 5.5 * square)
    axis_x, diag_x = 2.0 * sums[1] - s23, p12 - 2.0 * p3
    eq_x = 2.0 * xx - yz_sum
    even_x = RATE[9] * (axis_x + diag_x - eq_x)
    even_px = RATE[10] * (diag_x - 2.0 * axis_x + 0.5 * eq_x)
    axis_w, diag_w = sums[3] - sums[5], p1 - p2
    even_w = RATE[11] * (axis_w + diag_w - yz_dif)
    even_pw = RATE[12] * (diag_w - 2.0 * axis_w + 0.5 * yz_dif)
    moment_xy = d1 - jx * uy
    even_xy = RATE[13] * moment_xy
    even_yz = RATE[14] * (d3 - jy * uz)
    even_xz = RATE[15] * (d2 - jx * uz)
    flow_x = RATE[4] * (ab - 4.0 * difs[1] + (2.0 / 3.0) * jx)
    flow_y = RATE[6] * (cd - 4.0 * difs[3] + (2.0 / 3.0) * jy)
    flow_z = RATE[8] * (eg - 4.0 * difs[5] + (2.0 / 3.0) * jz)
    twist_x = RATE[16] * (a - b)
    twist_y = RATE[17] * (d - c)
    twist_z = RATE[18] * (e - g)

    base_axis = -11.0 * even_e - 4.0 * even_s
    base_diag = 8.0 * even_e + even_s
    lean = even_x - 2.0 * even_px
    tilt = even_w - 2.0 * even_pw
    side_x = even_x + even_px
    side_w = even_w + even_pw
    flat = base_diag + side_x
    diag_xy, diag_xz = flat + side_w, flat - side_w
    diag_yz = base_diag - 2.0 * side_x
    low = base_axis - lean
    even = {
        1: base_axis + 2.0 * lean,
        3: low + tilt,
        5: low - tilt,
        7: diag_xy + even_xy,
        9: diag_xy - even_xy,
        11: diag_xz + even_xz,
        13: diag_xz - even_xz,
        15: diag_yz + even_yz,
        17: diag_yz - even_yz,
    }
    x_up, x_down = flow_x + twist_x, flow_x - twist_x
    y_up, y_down = flow_y + twist_y, flow_y - twist_y
    z_up, z_down = flow_z + twist_z, flow_z - twist_z
    odd = {
        1: -4.0 * flow_x,
        3: -4.0 * flow_y,
        5: -4.0 * flow_z,
        7: x_up + y_down,
        9: x_up - y_down,
        11: x_down + z_up,
        13: x_down - z_up,
        15: y_up + z_down,
        17: y_up - z_down,
    }
    post = [None] * Q
    post[0] = jnp.where(solid, f[0], f[0] + 30.0 * even_e - 12.0 * even_s)
    for i in range(1, Q, 2):
        post[i] = jnp.where(solid, f[i + 1], f[i] - (even[i] + odd[i]))
        post[i + 1] = jnp.where(solid, f[i], f[i + 1] - (even[i] - odd[i]))
    return post, jx, moment_xy


class Sizes:
    def __init__(self, planes, depth, width, count):
        self.planes, self.depth, self.width, self.count = planes, depth, width, count
        self.deep, self.wide = depth // BLOCK, width // BLOCK
        assert count >= 4 and count & (count - 1) == 0
        assert len(eastward) * planes + 4 <= width and 2 * planes <= width

    def slots(self, delta):
        return (2 if delta == self.count // 2 else 1) * len(rising) + 1

    def tile(self, ref, i, y):
        return ref[i, pl.ds(y * self.depth, self.depth), :]

    def lanes(self):
        return lax.broadcasted_iota(jnp.int32, (self.depth, self.width), 1)

    def rows(self):
        return lax.broadcasted_iota(jnp.int32, (self.depth, self.width), 0)

    def spread(self, row):
        return jnp.broadcast_to(row, (self.depth, self.width))

    def solid_tile(self, mask_ref, y):
        base = y // BLOCK * self.deep
        out = self.spread(mask_ref[base : base + 1, :])
        rows = self.rows()
        for step in range(1, self.deep):
            line = self.spread(mask_ref[base + step : base + step + 1, :])
            out = jnp.where(rows >= step * BLOCK, line, out)
        return out


def roll(value, shift, axis=1):
    shift = shift % value.shape[axis]
    return pltpu.roll(value, shift, axis) if shift else value


def edge_columns(z):
    return [
        (7, z.planes - 1, True),
        (10, z.planes - 1, False),
        (9, 0, True),
        (8, 0, False),
    ]


def wall_columns(z, ref, lanes):
    out = jnp.zeros((z.depth, z.width), jnp.float32)
    start = len(eastward) * z.planes
    for k, (i, y, right) in enumerate(edge_columns(z)):
        at = start + k
        moved = roll(z.tile(ref, i, y), at - (z.width - 1 if right else 0))
        out = jnp.where(lanes == at, moved, out)
    return out


def pack_x(z, whole, ref, sends, extra=None):
    me = lax.axis_index("gx")
    lanes = z.lanes()
    right_edge = wall_columns(z, ref, lanes)
    left_edge = right_edge
    for j in range(len(eastward)):
        for y in range(z.planes):
            at = j * z.planes + y
            hit = lanes == at
            moved = roll(z.tile(ref, eastward[j], y), at - (z.width - 1))
            right_edge = jnp.where(hit, moved, right_edge)
            moved = roll(z.tile(ref, westward[j], y), at)
            left_edge = jnp.where(hit, moved, left_edge)
    far = lax.div(whole, z.width)
    for delta in range(1, z.count):
        send = sends[delta - 1]
        partner = jnp.bitwise_xor(me, delta)
        ahead = lax.rem(me - partner + z.count, z.count)
        at_top = (ahead == far) | (ahead == lax.rem(far + 1, z.count))
        for s in range(len(rising)):
            top = z.tile(ref, rising[s], z.planes - 1)
            bottom = z.tile(ref, falling[s], 0)
            if delta == z.count // 2:
                send[s] = top
                send[len(rising) + s] = bottom
            else:
                send[s] = jnp.where(at_top, top, bottom)
        to_right = partner == lax.rem(me + 1, z.count)
        slots = z.slots(delta)
        send[slots - 1] = jnp.where(to_right, right_edge, left_edge)
        if extra is not None:
            send[slots] = extra


def shift_xy(z, whole, part, ref, gets, out, tops, bottoms, edges):
    me = lax.axis_index("gx")
    lanes = z.lanes()
    last = z.width - 1
    for s in range(len(rising)):
        tops[me, s] = z.tile(ref, rising[s], z.planes - 1)
        bottoms[me, s] = z.tile(ref, falling[s], 0)
    edges[me] = wall_columns(z, ref, lanes)
    for delta in range(1, z.count):
        get = gets[delta - 1]
        partner = jnp.bitwise_xor(me, delta)
        for s in range(len(rising)):
            tops[partner, s] = get[s]
            second = len(rising) + s if delta == z.count // 2 else s
            bottoms[partner, s] = get[second]
        edges[partner] = get[z.slots(delta) - 1]

    left = edges[lax.rem(me + z.count - 1, z.count)]
    right = edges[lax.rem(me + 1, z.count)]

    def moved(i, y):
        value = z.tile(ref, i, y)
        if CX[i] == 1:
            at = eastward.index(i) * z.planes + y
            return jnp.where(lanes == 0, roll(left, -at), roll(value, 1))
        if CX[i] == -1:
            at = westward.index(i) * z.planes + y
            return jnp.where(lanes == last, roll(right, last - at), roll(value, -1))
        return value

    for i in range(Q):
        for y in range(z.planes):
            source = y - CY[i]
            if 0 <= source < z.planes:
                out[i, pl.ds(y * z.depth, z.depth), :] = moved(i, source)

    weight = part.astype(jnp.float32) / fraction_unit
    far = lax.div(whole, z.width)
    rest = lax.rem(whole, z.width)
    start = len(eastward) * z.planes
    columns = {i: start + k for k, (i, _, _) in enumerate(edge_columns(z))}

    def window(i, planes, s, block, offset):
        pair = []
        for step in range(2):
            here = lax.rem(block + step, z.count)
            value = planes[here, s]
            if CX[i] == 1:
                side = edges[lax.rem(here + z.count - 1, z.count)]
                value = jnp.where(lanes == 0, roll(side, -columns[i]), roll(value, 1))
            elif CX[i] == -1:
                side = edges[lax.rem(here + 1, z.count)]
                value = jnp.where(lanes == last, roll(side, last - columns[i]), roll(value, -1))
            pair.append(value)
        first = jnp.where(lanes >= offset, pair[0], pair[1])
        second = jnp.where(lanes > offset, pair[0], pair[1])
        first = pltpu.roll(first, lax.rem(z.width - offset, z.width), 1)
        second = pltpu.roll(second, last - offset, 1)
        return first, second

    for s, i in enumerate(rising):
        near, next_one = window(i, tops, s, lax.rem(me + far, z.count), rest)
        fix = 6.0 * weights[i] * CX[i] * wall_speed
        value = (1.0 - weight) * near + weight * next_one
        out[i, pl.ds(0, z.depth), :] = value - fix if CX[i] else value
    for s, i in enumerate(falling):
        block = lax.rem(me + 2 * z.count - far - 1, z.count)
        next_one, near = window(i, bottoms, s, block, last - rest)
        fix = 6.0 * weights[i] * CX[i] * wall_speed
        value = (1.0 - weight) * near + weight * next_one
        out[i, pl.ds((z.planes - 1) * z.depth, z.depth), :] = value + fix if CX[i] else value


def first_kernel(z, whole_ref, pop_ref, solid_ref, post_ref, acc_ref, mask_ref, *sends):
    grow = lax.broadcasted_iota(jnp.int32, (z.wide, z.width), 1) // BLOCK
    grow = grow == lax.broadcasted_iota(jnp.int32, (z.wide, z.width), 0)
    grow = grow.astype(jnp.float32)
    for k in range(solid_ref.shape[0]):
        flags = jnp.where(solid_ref[k] > 0, 1.0, 0.0)
        line = jnp.dot(flags, grow, preferred_element_type=jnp.float32)
        mask_ref[pl.ds(k * z.deep, z.deep), :] = line
    for y in range(z.planes):
        solid = z.solid_tile(mask_ref, y) > 0.5
        f = [z.tile(pop_ref, i, y) * np.float32(weights[i]) for i in range(Q)]
        post, jx, moment_xy = collide(f, solid)
        here = pl.ds(y * z.depth, z.depth)
        for i in range(Q):
            post_ref[i, here, :] = post[i]
        acc_ref[0, here, :] = jnp.where(solid, 0.0, jx)
        acc_ref[1, here, :] = jnp.where(solid, 0.0, -(1.0 - 0.5 * visc_rate) * moment_xy)
    pack_x(z, whole_ref[0], post_ref, sends)


def second_kernel(z, whole_ref, part_ref, post_ref, mask_ref, *refs):
    gets, (h_ref, inner_ref, outer_ref), scratch = refs[: z.count - 1], refs[z.count - 1 : z.count + 2], refs[z.count + 2 :]
    shift_xy(z, whole_ref[0], part_ref[0], post_ref, gets, h_ref, *scratch)
    even = lax.rem(lax.axis_index("gz"), 2) == 0

    def line(i, row):
        return h_ref[i, pl.ds(row, z.planes, stride=z.depth), :]

    def put(slot, up, down):
        inner_ref[slot] = jnp.where(even, up, down)
        outer_ref[slot] = jnp.where(even, down, up)

    for i in near_list:
        put(near_slot[i], line(i, z.depth - 1), line(mirror[i], 0))
    for i in upward:
        put(far_slot[i], line(i, z.depth - 2), line(mirror[i], 1))
    for k in range(z.planes // BLOCK):
        up = mask_ref[(k + 1) * z.deep - 1 : (k + 1) * z.deep, :]
        down = mask_ref[k * z.deep : k * z.deep + 1, :]
        shape = (BLOCK, z.width)
        here = pl.ds(k * BLOCK, BLOCK)
        inner_ref[MASK_SLOT, here, :] = jnp.broadcast_to(jnp.where(even, up, down), shape)
        outer_ref[MASK_SLOT, here, :] = jnp.broadcast_to(jnp.where(even, down, up), shape)


def third_kernel(z, whole_ref, h_ref, inner_ref, outer_ref, mask_ref, old_ref, *refs):
    (g_ref, acc_ref, part_ref), sends = refs[:3], refs[3 : 2 + z.count]
    sides, extra = refs[2 + z.count :]
    even = lax.rem(lax.axis_index("gz"), 2) == 0
    sides[jnp.where(even, 1, 0)] = inner_ref[...]
    sides[jnp.where(even, 0, 1)] = outer_ref[...]
    chunk = min(8, z.planes)
    for side in range(2):
        for start in range(0, z.planes, chunk):
            here = pl.ds(start, chunk)
            f = [None] * Q
            for i in range(Q):
                k = i if side == 0 else mirror[i]
                if CZ[k] == 0:
                    f[i] = sides[side, near_slot[k], here, :]
                elif CZ[k] == 1:
                    f[i] = sides[side, far_slot[k], here, :]
                else:
                    row = start * z.depth + (0 if side == 0 else z.depth - 1)
                    f[i] = h_ref[i, pl.ds(row, chunk, stride=z.depth), :]
            post, _, _ = collide(f, sides[side, MASK_SLOT, here, :] > 0.5)
            for s, i in enumerate(upward):
                extra[side, s, here, :] = post[i if side == 0 else mirror[i]]
    rows, lanes = z.rows(), z.lanes()

    def moved(i, y, value, table, slot):
        if CZ[i] == 1:
            line = z.spread(table[0, slot(i), pl.ds(y, 1), :])
            return jnp.where(rows == 0, line, roll(value, 1, 0))
        if CZ[i] == -1:
            line = z.spread(table[1, slot(mirror[i]), pl.ds(y, 1), :])
            return jnp.where(rows == z.depth - 1, line, roll(value, -1, 0))
        return value

    sums = jnp.zeros((z.depth, z.width), jnp.float32)
    for y in range(z.planes):
        solid = z.solid_tile(mask_ref, y) > 0.5
        f = [moved(i, y, z.tile(h_ref, i, y), sides, near_slot.get) for i in range(Q)]
        post, jx, moment_xy = collide(f, solid)
        here = pl.ds(y * z.depth, z.depth)
        for i in range(Q):
            g_ref[i, here, :] = moved(i, y, post[i], extra, upward.index)
        fields = [jx, -(1.0 - 0.5 * visc_rate) * moment_xy]
        for k in range(2):
            value = old_ref[k, here, :] + jnp.where(solid, 0.0, fields[k])
            acc_ref[k, here, :] = value
            total = z.spread(jnp.sum(value, axis=1, keepdims=True))
            sums = jnp.where(lanes == k * z.planes + y, total, sums)
    part_ref[...] = sums
    pack_x(z, whole_ref[1], g_ref, sends, sums)


def fourth_kernel(z, whole_ref, part_ref, g_ref, own_ref, *refs):
    gets, (out_ref, profile_ref), scratch = refs[: z.count - 1], refs[z.count - 1 : z.count + 1], refs[z.count + 1 :]
    shift_xy(z, whole_ref[1], part_ref[1], g_ref, gets, out_ref, *scratch)
    terms = [own_ref[...]] + [gets[d - 1][z.slots(d)] for d in range(1, z.count)]
    while len(terms) > 1:
        terms = [terms[k] + terms[k + 1] for k in range(0, len(terms), 2)]
    profile_ref[...] = terms[0].T[: profile_ref.shape[0], :]


def local(count, ranks, pop_ratio, solid_blocks, shift_whole, shift_frac):
    _, planes, depth, width = pop_ratio.shape
    z = Sizes(planes, depth, width, count)
    assert ranks % 2 == 0
    f32 = lambda *shape: jax.ShapeDtypeStruct(shape, jnp.float32)
    vmem = pl.BlockSpec(memory_space=pltpu.VMEM)
    smem = pl.BlockSpec(memory_space=pltpu.SMEM)
    cells = f32(Q, planes * depth, width)
    fields = f32(2, planes * depth, width)
    halo = f32(Q + 1, planes, width)
    shifts = [pltpu.VMEM((count, len(rising), depth, width), jnp.float32)] * 2
    shifts.append(pltpu.VMEM((count, depth, width), jnp.float32))

    def buffers(more):
        return [f32(z.slots(d) + more, depth, width) for d in range(1, count)]

    def call(body, ins, outs, scratch=()):
        return pl.pallas_call(
            functools.partial(body, z),
            out_shape=outs,
            in_specs=ins,
            out_specs=[vmem] * len(outs),
            scratch_shapes=list(scratch),
            name=body.__name__,
        )

    def swap_x(values):
        return [
            lax.ppermute(values[d - 1], "gx", [(i, i ^ d) for i in range(count)])
            for d in range(1, count)
        ]

    pairs = [(i, i ^ 1) for i in range(ranks)]
    across = [(i, (i - 1 if i % 2 == 0 else i + 1) % ranks) for i in range(ranks)]

    pop = pop_ratio.reshape(cells.shape)
    post, old, mask, *sends = call(
        first_kernel, [smem, vmem, vmem], [cells, fields, f32(planes // BLOCK * z.deep, width)] + buffers(0)
    )(shift_whole, pop, solid_blocks)
    gets = swap_x(sends)
    h, inner, outer = call(
        second_kernel, [smem, smem] + [vmem] * (1 + count), [cells, halo, halo], shifts
    )(shift_whole, shift_frac, post, mask, *gets)
    outer = lax.ppermute(outer, "gz", across)
    inner = lax.ppermute(inner, "gz", pairs)
    g, acc, own, *sends = call(
        third_kernel,
        [smem] + [vmem] * 5,
        [cells, fields, f32(depth, width)] + buffers(1),
        [
            pltpu.VMEM((2, Q + 1, planes, width), jnp.float32),
            pltpu.VMEM((2, len(upward), planes, width), jnp.float32),
        ],
    )(shift_whole, h, inner, outer, mask, old)
    gets = swap_x(sends)
    out, profile = call(
        fourth_kernel, [smem, smem] + [vmem] * (1 + count), [cells, f32(2 * planes, depth)], shifts
    )(shift_whole, shift_frac, g, own, *gets)
    return (
        out.reshape(pop_ratio.shape),
        acc.reshape(2, planes, depth, width),
        profile.reshape(2, planes, depth),
    )


def solution(mesh):
    return jax.shard_map(
        functools.partial(local, mesh.shape["gx"], mesh.shape["gz"]),
        mesh=mesh,
        in_specs=(P(None, None, "gz", "gx"), P(None, "gz", "gx"), P(), P()),
        out_specs=(P(None, None, "gz", "gx"), P(None, None, "gz", "gx"), P(None, None, "gz")),
        check_vma=False,
    )
```

```python
import functools

import jax
import jax.numpy as jnp
import numpy as np
from jax import lax
from jax.experimental import pallas as pl
from jax.experimental.pallas import tpu as pltpu
from jax.sharding import PartitionSpec as P

BLOCK = 4
velocity_list = [
    (0, 0, 0),
    (1, 0, 0),
    (-1, 0, 0),
    (0, 1, 0),
    (0, -1, 0),
    (0, 0, 1),
    (0, 0, -1),
    (1, 1, 0),
    (-1, -1, 0),
    (1, -1, 0),
    (-1, 1, 0),
    (1, 0, 1),
    (-1, 0, -1),
    (1, 0, -1),
    (-1, 0, 1),
    (0, 1, 1),
    (0, -1, -1),
    (0, 1, -1),
    (0, -1, 1),
]
Q = len(velocity_list)
weights = [1.0 / 3.0] + [1.0 / 18.0] * 6 + [1.0 / 36.0] * 12
CX = [v[0] for v in velocity_list]
CY = [v[1] for v in velocity_list]
CZ = [v[2] for v in velocity_list]
opposite = [velocity_list.index((-x, -y, -z)) for x, y, z in velocity_list]
mirror = [velocity_list.index((x, y, -z)) for x, y, z in velocity_list]
rising = [i for i in range(Q) if CY[i] == 1]
falling = [i for i in range(Q) if CY[i] == -1]
level_y = [i for i in range(Q) if CY[i] == 0]
eastward = [i for i in range(Q) if CX[i] == 1]
westward = [i for i in range(Q) if CX[i] == -1]
upward = [i for i in range(Q) if CZ[i] == 1]
level = [i for i in range(Q) if CZ[i] == 0]
near_list = level + upward
near_slot = {i: s for s, i in enumerate(near_list)}
far_slot = {i: len(near_list) + s for s, i in enumerate(upward)}
MASK_SLOT = Q
wall_speed = 0.08
visc_rate = 1.25
fraction_unit = 4096.0
relax_rates = [0.0, 1.19, 1.4, 0.0, 1.2, 0.0, 1.2, 0.0, 1.2, 1.25, 1.4, 1.25, 1.4]
relax_rates += [1.25, 1.25, 1.25, 1.98, 1.98, 1.98]


def row_norms():
    v = np.array(velocity_list, dtype=np.float64)
    x, y, z = v[:, 0], v[:, 1], v[:, 2]
    s = x * x + y * y + z * z
    rows = [
        np.ones(Q),
        19 * s - 30,
        (21 * s * s - 53 * s + 24) / 2,
        x,
        (5 * s - 9) * x,
        y,
        (5 * s - 9) * y,
        z,
        (5 * s - 9) * z,
        3 * x * x - s,
        (3 * s - 5) * (3 * x * x - s),
        y * y - z * z,
        (3 * s - 5) * (y * y - z * z),
        x * y,
        y * z,
        x * z,
        (y * y - z * z) * x,
        (z * z - x * x) * y,
        (x * x - y * y) * z,
    ]
    return [float(np.sum(row * row)) for row in rows]


RATE = [rate / norm for rate, norm in zip(relax_rates, row_norms())]


def collide(f, solid):
    sums = {i: f[i] + f[i + 1] for i in range(1, Q, 2)}
    difs = {i: f[i] - f[i + 1] for i in range(1, Q, 2)}
    p1, d1 = sums[7] + sums[9], sums[7] - sums[9]
    p2, d2 = sums[11] + sums[13], sums[11] - sums[13]
    p3, d3 = sums[15] + sums[17], sums[15] - sums[17]
    s23 = sums[3] + sums[5]
    axis = sums[1] + s23
    p12 = p1 + p2
    diag = p12 + p3
    rho = f[0] + axis + diag
    inverse = 1.0 / rho
    a, c = difs[7] + difs[9], difs[7] - difs[9]
    b, e = difs[11] + difs[13], difs[11] - difs[13]
    d, g = difs[15] + difs[17], difs[15] - difs[17]
    ab, cd, eg = a + b, c + d, e + g
    jx, jy, jz = difs[1] + ab, difs[3] + cd, difs[5] + eg
    ux, uy, uz = jx * inverse, jy * inverse, jz * inverse
    xx, yy, zz = jx * ux, jy * uy, jz * uz
    yz_sum, yz_dif = yy + zz, yy - zz
    square = xx + yz_sum

    even_e = RATE[1] * (8.0 * diag - 11.0 * axis - 30.0 * f[0] + 11.0 * rho - 19.0 * square)
    even_s = RATE[2] * (12.0 * f[0] - 4.0 * axis + diag - 3.0 * rho + 5.5 * square)
    axis_x, diag_x = 2.0 * sums[1] - s23, p12 - 2.0 * p3
    eq_x = 2.0 * xx - yz_sum
    even_x = RATE[9] * (axis_x + diag_x - eq_x)
    even_px = RATE[10] * (diag_x - 2.0 * axis_x + 0.5 * eq_x)
    axis_w, diag_w = sums[3] - sums[5], p1 - p2
    even_w = RATE[11] * (axis_w + diag_w - yz_dif)
    even_pw = RATE[12] * (diag_w - 2.0 * axis_w + 0.5 * yz_dif)
    moment_xy = d1 - jx * uy
    even_xy = RATE[13] * moment_xy
    even_yz = RATE[14] * (d3 - jy * uz)
    even_xz = RATE[15] * (d2 - jx * uz)
    flow_x = RATE[4] * (ab - 4.0 * difs[1] + (2.0 / 3.0) * jx)
    flow_y = RATE[6] * (cd - 4.0 * difs[3] + (2.0 / 3.0) * jy)
    flow_z = RATE[8] * (eg - 4.0 * difs[5] + (2.0 / 3.0) * jz)
    twist_x = RATE[16] * (a - b)
    twist_y = RATE[17] * (d - c)
    twist_z = RATE[18] * (e - g)

    base_axis = -11.0 * even_e - 4.0 * even_s
    base_diag = 8.0 * even_e + even_s
    lean = even_x - 2.0 * even_px
    tilt = even_w - 2.0 * even_pw
    side_x = even_x + even_px
    side_w = even_w + even_pw
    flat = base_diag + side_x
    diag_xy, diag_xz = flat + side_w, flat - side_w
    diag_yz = base_diag - 2.0 * side_x
    low = base_axis - lean
    even = {
        1: base_axis + 2.0 * lean,
        3: low + tilt,
        5: low - tilt,
        7: diag_xy + even_xy,
        9: diag_xy - even_xy,
        11: diag_xz + even_xz,
        13: diag_xz - even_xz,
        15: diag_yz + even_yz,
        17: diag_yz - even_yz,
    }
    x_up, x_down = flow_x + twist_x, flow_x - twist_x
    y_up, y_down = flow_y + twist_y, flow_y - twist_y
    z_up, z_down = flow_z + twist_z, flow_z - twist_z
    odd = {
        1: -4.0 * flow_x,
        3: -4.0 * flow_y,
        5: -4.0 * flow_z,
        7: x_up + y_down,
        9: x_up - y_down,
        11: x_down + z_up,
        13: x_down - z_up,
        15: y_up + z_down,
        17: y_up - z_down,
    }
    post = [None] * Q
    post[0] = jnp.where(solid, f[0], f[0] + 30.0 * even_e - 12.0 * even_s)
    for i in range(1, Q, 2):
        post[i] = jnp.where(solid, f[i + 1], f[i] - (even[i] + odd[i]))
        post[i + 1] = jnp.where(solid, f[i], f[i + 1] - (even[i] - odd[i]))
    return post, jx, moment_xy


CHUNKS = 4


class Sizes:
    def __init__(self, planes, depth, width, count):
        self.planes, self.depth, self.width, self.count = planes, depth, width, count
        self.deep, self.wide = depth // BLOCK, width // BLOCK
        assert count >= 4 and count & (count - 1) == 0
        assert len(eastward) * planes + 4 <= width and 2 * planes <= width

    def slots(self, delta):
        return (2 if delta == self.count // 2 else 1) * len(rising) + 1

    def tile(self, ref, i, y):
        return ref[i, pl.ds(y * self.depth, self.depth), :]

    def lanes(self):
        return lax.broadcasted_iota(jnp.int32, (self.depth, self.width), 1)

    def rows(self):
        return lax.broadcasted_iota(jnp.int32, (self.depth, self.width), 0)

    def spread(self, row):
        return jnp.broadcast_to(row, (self.depth, self.width))

    def solid_tile(self, mask_ref, y):
        base = y // BLOCK * self.deep
        out = self.spread(mask_ref[base : base + 1, :])
        rows = self.rows()
        for step in range(1, self.deep):
            line = self.spread(mask_ref[base + step : base + step + 1, :])
            out = jnp.where(rows >= step * BLOCK, line, out)
        return out


def roll(value, shift, axis=1):
    shift = shift % value.shape[axis]
    return pltpu.roll(value, shift, axis) if shift else value


def edge_columns(z):
    return [
        (7, z.planes - 1, True),
        (10, z.planes - 1, False),
        (9, 0, True),
        (8, 0, False),
    ]


def wall_columns(z, ref, lanes):
    out = jnp.zeros((z.depth, z.width), jnp.float32)
    start = len(eastward) * z.planes
    for k, (i, y, right) in enumerate(edge_columns(z)):
        at = start + k
        moved = roll(z.tile(ref, i, y), at - (z.width - 1 if right else 0))
        out = jnp.where(lanes == at, moved, out)
    return out


def pack_x(z, whole, ref, sends, extra=None):
    me = lax.axis_index("gx")
    lanes = z.lanes()
    right_edge = wall_columns(z, ref, lanes)
    left_edge = right_edge
    for j in range(len(eastward)):
        for y in range(z.planes):
            at = j * z.planes + y
            hit = lanes == at
            moved = roll(z.tile(ref, eastward[j], y), at - (z.width - 1))
            right_edge = jnp.where(hit, moved, right_edge)
            moved = roll(z.tile(ref, westward[j], y), at)
            left_edge = jnp.where(hit, moved, left_edge)
    far = lax.div(whole, z.width)
    for delta in range(1, z.count):
        send = sends[delta - 1]
        partner = jnp.bitwise_xor(me, delta)
        ahead = lax.rem(me - partner + z.count, z.count)
        at_top = (ahead == far) | (ahead == lax.rem(far + 1, z.count))
        for s in range(len(rising)):
            top = z.tile(ref, rising[s], z.planes - 1)
            bottom = z.tile(ref, falling[s], 0)
            if delta == z.count // 2:
                send[s] = top
                send[len(rising) + s] = bottom
            else:
                send[s] = jnp.where(at_top, top, bottom)
        to_right = partner == lax.rem(me + 1, z.count)
        slots = z.slots(delta)
        send[slots - 1] = jnp.where(to_right, right_edge, left_edge)
        if extra is not None:
            send[slots] = extra


def shift_xy(z, step, scalars, ref, gets, out, tops, bottoms, edges, finish=None):
    me = lax.axis_index("gx")
    lanes = z.lanes()
    last = z.width - 1
    for s in range(len(rising)):
        tops[me, s] = z.tile(ref, rising[s], z.planes - 1)
        bottoms[me, s] = z.tile(ref, falling[s], 0)
    edges[me] = wall_columns(z, ref, lanes)
    for delta in range(1, z.count):
        get = gets[delta - 1]
        partner = jnp.bitwise_xor(me, delta)
        for s in range(len(rising)):
            tops[partner, s] = get[s]
            second = len(rising) + s if delta == z.count // 2 else s
            bottoms[partner, s] = get[second]
        edges[partner] = get[z.slots(delta) - 1]

    left = edges[lax.rem(me + z.count - 1, z.count)]
    right = edges[lax.rem(me + 1, z.count)]

    def moved(i, y):
        value = z.tile(ref, i, y)
        if CX[i] == 1:
            at = eastward.index(i) * z.planes + y
            return jnp.where(lanes == 0, roll(left, -at), roll(value, 1))
        if CX[i] == -1:
            at = westward.index(i) * z.planes + y
            return jnp.where(lanes == last, roll(right, last - at), roll(value, -1))
        return value

    def interior(start, stop):
        for i in range(Q):
            for y in range(start, stop):
                if 0 <= y - CY[i] < z.planes:
                    out[i, pl.ds(y * z.depth, z.depth), :] = moved(i, y - CY[i])

    group = z.planes // CHUNKS
    for k in range(1, CHUNKS - 1):
        interior(k * group, (k + 1) * group)
        if finish is not None:
            finish(k)
    interior(0, group)
    interior(z.planes - group, z.planes)
    whole_ref, part_ref = scalars()
    whole, part = whole_ref[step], part_ref[step]
    weight = part.astype(jnp.float32) / fraction_unit
    far = lax.div(whole, z.width)
    rest = lax.rem(whole, z.width)
    start = len(eastward) * z.planes
    columns = {i: start + k for k, (i, _, _) in enumerate(edge_columns(z))}

    def window(i, planes, s, block, offset):
        pair = []
        for step in range(2):
            here = lax.rem(block + step, z.count)
            value = planes[here, s]
            if CX[i] == 1:
                side = edges[lax.rem(here + z.count - 1, z.count)]
                value = jnp.where(lanes == 0, roll(side, -columns[i]), roll(value, 1))
            elif CX[i] == -1:
                side = edges[lax.rem(here + 1, z.count)]
                value = jnp.where(lanes == last, roll(side, last - columns[i]), roll(value, -1))
            pair.append(value)
        first = jnp.where(lanes >= offset, pair[0], pair[1])
        second = jnp.where(lanes > offset, pair[0], pair[1])
        first = pltpu.roll(first, lax.rem(z.width - offset, z.width), 1)
        second = pltpu.roll(second, last - offset, 1)
        return first, second

    for s, i in enumerate(rising):
        near, next_one = window(i, tops, s, lax.rem(me + far, z.count), rest)
        fix = 6.0 * weights[i] * CX[i] * wall_speed
        value = (1.0 - weight) * near + weight * next_one
        out[i, pl.ds(0, z.depth), :] = value - fix if CX[i] else value
    if finish is not None:
        finish(0)
    for s, i in enumerate(falling):
        block = lax.rem(me + 2 * z.count - far - 1, z.count)
        next_one, near = window(i, bottoms, s, block, last - rest)
        fix = 6.0 * weights[i] * CX[i] * wall_speed
        value = (1.0 - weight) * near + weight * next_one
        out[i, pl.ds((z.planes - 1) * z.depth, z.depth), :] = value + fix if CX[i] else value
    if finish is not None:
        finish(CHUNKS - 1)


def first_kernel(z, whole_hbm, pop_hbm, solid_hbm, post_ref, acc_ref, mask_ref, *refs):
    sends, (whole_ref, pop_ref, solid_ref, sems) = refs[: z.count - 1], refs[z.count - 1 :]
    group = z.planes // CHUNKS * z.depth
    copies = [pltpu.make_async_copy(solid_hbm, solid_ref, sems.at[CHUNKS])]
    for k in range(CHUNKS):
        part = (slice(None), pl.ds(k * group, group), slice(None))
        copies.append(pltpu.make_async_copy(pop_hbm.at[part], pop_ref.at[part], sems.at[k]))
    copies.append(pltpu.make_async_copy(whole_hbm, whole_ref, sems.at[CHUNKS + 1]))
    for copy in copies:
        copy.start()
    copies[0].wait()
    grow = lax.broadcasted_iota(jnp.int32, (z.wide, z.width), 1) // BLOCK
    grow = grow == lax.broadcasted_iota(jnp.int32, (z.wide, z.width), 0)
    grow = grow.astype(jnp.float32)
    for k in range(solid_ref.shape[0]):
        flags = jnp.where(solid_ref[k] > 0, 1.0, 0.0)
        line = jnp.dot(flags, grow, preferred_element_type=jnp.float32)
        mask_ref[pl.ds(k * z.deep, z.deep), :] = line
    for y in range(z.planes):
        if y % (z.planes // CHUNKS) == 0:
            copies[1 + y // (z.planes // CHUNKS)].wait()
        solid = z.solid_tile(mask_ref, y) > 0.5
        f = [z.tile(pop_ref, i, y) * np.float32(weights[i]) for i in range(Q)]
        post, jx, moment_xy = collide(f, solid)
        here = pl.ds(y * z.depth, z.depth)
        for i in range(Q):
            post_ref[i, here, :] = post[i]
        acc_ref[0, here, :] = jnp.where(solid, 0.0, jx)
        acc_ref[1, here, :] = jnp.where(solid, 0.0, -(1.0 - 0.5 * visc_rate) * moment_xy)
    copies[-1].wait()
    pack_x(z, whole_ref[0], post_ref, sends)


def fetch_scalars(whole_hbm, part_hbm, whole_ref, part_ref, sems):
    copies = [
        pltpu.make_async_copy(whole_hbm, whole_ref, sems.at[0]),
        pltpu.make_async_copy(part_hbm, part_ref, sems.at[1]),
    ]
    for copy in copies:
        copy.start()

    def scalars():
        for copy in copies:
            copy.wait()
        return whole_ref, part_ref

    return scalars


def second_kernel(z, whole_hbm, part_hbm, post_ref, mask_ref, *refs):
    gets, (h_ref, inner_ref, outer_ref) = refs[: z.count - 1], refs[z.count - 1 : z.count + 2]
    scratch = refs[z.count + 2 :]
    scalars = fetch_scalars(whole_hbm, part_hbm, *scratch[3:])
    shift_xy(z, 0, scalars, post_ref, gets, h_ref, *scratch[:3])
    even = lax.rem(lax.axis_index("gz"), 2) == 0

    def line(i, row):
        return h_ref[i, pl.ds(row, z.planes, stride=z.depth), :]

    def put(slot, up, down):
        inner_ref[slot] = jnp.where(even, up, down)
        outer_ref[slot] = jnp.where(even, down, up)

    for i in near_list:
        put(near_slot[i], line(i, z.depth - 1), line(mirror[i], 0))
    for i in upward:
        put(far_slot[i], line(i, z.depth - 2), line(mirror[i], 1))
    for k in range(z.planes // BLOCK):
        up = mask_ref[(k + 1) * z.deep - 1 : (k + 1) * z.deep, :]
        down = mask_ref[k * z.deep : k * z.deep + 1, :]
        shape = (BLOCK, z.width)
        here = pl.ds(k * BLOCK, BLOCK)
        inner_ref[MASK_SLOT, here, :] = jnp.broadcast_to(jnp.where(even, up, down), shape)
        outer_ref[MASK_SLOT, here, :] = jnp.broadcast_to(jnp.where(even, down, up), shape)


def third_kernel(z, whole_hbm, h_ref, inner_ref, outer_ref, mask_ref, old_ref, *refs):
    (g_ref, acc_hbm, part_ref), sends = refs[:3], refs[3 : 2 + z.count]
    sides, extra, acc_ref, whole_ref, sems = refs[2 + z.count :]
    whole_copy = pltpu.make_async_copy(whole_hbm, whole_ref, sems.at[0])
    whole_copy.start()
    acc_copy = pltpu.make_async_copy(acc_ref, acc_hbm, sems.at[1])
    even = lax.rem(lax.axis_index("gz"), 2) == 0
    sides[jnp.where(even, 1, 0)] = inner_ref[...]
    sides[jnp.where(even, 0, 1)] = outer_ref[...]
    chunk = min(8, z.planes)
    for side in range(2):
        for start in range(0, z.planes, chunk):
            here = pl.ds(start, chunk)
            f = [None] * Q
            for i in range(Q):
                k = i if side == 0 else mirror[i]
                if CZ[k] == 0:
                    f[i] = sides[side, near_slot[k], here, :]
                elif CZ[k] == 1:
                    f[i] = sides[side, far_slot[k], here, :]
                else:
                    row = start * z.depth + (0 if side == 0 else z.depth - 1)
                    f[i] = h_ref[i, pl.ds(row, chunk, stride=z.depth), :]
            post, _, _ = collide(f, sides[side, MASK_SLOT, here, :] > 0.5)
            for s, i in enumerate(upward):
                extra[side, s, here, :] = post[i if side == 0 else mirror[i]]
    rows, lanes = z.rows(), z.lanes()

    def moved(i, y, value, table, slot):
        if CZ[i] == 1:
            line = z.spread(table[0, slot(i), pl.ds(y, 1), :])
            return jnp.where(rows == 0, line, roll(value, 1, 0))
        if CZ[i] == -1:
            line = z.spread(table[1, slot(mirror[i]), pl.ds(y, 1), :])
            return jnp.where(rows == z.depth - 1, line, roll(value, -1, 0))
        return value

    sums = jnp.zeros((z.depth, z.width), jnp.float32)
    for y in range(z.planes):
        solid = z.solid_tile(mask_ref, y) > 0.5
        f = [moved(i, y, z.tile(h_ref, i, y), sides, near_slot.get) for i in range(Q)]
        post, jx, moment_xy = collide(f, solid)
        here = pl.ds(y * z.depth, z.depth)
        for i in range(Q):
            g_ref[i, here, :] = moved(i, y, post[i], extra, upward.index)
        fields = [jx, -(1.0 - 0.5 * visc_rate) * moment_xy]
        for k in range(2):
            value = old_ref[k, here, :] + jnp.where(solid, 0.0, fields[k])
            acc_ref[k, here, :] = value
            total = z.spread(jnp.sum(value, axis=1, keepdims=True))
            sums = jnp.where(lanes == k * z.planes + y, total, sums)
    acc_copy.start()
    part_ref[...] = sums
    whole_copy.wait()
    pack_x(z, whole_ref[1], g_ref, sends, sums)
    acc_copy.wait()


def fourth_kernel(z, whole_hbm, part_hbm, g_ref, own_ref, *refs):
    gets, (out_hbm, profile_hbm) = refs[: z.count - 1], refs[z.count - 1 : z.count + 1]
    scratch = refs[z.count + 1 :]
    scalars = fetch_scalars(whole_hbm, part_hbm, *scratch[3:6])
    out_ref, profile_ref, sems = scratch[6:]
    terms = [own_ref[...]] + [gets[d - 1][z.slots(d)] for d in range(1, z.count)]
    while len(terms) > 1:
        terms = [terms[k] + terms[k + 1] for k in range(0, len(terms), 2)]
    for k in range(2):
        profile_ref[k] = terms[0][:, k * z.planes : (k + 1) * z.planes]
    copies = [pltpu.make_async_copy(profile_ref, profile_hbm, sems.at[CHUNKS])]
    copies[0].start()

    def finish(k):
        group = z.planes // CHUNKS * z.depth
        part = (slice(None), pl.ds(k * group, group), slice(None))
        copies.append(pltpu.make_async_copy(out_ref.at[part], out_hbm.at[part], sems.at[k]))
        copies[-1].start()

    shift_xy(z, 1, scalars, g_ref, gets, out_ref, *scratch[:3], finish)
    for copy in copies:
        copy.wait()


def local(count, ranks, pop_ratio, solid_blocks, shift_whole, shift_frac):
    _, planes, depth, width = pop_ratio.shape
    z = Sizes(planes, depth, width, count)
    assert ranks % 2 == 0
    f32 = lambda *shape: pltpu.VMEM(shape, jnp.float32)
    hbm = lambda ref: jax.ShapeDtypeStruct(ref.shape, ref.dtype)
    keep = lambda *values: [pltpu.with_memory_space_constraint(v, pltpu.VMEM) for v in values]
    vmem = pl.BlockSpec(memory_space=pltpu.VMEM)
    outside = pl.BlockSpec(memory_space=pl.ANY)
    cells = f32(Q, planes * depth, width)
    fields = f32(2, planes * depth, width)
    halo = f32(Q + 1, planes, width)
    shifts = [pltpu.VMEM((count, len(rising), depth, width), jnp.float32)] * 2
    shifts.append(pltpu.VMEM((count, depth, width), jnp.float32))
    pair = pltpu.SMEM(shift_whole.shape, jnp.int32)
    sems = lambda number: pltpu.SemaphoreType.DMA((number,))
    shifts += [pair, pair, sems(2)]
    outer_keep = lambda *values: [pltpu.with_memory_space_constraint(v, pltpu.HBM) for v in values]
    shift_whole, shift_frac, solid_blocks = outer_keep(shift_whole, shift_frac, solid_blocks)

    def buffers(more):
        return [f32(z.slots(d) + more, depth, width) for d in range(1, count)]

    def call(body, ins, outs, scratch=(), direct=()):
        specs = [outside if k in direct else vmem for k in range(len(outs))]
        return pl.pallas_call(
            functools.partial(body, z),
            out_shape=outs,
            in_specs=ins,
            out_specs=specs,
            scratch_shapes=list(scratch),
            compiler_params=pltpu.CompilerParams(vmem_limit_bytes=8 << 20),
            name=body.__name__,
        )

    def swap_x(values):
        return [
            lax.ppermute(values[d - 1], "gx", [(i, i ^ d) for i in range(count)])
            for d in range(1, count)
        ]

    pairs = [(i, i ^ 1) for i in range(ranks)]
    across = [(i, (i - 1 if i % 2 == 0 else i + 1) % ranks) for i in range(ranks)]

    (pop,) = outer_keep(pop_ratio.reshape(cells.shape))
    post, old, mask, *sends = call(
        first_kernel,
        [outside] * 3,
        [cells, fields, f32(planes // BLOCK * z.deep, width)] + buffers(0),
        [pair, cells, pltpu.VMEM(solid_blocks.shape, jnp.int32), sems(CHUNKS + 2)],
    )(shift_whole, pop, solid_blocks)
    gets = swap_x(sends)
    h, inner, outer = call(
        second_kernel, [outside] * 2 + [vmem] * (1 + count), [cells, halo, halo], shifts
    )(shift_whole, shift_frac, *keep(post, mask, *gets))
    outer = lax.ppermute(outer, "gz", across)
    inner = lax.ppermute(inner, "gz", pairs)
    g, acc, own, *sends = call(
        third_kernel,
        [outside] + [vmem] * 5,
        [cells, hbm(fields), f32(depth, width)] + buffers(1),
        [
            pltpu.VMEM((2, Q + 1, planes, width), jnp.float32),
            pltpu.VMEM((2, len(upward), planes, width), jnp.float32),
            fields,
            pair,
            sems(2),
        ],
        [1],
    )(shift_whole, *keep(h, inner, outer, mask, old))
    gets = swap_x(sends)
    out, profile = call(
        fourth_kernel,
        [outside] * 2 + [vmem] * (1 + count),
        [hbm(cells), hbm(f32(2, depth, planes))],
        shifts + [cells, f32(2, depth, planes), sems(CHUNKS + 1)],
        [0, 1],
    )(shift_whole, shift_frac, *keep(g, own, *gets))
    return (
        out.reshape(pop_ratio.shape),
        acc.reshape(2, planes, depth, width),
        jnp.swapaxes(profile, 1, 2),
    )


def solution(mesh):
    return jax.shard_map(
        functools.partial(local, mesh.shape["gx"], mesh.shape["gz"]),
        mesh=mesh,
        in_specs=(P(None, None, "gz", "gx"), P(None, "gz", "gx"), P(), P()),
        out_specs=(P(None, None, "gz", "gx"), P(None, None, "gz", "gx"), P(None, None, "gz")),
        check_vma=False,
    )
```

```python
import functools

import jax
import jax.numpy as jnp
import numpy as np
from jax import lax
from jax.experimental import pallas as pl
from jax.experimental.pallas import tpu as pltpu
from jax.sharding import PartitionSpec as P


BLOCK = 4
velocity_list = [
    (0, 0, 0),
    (1, 0, 0),
    (-1, 0, 0),
    (0, 1, 0),
    (0, -1, 0),
    (0, 0, 1),
    (0, 0, -1),
    (1, 1, 0),
    (-1, -1, 0),
    (1, -1, 0),
    (-1, 1, 0),
    (1, 0, 1),
    (-1, 0, -1),
    (1, 0, -1),
    (-1, 0, 1),
    (0, 1, 1),
    (0, -1, -1),
    (0, 1, -1),
    (0, -1, 1),
]
Q = len(velocity_list)
weights = [1.0 / 3.0] + [1.0 / 18.0] * 6 + [1.0 / 36.0] * 12
CX = [v[0] for v in velocity_list]
CY = [v[1] for v in velocity_list]
CZ = [v[2] for v in velocity_list]
opposite = [velocity_list.index((-x, -y, -z)) for x, y, z in velocity_list]
mirror = [velocity_list.index((x, y, -z)) for x, y, z in velocity_list]
rising = [i for i in range(Q) if CY[i] == 1]
falling = [i for i in range(Q) if CY[i] == -1]
eastward = [i for i in range(Q) if CX[i] == 1]
westward = [i for i in range(Q) if CX[i] == -1]
upward = [i for i in range(Q) if CZ[i] == 1]
level = [i for i in range(Q) if CZ[i] == 0]
downward = [mirror[i] for i in upward]
straight = [i for i in range(Q) if CX[i] == 0]
slanted = [i for i in range(Q) if CX[i] != 0]
SPANS = [(i, next(k for k in range(i, Q + 1) if k == Q or CX[k] == 0)) for i in slanted if CX[i - 1] == 0]
PART, SUMS = len(upward), 2 * len(upward)
MASK = SUMS + 4
SLOTS = MASK + 1
wall_speed = 0.08
visc_rate = 1.25
fraction_unit = 4096.0
relax_rates = [0.0, 1.19, 1.4, 0.0, 1.2, 0.0, 1.2, 0.0, 1.2, 1.25, 1.4, 1.25, 1.4]
relax_rates += [1.25, 1.25, 1.25, 1.98, 1.98, 1.98]


def row_norms():
    v = np.array(velocity_list, dtype=np.float64)
    x, y, z = v[:, 0], v[:, 1], v[:, 2]
    s = x * x + y * y + z * z
    rows = [
        np.ones(Q),
        19 * s - 30,
        (21 * s * s - 53 * s + 24) / 2,
        x,
        (5 * s - 9) * x,
        y,
        (5 * s - 9) * y,
        z,
        (5 * s - 9) * z,
        3 * x * x - s,
        (3 * s - 5) * (3 * x * x - s),
        y * y - z * z,
        (3 * s - 5) * (y * y - z * z),
        x * y,
        y * z,
        x * z,
        (y * y - z * z) * x,
        (z * z - x * x) * y,
        (x * x - y * y) * z,
    ]
    return [float(np.sum(row * row)) for row in rows]


RATE = [rate / norm for rate, norm in zip(relax_rates, row_norms())]


def plus(a, b):
    return b if a is None else a if b is None else a + b


def minus(a, b):
    return a if b is None else -b if a is None else a - b


def scaled(factor, a):
    return None if a is None else factor * a


def moments(f):
    sums = {i: plus(f[i], f[i + 1]) for i in range(1, Q, 2)}
    difs = {i: minus(f[i], f[i + 1]) for i in range(1, Q, 2)}
    p1, d1 = plus(sums[7], sums[9]), minus(sums[7], sums[9])
    p2, d2 = plus(sums[11], sums[13]), minus(sums[11], sums[13])
    p3, d3 = plus(sums[15], sums[17]), minus(sums[15], sums[17])
    s23 = plus(sums[3], sums[5])
    axis = plus(sums[1], s23)
    p12 = plus(p1, p2)
    diag = plus(p12, p3)
    a, c = plus(difs[7], difs[9]), minus(difs[7], difs[9])
    b, e = plus(difs[11], difs[13]), minus(difs[11], difs[13])
    d, g = plus(difs[15], difs[17]), minus(difs[15], difs[17])
    ab, cd, eg = plus(a, b), plus(c, d), plus(e, g)
    axis_x, diag_x = minus(scaled(2.0, sums[1]), s23), minus(p12, scaled(2.0, p3))
    axis_w, diag_w = minus(sums[3], sums[5]), minus(p1, p2)
    kept = [
        plus(f[0], plus(axis, diag)),
        plus(difs[1], ab),
        plus(difs[3], cd),
        plus(difs[5], eg),
    ]
    others = [
        minus(minus(scaled(8.0, diag), scaled(11.0, axis)), scaled(30.0, f[0])),
        plus(scaled(12.0, f[0]), minus(diag, scaled(4.0, axis))),
        minus(ab, scaled(4.0, difs[1])),
        minus(cd, scaled(4.0, difs[3])),
        minus(eg, scaled(4.0, difs[5])),
        plus(axis_x, diag_x),
        minus(diag_x, scaled(2.0, axis_x)),
        plus(axis_w, diag_w),
        minus(diag_w, scaled(2.0, axis_w)),
        d1,
        d3,
        d2,
        minus(a, b),
        minus(d, c),
        minus(e, g),
    ]
    return kept, others


ORDER = [1, 2, 4, 6, 8, 9, 10, 11, 12, 13, 14, 15, 16, 17, 18]


def equilibrium(rho, jx, jy, jz):
    inverse = 1.0 / rho
    ux, uy, uz = jx * inverse, jy * inverse, jz * inverse
    xx, yy, zz = jx * ux, jy * uy, jz * uz
    yz_sum, yz_dif = yy + zz, yy - zz
    square = xx + yz_sum
    eq_x = 2.0 * xx - yz_sum
    third = -2.0 / 3.0
    eq = [19.0 * square - 11.0 * rho, 3.0 * rho - 5.5 * square]
    eq += [third * jx, third * jy, third * jz]
    eq += [eq_x, -0.5 * eq_x, yz_dif, -0.5 * yz_dif, jx * uy, jy * uz, jx * uz]
    return eq + [None] * 3


def relax(moment):
    scaled_by = [scaled(RATE[k], m) for k, m in zip(ORDER, moment)]
    even_e, even_s, flow_x, flow_y, flow_z, even_x, even_px, even_w, even_pw = scaled_by[:9]
    even_xy, even_yz, even_xz, twist_x, twist_y, twist_z = scaled_by[9:]
    base_axis = minus(scaled(-11.0, even_e), scaled(4.0, even_s))
    base_diag = plus(scaled(8.0, even_e), even_s)
    lean = minus(even_x, scaled(2.0, even_px))
    tilt = minus(even_w, scaled(2.0, even_pw))
    side_x, side_w = plus(even_x, even_px), plus(even_w, even_pw)
    flat = plus(base_diag, side_x)
    diag_xy, diag_xz = plus(flat, side_w), minus(flat, side_w)
    diag_yz = minus(base_diag, scaled(2.0, side_x))
    low = minus(base_axis, lean)
    even = {
        1: plus(base_axis, scaled(2.0, lean)),
        3: plus(low, tilt),
        5: minus(low, tilt),
        7: plus(diag_xy, even_xy),
        9: minus(diag_xy, even_xy),
        11: plus(diag_xz, even_xz),
        13: minus(diag_xz, even_xz),
        15: plus(diag_yz, even_yz),
        17: minus(diag_yz, even_yz),
    }
    x_up, x_down = plus(flow_x, twist_x), minus(flow_x, twist_x)
    y_up, y_down = plus(flow_y, twist_y), minus(flow_y, twist_y)
    z_up, z_down = plus(flow_z, twist_z), minus(flow_z, twist_z)
    odd = {
        1: scaled(-4.0, flow_x),
        3: scaled(-4.0, flow_y),
        5: scaled(-4.0, flow_z),
        7: plus(x_up, y_down),
        9: minus(x_up, y_down),
        11: plus(x_down, z_up),
        13: minus(x_down, z_up),
        15: plus(y_up, z_down),
        17: minus(y_up, z_down),
    }
    out = [minus(scaled(12.0, even_s), scaled(30.0, even_e))]
    for i in range(1, Q, 2):
        out += [plus(even[i], odd[i]), minus(even[i], odd[i])]
    return out


def collide(f, solid):
    kept, others = moments(f)
    rest = [minus(m, e) for m, e in zip(others, equilibrium(*kept))]
    change = relax(rest)
    post = [jnp.where(solid, f[opposite[i]], f[i] - change[i]) for i in range(Q)]
    return post, kept[1], rest[9]


CHUNKS = 4


class Sizes:
    def __init__(self, planes, depth, width, count):
        self.planes, self.depth, self.width, self.count = planes, depth, width, count
        self.deep, self.wide = depth // BLOCK, width // BLOCK
        assert count >= 4 and count & (count - 1) == 0
        assert len(eastward) * planes + 4 <= width and 2 * planes <= width

    def slots(self, delta):
        return (2 if delta == self.count // 2 else 1) * len(rising) + 1

    def tile(self, ref, i, y):
        return ref[i, pl.ds(y * self.depth, self.depth), :]

    def lanes(self):
        return lax.broadcasted_iota(jnp.int32, (self.depth, self.width), 1)

    def rows(self):
        return lax.broadcasted_iota(jnp.int32, (self.depth, self.width), 0)

    def spread(self, row):
        return jnp.broadcast_to(row, (self.depth, self.width))

    def solid_tile(self, mask_ref, y):
        base = y // BLOCK * self.deep
        out = self.spread(mask_ref[base : base + 1, :])
        rows = self.rows()
        for step in range(1, self.deep):
            line = self.spread(mask_ref[base + step : base + step + 1, :])
            out = jnp.where(rows >= step * BLOCK, line, out)
        return out


def roll(value, shift, axis=1):
    shift = shift % value.shape[axis]
    return pltpu.roll(value, shift, axis) if shift else value


def edge_columns(z):
    return [
        (7, z.planes - 1, True),
        (10, z.planes - 1, False),
        (9, 0, True),
        (8, 0, False),
    ]


def wall_columns(z, ref, lanes):
    out = jnp.zeros((z.depth, z.width), jnp.float32)
    start = len(eastward) * z.planes
    for k, (i, y, right) in enumerate(edge_columns(z)):
        at = start + k
        moved = roll(z.tile(ref, i, y), at - (z.width - 1 if right else 0))
        out = jnp.where(lanes == at, moved, out)
    return out


def pack_x(z, whole, ref, sends, extra=None):
    me = lax.axis_index("gx")
    lanes = z.lanes()
    right_edge = wall_columns(z, ref, lanes)
    left_edge = right_edge
    for j in range(len(eastward)):
        for y in range(z.planes):
            at = j * z.planes + y
            hit = lanes == at
            moved = roll(z.tile(ref, eastward[j], y), at - (z.width - 1))
            right_edge = jnp.where(hit, moved, right_edge)
            moved = roll(z.tile(ref, westward[j], y), at)
            left_edge = jnp.where(hit, moved, left_edge)
    far = lax.div(whole, z.width)
    for delta in range(1, z.count):
        send = sends[delta - 1]
        partner = jnp.bitwise_xor(me, delta)
        ahead = lax.rem(me - partner + z.count, z.count)
        at_top = (ahead == far) | (ahead == lax.rem(far + 1, z.count))
        for s in range(len(rising)):
            top = z.tile(ref, rising[s], z.planes - 1)
            bottom = z.tile(ref, falling[s], 0)
            if delta == z.count // 2:
                send[s] = top
                send[len(rising) + s] = bottom
            else:
                send[s] = jnp.where(at_top, top, bottom)
        to_right = partner == lax.rem(me + 1, z.count)
        slots = z.slots(delta)
        send[slots - 1] = jnp.where(to_right, right_edge, left_edge)
        if extra is not None:
            send[slots] = extra


def fill_tables(z, ref, gets, tops, bottoms, edges):
    me = lax.axis_index("gx")
    for s in range(len(rising)):
        tops[me, s] = z.tile(ref, rising[s], z.planes - 1)
        bottoms[me, s] = z.tile(ref, falling[s], 0)
    edges[me] = wall_columns(z, ref, z.lanes())
    for delta in range(1, z.count):
        get = gets[delta - 1]
        partner = jnp.bitwise_xor(me, delta)
        for s in range(len(rising)):
            tops[partner, s] = get[s]
            second = len(rising) + s if delta == z.count // 2 else s
            bottoms[partner, s] = get[second]
        edges[partner] = get[z.slots(delta) - 1]
    left = edges[lax.rem(me + z.count - 1, z.count)]
    right = edges[lax.rem(me + 1, z.count)]
    return left, right


def moved_x(z, ref, i, y, left, right):
    lanes, last = z.lanes(), z.width - 1
    value = z.tile(ref, i, y)
    if CX[i] == 1:
        at = eastward.index(i) * z.planes + y
        return jnp.where(lanes == 0, roll(left, -at), roll(value, 1))
    if CX[i] == -1:
        at = westward.index(i) * z.planes + y
        return jnp.where(lanes == last, roll(right, last - at), roll(value, -1))
    return value


def sliding(z, whole, part, tops, bottoms, edges, put):
    me = lax.axis_index("gx")
    lanes, last = z.lanes(), z.width - 1
    weight = part.astype(jnp.float32) / fraction_unit
    far = lax.div(whole, z.width)
    rest = lax.rem(whole, z.width)
    start = len(eastward) * z.planes
    columns = {i: start + k for k, (i, _, _) in enumerate(edge_columns(z))}

    def window(i, planes, s, block, offset):
        pair = []
        for step in range(2):
            here = lax.rem(block + step, z.count)
            value = planes[here, s]
            if CX[i] == 1:
                side = edges[lax.rem(here + z.count - 1, z.count)]
                value = jnp.where(lanes == 0, roll(side, -columns[i]), roll(value, 1))
            elif CX[i] == -1:
                side = edges[lax.rem(here + 1, z.count)]
                value = jnp.where(lanes == last, roll(side, last - columns[i]), roll(value, -1))
            pair.append(value)
        first = jnp.where(lanes >= offset, pair[0], pair[1])
        second = jnp.where(lanes > offset, pair[0], pair[1])
        first = pltpu.roll(first, lax.rem(z.width - offset, z.width), 1)
        second = pltpu.roll(second, last - offset, 1)
        return first, second

    for s, i in enumerate(rising):
        near, next_one = window(i, tops, s, lax.rem(me + far, z.count), rest)
        fix = 6.0 * weights[i] * CX[i] * wall_speed
        value = (1.0 - weight) * near + weight * next_one
        put(i, value - fix if CX[i] else value)
    for s, i in enumerate(falling):
        block = lax.rem(me + 2 * z.count - far - 1, z.count)
        next_one, near = window(i, bottoms, s, block, last - rest)
        fix = 6.0 * weights[i] * CX[i] * wall_speed
        value = (1.0 - weight) * near + weight * next_one
        put(i, value + fix if CX[i] else value)


def wall_slot(i):
    return rising.index(i) if CY[i] == 1 else len(rising) + falling.index(i)


def first_kernel(z, whole_hbm, pop_hbm, solid_hbm, post_ref, acc_ref, mask_ref, *refs):
    sends, (whole_ref, pop_ref, solid_ref, sems) = refs[: z.count - 1], refs[z.count - 1 :]
    group = z.planes // CHUNKS * z.depth
    copies = [pltpu.make_async_copy(solid_hbm, solid_ref, sems.at[CHUNKS])]
    for k in range(CHUNKS):
        part = (slice(None), pl.ds(k * group, group), slice(None))
        copies.append(pltpu.make_async_copy(pop_hbm.at[part], pop_ref.at[part], sems.at[k]))
    copies.append(pltpu.make_async_copy(whole_hbm, whole_ref, sems.at[CHUNKS + 1]))
    for copy in copies:
        copy.start()
    copies[0].wait()
    grow = lax.broadcasted_iota(jnp.int32, (z.wide, z.width), 1) // BLOCK
    grow = grow == lax.broadcasted_iota(jnp.int32, (z.wide, z.width), 0)
    grow = grow.astype(jnp.float32)
    for k in range(solid_ref.shape[0]):
        flags = jnp.where(solid_ref[k] > 0, 1.0, 0.0)
        line = jnp.dot(flags, grow, preferred_element_type=jnp.float32)
        mask_ref[pl.ds(k * z.deep, z.deep), :] = line
    for y in range(z.planes):
        if y % (z.planes // CHUNKS) == 0:
            copies[1 + y // (z.planes // CHUNKS)].wait()
        solid = z.solid_tile(mask_ref, y) > 0.5
        f = [z.tile(pop_ref, i, y) * np.float32(weights[i]) for i in range(Q)]
        post, jx, moment_xy = collide(f, solid)
        here = pl.ds(y * z.depth, z.depth)
        for i in range(Q):
            post_ref[i, here, :] = post[i]
        acc_ref[0, here, :] = jnp.where(solid, 0.0, jx)
        acc_ref[1, here, :] = jnp.where(solid, 0.0, -(1.0 - 0.5 * visc_rate) * moment_xy)
    copies[-1].wait()
    pack_x(z, whole_ref[0], post_ref, sends)


def fetch_scalars(whole_hbm, part_hbm, whole_ref, part_ref, sems):
    copies = [
        pltpu.make_async_copy(whole_hbm, whole_ref, sems.at[0]),
        pltpu.make_async_copy(part_hbm, part_ref, sems.at[1]),
    ]
    for copy in copies:
        copy.start()

    def scalars():
        for copy in copies:
            copy.wait()
        return whole_ref, part_ref

    return scalars


def second_kernel(z, whole_hbm, part_hbm, post_ref, mask_ref, *refs):
    gets, outs = refs[: z.count - 1], refs[z.count - 1 : z.count + 3]
    inner_ref, outer_ref, wall_ref, side_ref = outs
    tops, bottoms, edges, whole_ref, part_ref, sems, rows_ref = refs[z.count + 3 :]
    scalars = fetch_scalars(whole_hbm, part_hbm, whole_ref, part_ref, sems)
    left, right = fill_tables(z, post_ref, gets, tops, bottoms, edges)
    side_ref[0], side_ref[1] = left, right
    columns = {1: left.T, -1: right.T}
    shape = (z.planes, z.width)
    lanes = lax.broadcasted_iota(jnp.int32, shape, 1)
    heights = lax.broadcasted_iota(jnp.int32, shape, 0)
    even = lax.rem(lax.axis_index("gz"), 2) == 0

    def line(i, row):
        value = post_ref[i, pl.ds(row, z.planes, stride=z.depth), :]
        if CX[i]:
            j = (eastward if CX[i] == 1 else westward).index(i)
            column = columns[CX[i]][j * z.planes : (j + 1) * z.planes, row : row + 1]
            edge = 0 if CX[i] == 1 else z.width - 1
            value = jnp.where(lanes == edge, jnp.broadcast_to(column, shape), roll(value, CX[i]))
        if CY[i]:
            enter = 0 if CY[i] == 1 else z.planes - 1
            wall = jnp.broadcast_to(wall_ref[wall_slot(i), row : row + 1, :], shape)
            value = jnp.where(heights == enter, wall, roll(value, CY[i], 0))
        return value

    jobs = []
    for side in range(2):
        near, far = (z.depth - 1, z.depth - 2) if side == 0 else (0, 1)
        for k in range(Q):
            row = near if CZ[k] >= 0 else far
            i = k if CZ[k] >= 0 else mirror[k]
            jobs.append((side, k, i if side == 0 else mirror[i], row))
    for still in (True, False):
        for side, k, i, row in jobs:
            if (CY[i] == 0) == still:
                rows_ref[side, k] = line(i, row)
        if still:
            whole, part = (value[0] for value in scalars())

            def put(i, value):
                wall_ref[wall_slot(i)] = value

            sliding(z, whole, part, tops, bottoms, edges, put)

    chunk = min(8, z.planes)
    for start in range(0, z.planes, chunk):
        here = pl.ds(start, chunk)
        found = []
        for side in range(2):
            f = [None] * Q
            for i in level:
                f[i] = rows_ref[side, i, here, :]
            for i in upward:
                f[i] = rows_ref[side, mirror[i], here, :]
            kept, others = moments(f)
            change = relax(others)
            values = [rows_ref[side, i, here, :] for i in upward]
            values += [f[i] - change[i] for i in upward]
            found.append(values + kept)
        for slot in range(MASK):
            up, down = found[0][slot], found[1][slot]
            inner_ref[slot, here, :] = jnp.where(even, up, down)
            outer_ref[slot, here, :] = jnp.where(even, down, up)
    for k in range(z.planes // BLOCK):
        up = mask_ref[(k + 1) * z.deep - 1 : (k + 1) * z.deep, :]
        down = mask_ref[k * z.deep : k * z.deep + 1, :]
        here = pl.ds(k * BLOCK, BLOCK)
        block = (BLOCK, z.width)
        inner_ref[MASK, here, :] = jnp.broadcast_to(jnp.where(even, up, down), block)
        outer_ref[MASK, here, :] = jnp.broadcast_to(jnp.where(even, down, up), block)


def bulk_kernel(z, post_ref, wall_ref, side_ref, h_ref):
    left, right = side_ref[0], side_ref[1]
    for i in range(Q):
        for y in range(z.planes):
            here = pl.ds(y * z.depth, z.depth)
            if 0 <= y - CY[i] < z.planes:
                h_ref[i, here, :] = moved_x(z, post_ref, i, y - CY[i], left, right)
            else:
                h_ref[i, here, :] = wall_ref[wall_slot(i)]


def third_kernel(z, whole_hbm, h_ref, inner_ref, outer_ref, mask_ref, old_ref, *refs):
    (g_ref, acc_hbm, part_ref), sends = refs[:3], refs[3 : 2 + z.count]
    sides, extra, acc_ref, whole_ref, sems = refs[2 + z.count :]
    whole_copy = pltpu.make_async_copy(whole_hbm, whole_ref, sems.at[0])
    whole_copy.start()
    acc_copy = pltpu.make_async_copy(acc_ref, acc_hbm, sems.at[1])
    even = lax.rem(lax.axis_index("gz"), 2) == 0
    sides[jnp.where(even, 1, 0)] = inner_ref[...]
    sides[jnp.where(even, 0, 1)] = outer_ref[...]
    chunk = min(8, z.planes)
    for side in range(2):
        for start in range(0, z.planes, chunk):
            here = pl.ds(start, chunk)
            row = start * z.depth + (0 if side == 0 else z.depth - 1)
            f = [None] * Q
            for i in downward:
                k = i if side == 0 else mirror[i]
                f[i] = h_ref[k, pl.ds(row, chunk, stride=z.depth), :]
            kept, others = moments(f)
            kept = [plus(kept[k], sides[side, SUMS + k, here, :]) for k in range(4)]
            change = relax([minus(m, e) for m, e in zip(others, equilibrium(*kept))])
            solid = sides[side, MASK, here, :] > 0.5
            for s, i in enumerate(upward):
                value = sides[side, PART + s, here, :] - change[i]
                extra[side, s, here, :] = jnp.where(solid, f[opposite[i]], value)
    rows, lanes = z.rows(), z.lanes()

    def moved(i, y, value, table, slot):
        if CZ[i] == 1:
            line = z.spread(table[0, slot(i), pl.ds(y, 1), :])
            return jnp.where(rows == 0, line, roll(value, 1, 0))
        if CZ[i] == -1:
            line = z.spread(table[1, slot(mirror[i]), pl.ds(y, 1), :])
            return jnp.where(rows == z.depth - 1, line, roll(value, -1, 0))
        return value

    sums = jnp.zeros((z.depth, z.width), jnp.float32)
    for y in range(z.planes):
        solid = z.solid_tile(mask_ref, y) > 0.5
        f = [moved(i, y, z.tile(h_ref, i, y), sides, upward.index) for i in range(Q)]
        post, jx, moment_xy = collide(f, solid)
        here = pl.ds(y * z.depth, z.depth)
        for i in range(Q):
            g_ref[i, here, :] = moved(i, y, post[i], extra, upward.index)
        fields = [jx, -(1.0 - 0.5 * visc_rate) * moment_xy]
        for k in range(2):
            value = old_ref[k, here, :] + jnp.where(solid, 0.0, fields[k])
            acc_ref[k, here, :] = value
            total = z.spread(jnp.sum(value, axis=1, keepdims=True))
            sums = jnp.where(lanes == k * z.planes + y, total, sums)
    acc_copy.start()
    part_ref[...] = sums
    whole_copy.wait()
    pack_x(z, whole_ref[1], g_ref, sends, sums)
    acc_copy.wait()


def direct_kernel(z, g_ref, out_hbm, sems):
    inner = (z.planes - 1) * z.depth
    copies = []
    for k, i in enumerate(straight):
        source, target = g_ref.at[i], out_hbm.at[i]
        if CY[i] == 1:
            source, target = source.at[pl.ds(0, inner), :], target.at[pl.ds(z.depth, inner), :]
        elif CY[i] == -1:
            source, target = source.at[pl.ds(z.depth, inner), :], target.at[pl.ds(0, inner), :]
        copies.append(pltpu.make_async_copy(source, target, sems.at[k]))
        copies[-1].start()
    for copy in copies:
        copy.wait()


def fourth_kernel(z, whole_hbm, part_hbm, g_ref, own_ref, *refs):
    gets, (_, out_hbm, profile_hbm) = refs[: z.count - 1], refs[z.count - 1 : z.count + 2]
    tops, bottoms, edges, whole_ref, part_ref, pair_sems, out_ref, profile_ref, sems = refs[z.count + 2 :]
    scalars = fetch_scalars(whole_hbm, part_hbm, whole_ref, part_ref, pair_sems)
    terms = [own_ref[...]] + [gets[d - 1][z.slots(d)] for d in range(1, z.count)]
    while len(terms) > 1:
        terms = [terms[k] + terms[k + 1] for k in range(0, len(terms), 2)]
    for k in range(2):
        profile_ref[k] = terms[0][:, k * z.planes : (k + 1) * z.planes]
    copies = []

    def send(source, target):
        copies.append(pltpu.make_async_copy(source, target, sems.at[len(copies)]))
        copies[-1].start()

    send(profile_ref, profile_hbm)
    left, right = fill_tables(z, g_ref, gets, tops, bottoms, edges)
    group = z.planes // CHUNKS

    def interior(k):
        for i in slanted:
            for y in range(k * group, (k + 1) * group):
                if 0 <= y - CY[i] < z.planes:
                    here = pl.ds(y * z.depth, z.depth)
                    out_ref[i, here, :] = moved_x(z, g_ref, i, y - CY[i], left, right)

    def finish(k):
        here = pl.ds(k * group * z.depth, group * z.depth)
        for first, last in SPANS:
            part = (pl.ds(first, last - first), here, slice(None))
            send(out_ref.at[part], out_hbm.at[part])

    for k in range(1, CHUNKS - 1):
        interior(k)
        finish(k)
    whole, part = (value[1] for value in scalars())

    def put(i, value):
        here = pl.ds(0 if CY[i] == 1 else (z.planes - 1) * z.depth, z.depth)
        out_ref[i, here, :] = value
        if CX[i] == 0:
            send(out_ref.at[i, here, :], out_hbm.at[i, here, :])

    sliding(z, whole, part, tops, bottoms, edges, put)
    for k in (0, CHUNKS - 1):
        interior(k)
        finish(k)
    for copy in copies:
        copy.wait()


def local(count, ranks, pop_ratio, solid_blocks, shift_whole, shift_frac):
    _, planes, depth, width = pop_ratio.shape
    z = Sizes(planes, depth, width, count)
    assert ranks % 2 == 0
    f32 = lambda *shape: pltpu.VMEM(shape, jnp.float32)
    hbm = lambda ref: jax.ShapeDtypeStruct(ref.shape, ref.dtype)
    keep = lambda *values: [pltpu.with_memory_space_constraint(v, pltpu.VMEM) for v in values]
    vmem = pl.BlockSpec(memory_space=pltpu.VMEM)
    outside = pl.BlockSpec(memory_space=pl.ANY)
    cells = f32(Q, planes * depth, width)
    fields = f32(2, planes * depth, width)
    halo = f32(SLOTS, planes, width)
    shifts = [pltpu.VMEM((count, len(rising), depth, width), jnp.float32)] * 2
    shifts.append(pltpu.VMEM((count, depth, width), jnp.float32))
    pair = pltpu.SMEM(shift_whole.shape, jnp.int32)
    sems = lambda number: pltpu.SemaphoreType.DMA((number,))
    shifts += [pair, pair, sems(2)]
    outer_keep = lambda *values: [pltpu.with_memory_space_constraint(v, pltpu.HBM) for v in values]
    shift_whole, shift_frac, solid_blocks = outer_keep(shift_whole, shift_frac, solid_blocks)

    def buffers(more):
        return [f32(z.slots(d) + more, depth, width) for d in range(1, count)]

    def call(body, ins, outs, scratch=(), direct=(), alias=None):
        specs = [outside if k in direct else vmem for k in range(len(outs))]
        return pl.pallas_call(
            functools.partial(body, z),
            out_shape=outs,
            in_specs=ins,
            out_specs=specs,
            scratch_shapes=list(scratch),
            input_output_aliases=alias or {},
            compiler_params=pltpu.CompilerParams(vmem_limit_bytes=8 << 20),
        )

    def swap_x(values):
        return [
            lax.ppermute(values[d - 1], "gx", [(i, i ^ d) for i in range(count)])
            for d in range(1, count)
        ]

    pairs = [(i, i ^ 1) for i in range(ranks)]
    across = [(i, (i - 1 if i % 2 == 0 else i + 1) % ranks) for i in range(ranks)]

    (pop,) = outer_keep(pop_ratio.reshape(cells.shape))
    post, old, mask, *sends = call(
        first_kernel,
        [outside] * 3,
        [cells, fields, f32(planes // BLOCK * z.deep, width)] + buffers(0),
        [pair, cells, pltpu.VMEM(solid_blocks.shape, jnp.int32), sems(CHUNKS + 2)],
    )(shift_whole, pop, solid_blocks)
    gets = swap_x(sends)
    walls, both = f32(2 * len(rising), depth, width), f32(2, depth, width)
    inner, outer, wall, side = call(
        second_kernel,
        [outside] * 2 + [vmem] * (1 + count),
        [halo, halo, walls, both],
        shifts + [f32(2, Q, planes, width)],
    )(shift_whole, shift_frac, *keep(post, mask, *gets))
    outer = lax.ppermute(outer, "gz", across)
    inner = lax.ppermute(inner, "gz", pairs)
    (h,) = call(bulk_kernel, [vmem] * 3, [cells])(*keep(post, wall, side))
    g, acc, own, *sends = call(
        third_kernel,
        [outside] + [vmem] * 5,
        [cells, hbm(fields), f32(depth, width)] + buffers(1),
        [
            pltpu.VMEM((2, SLOTS, planes, width), jnp.float32),
            pltpu.VMEM((2, len(upward), planes, width), jnp.float32),
            fields,
            pair,
            sems(2),
        ],
        [1],
    )(shift_whole, *keep(h, inner, outer, mask, old))
    gets = swap_x(sends)
    (out,) = call(direct_kernel, [vmem], [hbm(cells)], [sems(len(straight))], [0])(*keep(g))
    moves = 1 + len(SPANS) * CHUNKS + sum(CX[i] == 0 for i in rising + falling)
    out, profile = call(
        fourth_kernel,
        [outside] * 2 + [vmem] * (1 + count) + [outside],
        [hbm(cells), hbm(f32(2, depth, planes))],
        shifts + [cells, f32(2, depth, planes), sems(moves)],
        [0, 1],
        {3 + count: 0},
    )(shift_whole, shift_frac, *keep(g, own, *gets), out)
    return (
        out.reshape(pop_ratio.shape),
        acc.reshape(2, planes, depth, width),
        jnp.swapaxes(profile, 1, 2),
    )


def solution(mesh):
    return jax.shard_map(
        functools.partial(local, mesh.shape["gx"], mesh.shape["gz"]),
        mesh=mesh,
        in_specs=(P(None, None, "gz", "gx"), P(None, "gz", "gx"), P(), P()),
        out_specs=(P(None, None, "gz", "gx"), P(None, None, "gz", "gx"), P(None, None, "gz")),
        check_vma=False,
    )
```

```python
import functools

import jax
import jax.numpy as jnp
import numpy as np
from jax import lax
from jax.experimental import pallas as pl
from jax.experimental.pallas import tpu as pltpu
from jax.sharding import PartitionSpec as P


BLOCK = 4
velocity_list = [
    (0, 0, 0),
    (1, 0, 0),
    (-1, 0, 0),
    (0, 1, 0),
    (0, -1, 0),
    (0, 0, 1),
    (0, 0, -1),
    (1, 1, 0),
    (-1, -1, 0),
    (1, -1, 0),
    (-1, 1, 0),
    (1, 0, 1),
    (-1, 0, -1),
    (1, 0, -1),
    (-1, 0, 1),
    (0, 1, 1),
    (0, -1, -1),
    (0, 1, -1),
    (0, -1, 1),
]
Q = len(velocity_list)
weights = [1.0 / 3.0] + [1.0 / 18.0] * 6 + [1.0 / 36.0] * 12
CX = [v[0] for v in velocity_list]
CY = [v[1] for v in velocity_list]
CZ = [v[2] for v in velocity_list]
opposite = [velocity_list.index((-x, -y, -z)) for x, y, z in velocity_list]
mirror = [velocity_list.index((x, y, -z)) for x, y, z in velocity_list]
rising = [i for i in range(Q) if CY[i] == 1]
falling = [i for i in range(Q) if CY[i] == -1]
eastward = [i for i in range(Q) if CX[i] == 1]
westward = [i for i in range(Q) if CX[i] == -1]
upward = [i for i in range(Q) if CZ[i] == 1]
level = [i for i in range(Q) if CZ[i] == 0]
downward = [mirror[i] for i in upward]
straight = [i for i in range(Q) if CX[i] == 0]
slanted = [i for i in range(Q) if CX[i] != 0]
SPANS = [(i, next(k for k in range(i, Q + 1) if k == Q or CX[k] == 0)) for i in slanted if CX[i - 1] == 0]
PART, SUMS = len(upward), 2 * len(upward)
MASK = SUMS + 4
SLOTS = MASK + 1
wall_speed = 0.08
visc_rate = 1.25
fraction_unit = 4096.0
relax_rates = [0.0, 1.19, 1.4, 0.0, 1.2, 0.0, 1.2, 0.0, 1.2, 1.25, 1.4, 1.25, 1.4]
relax_rates += [1.25, 1.25, 1.25, 1.98, 1.98, 1.98]


def row_norms():
    v = np.array(velocity_list, dtype=np.float64)
    x, y, z = v[:, 0], v[:, 1], v[:, 2]
    s = x * x + y * y + z * z
    rows = [
        np.ones(Q),
        19 * s - 30,
        (21 * s * s - 53 * s + 24) / 2,
        x,
        (5 * s - 9) * x,
        y,
        (5 * s - 9) * y,
        z,
        (5 * s - 9) * z,
        3 * x * x - s,
        (3 * s - 5) * (3 * x * x - s),
        y * y - z * z,
        (3 * s - 5) * (y * y - z * z),
        x * y,
        y * z,
        x * z,
        (y * y - z * z) * x,
        (z * z - x * x) * y,
        (x * x - y * y) * z,
    ]
    return [float(np.sum(row * row)) for row in rows]


RATE = [rate / norm for rate, norm in zip(relax_rates, row_norms())]


def plus(a, b):
    return b if a is None else a if b is None else a + b


def minus(a, b):
    return a if b is None else -b if a is None else a - b


def scaled(factor, a):
    return None if a is None else factor * a


def moments(f):
    sums = {i: plus(f[i], f[i + 1]) for i in range(1, Q, 2)}
    difs = {i: minus(f[i], f[i + 1]) for i in range(1, Q, 2)}
    p1, d1 = plus(sums[7], sums[9]), minus(sums[7], sums[9])
    p2, d2 = plus(sums[11], sums[13]), minus(sums[11], sums[13])
    p3, d3 = plus(sums[15], sums[17]), minus(sums[15], sums[17])
    s23 = plus(sums[3], sums[5])
    axis = plus(sums[1], s23)
    p12 = plus(p1, p2)
    diag = plus(p12, p3)
    a, c = plus(difs[7], difs[9]), minus(difs[7], difs[9])
    b, e = plus(difs[11], difs[13]), minus(difs[11], difs[13])
    d, g = plus(difs[15], difs[17]), minus(difs[15], difs[17])
    ab, cd, eg = plus(a, b), plus(c, d), plus(e, g)
    axis_x, diag_x = minus(scaled(2.0, sums[1]), s23), minus(p12, scaled(2.0, p3))
    axis_w, diag_w = minus(sums[3], sums[5]), minus(p1, p2)
    kept = [
        plus(f[0], plus(axis, diag)),
        plus(difs[1], ab),
        plus(difs[3], cd),
        plus(difs[5], eg),
    ]
    others = [
        minus(minus(scaled(8.0, diag), scaled(11.0, axis)), scaled(30.0, f[0])),
        plus(scaled(12.0, f[0]), minus(diag, scaled(4.0, axis))),
        minus(ab, scaled(4.0, difs[1])),
        minus(cd, scaled(4.0, difs[3])),
        minus(eg, scaled(4.0, difs[5])),
        plus(axis_x, diag_x),
        minus(diag_x, scaled(2.0, axis_x)),
        plus(axis_w, diag_w),
        minus(diag_w, scaled(2.0, axis_w)),
        d1,
        d3,
        d2,
        minus(a, b),
        minus(d, c),
        minus(e, g),
    ]
    return kept, others


ORDER = [1, 2, 4, 6, 8, 9, 10, 11, 12, 13, 14, 15, 16, 17, 18]


def equilibrium(rho, jx, jy, jz):
    inverse = 1.0 / rho
    ux, uy, uz = jx * inverse, jy * inverse, jz * inverse
    xx, yy, zz = jx * ux, jy * uy, jz * uz
    yz_sum, yz_dif = yy + zz, yy - zz
    square = xx + yz_sum
    eq_x = 2.0 * xx - yz_sum
    third = -2.0 / 3.0
    eq = [19.0 * square - 11.0 * rho, 3.0 * rho - 5.5 * square]
    eq += [third * jx, third * jy, third * jz]
    eq += [eq_x, -0.5 * eq_x, yz_dif, -0.5 * yz_dif, jx * uy, jy * uz, jx * uz]
    return eq + [None] * 3


def relax(moment):
    scaled_by = [scaled(RATE[k], m) for k, m in zip(ORDER, moment)]
    even_e, even_s, flow_x, flow_y, flow_z, even_x, even_px, even_w, even_pw = scaled_by[:9]
    even_xy, even_yz, even_xz, twist_x, twist_y, twist_z = scaled_by[9:]
    base_axis = minus(scaled(-11.0, even_e), scaled(4.0, even_s))
    base_diag = plus(scaled(8.0, even_e), even_s)
    lean = minus(even_x, scaled(2.0, even_px))
    tilt = minus(even_w, scaled(2.0, even_pw))
    side_x, side_w = plus(even_x, even_px), plus(even_w, even_pw)
    flat = plus(base_diag, side_x)
    diag_xy, diag_xz = plus(flat, side_w), minus(flat, side_w)
    diag_yz = minus(base_diag, scaled(2.0, side_x))
    low = minus(base_axis, lean)
    even = {
        1: plus(base_axis, scaled(2.0, lean)),
        3: plus(low, tilt),
        5: minus(low, tilt),
        7: plus(diag_xy, even_xy),
        9: minus(diag_xy, even_xy),
        11: plus(diag_xz, even_xz),
        13: minus(diag_xz, even_xz),
        15: plus(diag_yz, even_yz),
        17: minus(diag_yz, even_yz),
    }
    x_up, x_down = plus(flow_x, twist_x), minus(flow_x, twist_x)
    y_up, y_down = plus(flow_y, twist_y), minus(flow_y, twist_y)
    z_up, z_down = plus(flow_z, twist_z), minus(flow_z, twist_z)
    odd = {
        1: scaled(-4.0, flow_x),
        3: scaled(-4.0, flow_y),
        5: scaled(-4.0, flow_z),
        7: plus(x_up, y_down),
        9: minus(x_up, y_down),
        11: plus(x_down, z_up),
        13: minus(x_down, z_up),
        15: plus(y_up, z_down),
        17: minus(y_up, z_down),
    }
    out = [minus(scaled(12.0, even_s), scaled(30.0, even_e))]
    for i in range(1, Q, 2):
        out += [plus(even[i], odd[i]), minus(even[i], odd[i])]
    return out


def collide(f, solid):
    kept, others = moments(f)
    rest = [minus(m, e) for m, e in zip(others, equilibrium(*kept))]
    change = relax(rest)
    post = [jnp.where(solid, f[opposite[i]], f[i] - change[i]) for i in range(Q)]
    return post, kept[1], rest[9]


CHUNKS = 4


class Sizes:
    def __init__(self, planes, depth, width, count):
        self.planes, self.depth, self.width, self.count = planes, depth, width, count
        self.deep, self.wide = depth // BLOCK, width // BLOCK
        assert count >= 4 and count & (count - 1) == 0
        assert len(eastward) * planes + 4 <= width and 2 * planes <= width

    def slots(self, delta):
        return (2 if delta == self.count // 2 else 1) * len(rising) + 1

    def tile(self, ref, i, y):
        return ref[i, pl.ds(y * self.depth, self.depth), :]

    def lanes(self):
        return lax.broadcasted_iota(jnp.int32, (self.depth, self.width), 1)

    def rows(self):
        return lax.broadcasted_iota(jnp.int32, (self.depth, self.width), 0)

    def spread(self, row):
        return jnp.broadcast_to(row, (self.depth, self.width))

    def solid_tile(self, mask_ref, y):
        base = y // BLOCK * self.deep
        out = self.spread(mask_ref[base : base + 1, :])
        rows = self.rows()
        for step in range(1, self.deep):
            line = self.spread(mask_ref[base + step : base + step + 1, :])
            out = jnp.where(rows >= step * BLOCK, line, out)
        return out


def roll(value, shift, axis=1):
    shift = shift % value.shape[axis]
    return pltpu.roll(value, shift, axis) if shift else value


def edge_columns(z):
    return [
        (7, z.planes - 1, True),
        (10, z.planes - 1, False),
        (9, 0, True),
        (8, 0, False),
    ]


def wall_columns(z, ref, lanes):
    out = jnp.zeros((z.depth, z.width), jnp.float32)
    start = len(eastward) * z.planes
    for k, (i, y, right) in enumerate(edge_columns(z)):
        at = start + k
        moved = roll(z.tile(ref, i, y), at - (z.width - 1 if right else 0))
        out = jnp.where(lanes == at, moved, out)
    return out


def pack_x(z, whole, ref, sends, extra=None):
    me = lax.axis_index("gx")
    lanes = z.lanes()
    right_edge = wall_columns(z, ref, lanes)
    left_edge = right_edge
    for j in range(len(eastward)):
        for y in range(z.planes):
            at = j * z.planes + y
            hit = lanes == at
            moved = roll(z.tile(ref, eastward[j], y), at - (z.width - 1))
            right_edge = jnp.where(hit, moved, right_edge)
            moved = roll(z.tile(ref, westward[j], y), at)
            left_edge = jnp.where(hit, moved, left_edge)
    far = lax.div(whole, z.width)
    for delta in range(1, z.count):
        send = sends[delta - 1]
        partner = jnp.bitwise_xor(me, delta)
        ahead = lax.rem(me - partner + z.count, z.count)
        at_top = (ahead == far) | (ahead == lax.rem(far + 1, z.count))
        for s in range(len(rising)):
            top = z.tile(ref, rising[s], z.planes - 1)
            bottom = z.tile(ref, falling[s], 0)
            if delta == z.count // 2:
                send[s] = top
                send[len(rising) + s] = bottom
            else:
                send[s] = jnp.where(at_top, top, bottom)
        to_right = partner == lax.rem(me + 1, z.count)
        slots = z.slots(delta)
        send[slots - 1] = jnp.where(to_right, right_edge, left_edge)
        if extra is not None:
            send[slots] = extra


def fill_tables(z, ref, gets, tops, bottoms, edges):
    me = lax.axis_index("gx")
    for s in range(len(rising)):
        tops[me, s] = z.tile(ref, rising[s], z.planes - 1)
        bottoms[me, s] = z.tile(ref, falling[s], 0)
    edges[me] = wall_columns(z, ref, z.lanes())
    for delta in range(1, z.count):
        get = gets[delta - 1]
        partner = jnp.bitwise_xor(me, delta)
        for s in range(len(rising)):
            tops[partner, s] = get[s]
            second = len(rising) + s if delta == z.count // 2 else s
            bottoms[partner, s] = get[second]
        edges[partner] = get[z.slots(delta) - 1]
    left = edges[lax.rem(me + z.count - 1, z.count)]
    right = edges[lax.rem(me + 1, z.count)]
    return left, right


def moved_x(z, ref, i, y, left, right):
    lanes, last = z.lanes(), z.width - 1
    value = z.tile(ref, i, y)
    if CX[i] == 1:
        at = eastward.index(i) * z.planes + y
        return jnp.where(lanes == 0, roll(left, -at), roll(value, 1))
    if CX[i] == -1:
        at = westward.index(i) * z.planes + y
        return jnp.where(lanes == last, roll(right, last - at), roll(value, -1))
    return value


def sliding(z, whole, part, tops, bottoms, edges, put):
    me = lax.axis_index("gx")
    lanes, last = z.lanes(), z.width - 1
    weight = part.astype(jnp.float32) / fraction_unit
    far = lax.div(whole, z.width)
    rest = lax.rem(whole, z.width)
    start = len(eastward) * z.planes
    columns = {i: start + k for k, (i, _, _) in enumerate(edge_columns(z))}

    def window(i, planes, s, block, offset):
        pair = []
        for step in range(2):
            here = lax.rem(block + step, z.count)
            value = planes[here, s]
            if CX[i] == 1:
                side = edges[lax.rem(here + z.count - 1, z.count)]
                value = jnp.where(lanes == 0, roll(side, -columns[i]), roll(value, 1))
            elif CX[i] == -1:
                side = edges[lax.rem(here + 1, z.count)]
                value = jnp.where(lanes == last, roll(side, last - columns[i]), roll(value, -1))
            pair.append(value)
        first = jnp.where(lanes >= offset, pair[0], pair[1])
        second = jnp.where(lanes > offset, pair[0], pair[1])
        first = pltpu.roll(first, lax.rem(z.width - offset, z.width), 1)
        second = pltpu.roll(second, last - offset, 1)
        return first, second

    for s, i in enumerate(rising):
        near, next_one = window(i, tops, s, lax.rem(me + far, z.count), rest)
        fix = 6.0 * weights[i] * CX[i] * wall_speed
        value = (1.0 - weight) * near + weight * next_one
        put(i, value - fix if CX[i] else value)
    for s, i in enumerate(falling):
        block = lax.rem(me + 2 * z.count - far - 1, z.count)
        next_one, near = window(i, bottoms, s, block, last - rest)
        fix = 6.0 * weights[i] * CX[i] * wall_speed
        value = (1.0 - weight) * near + weight * next_one
        put(i, value + fix if CX[i] else value)


def wall_slot(i):
    return rising.index(i) if CY[i] == 1 else len(rising) + falling.index(i)


def first_kernel(z, whole_hbm, part_hbm, pop_hbm, solid_hbm, post_ref, acc_ref, mask_ref, info_ref, *refs):
    sends, (whole_ref, part_ref, pop_ref, solid_ref, sems) = refs[: z.count - 1], refs[z.count - 1 :]
    group = z.planes // CHUNKS * z.depth
    copies = [pltpu.make_async_copy(solid_hbm, solid_ref, sems.at[CHUNKS])]
    for k in range(CHUNKS):
        part = (slice(None), pl.ds(k * group, group), slice(None))
        copies.append(pltpu.make_async_copy(pop_hbm.at[part], pop_ref.at[part], sems.at[k]))
    copies.append(pltpu.make_async_copy(whole_hbm, whole_ref, sems.at[CHUNKS + 1]))
    copies.append(pltpu.make_async_copy(part_hbm, part_ref, sems.at[CHUNKS + 2]))
    for copy in copies:
        copy.start()
    copies[0].wait()
    grow = lax.broadcasted_iota(jnp.int32, (z.wide, z.width), 1) // BLOCK
    grow = grow == lax.broadcasted_iota(jnp.int32, (z.wide, z.width), 0)
    grow = grow.astype(jnp.float32)
    for k in range(solid_ref.shape[0]):
        flags = jnp.where(solid_ref[k] > 0, 1.0, 0.0)
        line = jnp.dot(flags, grow, preferred_element_type=jnp.float32)
        mask_ref[pl.ds(k * z.deep, z.deep), :] = line
    for y in range(z.planes):
        if y % (z.planes // CHUNKS) == 0:
            copies[1 + y // (z.planes // CHUNKS)].wait()
        solid = z.solid_tile(mask_ref, y) > 0.5
        f = [z.tile(pop_ref, i, y) * np.float32(weights[i]) for i in range(Q)]
        post, jx, moment_xy = collide(f, solid)
        here = pl.ds(y * z.depth, z.depth)
        for i in range(Q):
            post_ref[i, here, :] = post[i]
        acc_ref[0, here, :] = jnp.where(solid, 0.0, jx)
        acc_ref[1, here, :] = jnp.where(solid, 0.0, -(1.0 - 0.5 * visc_rate) * moment_xy)
    copies[-2].wait()
    copies[-1].wait()
    for step in range(whole_ref.shape[0]):
        for k, ref in enumerate((whole_ref, part_ref)):
            value = ref[step].astype(jnp.float32)
            info_ref[pl.ds(2 * step + k, 1), :] = jnp.full((1, z.width), value, jnp.float32)
    pack_x(z, whole_ref[0], post_ref, sends)


def shift_of(info_ref, step):
    values = [jnp.max(info_ref[2 * step + k : 2 * step + k + 1, :]) for k in range(2)]
    return [value.astype(jnp.int32) for value in values]


def second_kernel(z, info_ref, post_ref, mask_ref, *refs):
    gets, outs = refs[: z.count - 1], refs[z.count - 1 : z.count + 3]
    inner_ref, outer_ref, wall_ref, side_ref = outs
    tops, bottoms, edges, rows_ref = refs[z.count + 3 :]
    whole, part = shift_of(info_ref, 0)
    left, right = fill_tables(z, post_ref, gets, tops, bottoms, edges)
    side_ref[0], side_ref[1] = left, right
    columns = {1: left.T, -1: right.T}
    shape = (z.planes, z.width)
    lanes = lax.broadcasted_iota(jnp.int32, shape, 1)
    heights = lax.broadcasted_iota(jnp.int32, shape, 0)
    even = lax.rem(lax.axis_index("gz"), 2) == 0

    def line(i, row):
        value = post_ref[i, pl.ds(row, z.planes, stride=z.depth), :]
        if CX[i]:
            j = (eastward if CX[i] == 1 else westward).index(i)
            column = columns[CX[i]][j * z.planes : (j + 1) * z.planes, row : row + 1]
            edge = 0 if CX[i] == 1 else z.width - 1
            value = jnp.where(lanes == edge, jnp.broadcast_to(column, shape), roll(value, CX[i]))
        if CY[i]:
            enter = 0 if CY[i] == 1 else z.planes - 1
            wall = jnp.broadcast_to(wall_ref[wall_slot(i), row : row + 1, :], shape)
            value = jnp.where(heights == enter, wall, roll(value, CY[i], 0))
        return value

    jobs = []
    for side in range(2):
        near, far = (z.depth - 1, z.depth - 2) if side == 0 else (0, 1)
        for k in range(Q):
            row = near if CZ[k] >= 0 else far
            i = k if CZ[k] >= 0 else mirror[k]
            jobs.append((side, k, i if side == 0 else mirror[i], row))
    for still in (True, False):
        for side, k, i, row in jobs:
            if (CY[i] == 0) == still:
                rows_ref[side, k] = line(i, row)
        if still:

            def put(i, value):
                wall_ref[wall_slot(i)] = value

            sliding(z, whole, part, tops, bottoms, edges, put)

    chunk = min(8, z.planes)
    for start in range(0, z.planes, chunk):
        here = pl.ds(start, chunk)
        found = []
        for side in range(2):
            f = [None] * Q
            for i in level:
                f[i] = rows_ref[side, i, here, :]
            for i in upward:
                f[i] = rows_ref[side, mirror[i], here, :]
            kept, others = moments(f)
            change = relax(others)
            values = [rows_ref[side, i, here, :] for i in upward]
            values += [f[i] - change[i] for i in upward]
            found.append(values + kept)
        for slot in range(MASK):
            up, down = found[0][slot], found[1][slot]
            inner_ref[slot, here, :] = jnp.where(even, up, down)
            outer_ref[slot, here, :] = jnp.where(even, down, up)
    for k in range(z.planes // BLOCK):
        up = mask_ref[(k + 1) * z.deep - 1 : (k + 1) * z.deep, :]
        down = mask_ref[k * z.deep : k * z.deep + 1, :]
        here = pl.ds(k * BLOCK, BLOCK)
        block = (BLOCK, z.width)
        inner_ref[MASK, here, :] = jnp.broadcast_to(jnp.where(even, up, down), block)
        outer_ref[MASK, here, :] = jnp.broadcast_to(jnp.where(even, down, up), block)


def bulk_kernel(z, post_ref, wall_ref, side_ref, h_ref):
    left, right = side_ref[0], side_ref[1]
    for i in range(Q):
        for y in range(z.planes):
            here = pl.ds(y * z.depth, z.depth)
            if 0 <= y - CY[i] < z.planes:
                h_ref[i, here, :] = moved_x(z, post_ref, i, y - CY[i], left, right)
            else:
                h_ref[i, here, :] = wall_ref[wall_slot(i)]


def third_kernel(z, info_ref, h_ref, inner_ref, outer_ref, mask_ref, old_ref, *refs):
    (g_ref, acc_ref, part_ref), sends = refs[:3], refs[3 : 2 + z.count]
    sides, extra = refs[2 + z.count :]
    whole, _ = shift_of(info_ref, 1)
    even = lax.rem(lax.axis_index("gz"), 2) == 0
    sides[jnp.where(even, 1, 0)] = inner_ref[...]
    sides[jnp.where(even, 0, 1)] = outer_ref[...]
    chunk = min(8, z.planes)
    for side in range(2):
        for start in range(0, z.planes, chunk):
            here = pl.ds(start, chunk)
            row = start * z.depth + (0 if side == 0 else z.depth - 1)
            f = [None] * Q
            for i in downward:
                k = i if side == 0 else mirror[i]
                f[i] = h_ref[k, pl.ds(row, chunk, stride=z.depth), :]
            kept, others = moments(f)
            kept = [plus(kept[k], sides[side, SUMS + k, here, :]) for k in range(4)]
            change = relax([minus(m, e) for m, e in zip(others, equilibrium(*kept))])
            solid = sides[side, MASK, here, :] > 0.5
            for s, i in enumerate(upward):
                value = sides[side, PART + s, here, :] - change[i]
                extra[side, s, here, :] = jnp.where(solid, f[opposite[i]], value)
    rows, lanes = z.rows(), z.lanes()

    def moved(i, y, value, table, slot):
        if CZ[i] == 1:
            line = z.spread(table[0, slot(i), pl.ds(y, 1), :])
            return jnp.where(rows == 0, line, roll(value, 1, 0))
        if CZ[i] == -1:
            line = z.spread(table[1, slot(mirror[i]), pl.ds(y, 1), :])
            return jnp.where(rows == z.depth - 1, line, roll(value, -1, 0))
        return value

    sums = jnp.zeros((z.depth, z.width), jnp.float32)
    for y in range(z.planes):
        solid = z.solid_tile(mask_ref, y) > 0.5
        f = [moved(i, y, z.tile(h_ref, i, y), sides, upward.index) for i in range(Q)]
        post, jx, moment_xy = collide(f, solid)
        here = pl.ds(y * z.depth, z.depth)
        for i in range(Q):
            g_ref[i, here, :] = moved(i, y, post[i], extra, upward.index)
        fields = [jx, -(1.0 - 0.5 * visc_rate) * moment_xy]
        for k in range(2):
            value = old_ref[k, here, :] + jnp.where(solid, 0.0, fields[k])
            acc_ref[k, here, :] = value
            total = z.spread(jnp.sum(value, axis=1, keepdims=True))
            sums = jnp.where(lanes == k * z.planes + y, total, sums)
    part_ref[...] = sums
    pack_x(z, whole, g_ref, sends, sums)


def direct_kernel(z, g_ref, acc_ref, out_hbm, acc_hbm, sems):
    inner = (z.planes - 1) * z.depth
    copies = [pltpu.make_async_copy(acc_ref, acc_hbm, sems.at[len(straight)])]
    copies[0].start()
    for k, i in enumerate(straight):
        source, target = g_ref.at[i], out_hbm.at[i]
        if CY[i] == 1:
            source, target = source.at[pl.ds(0, inner), :], target.at[pl.ds(z.depth, inner), :]
        elif CY[i] == -1:
            source, target = source.at[pl.ds(z.depth, inner), :], target.at[pl.ds(0, inner), :]
        copies.append(pltpu.make_async_copy(source, target, sems.at[k]))
        copies[-1].start()
    for copy in copies:
        copy.wait()


def fourth_kernel(z, info_ref, g_ref, own_ref, *refs):
    gets, (_, out_hbm, profile_hbm) = refs[: z.count - 1], refs[z.count - 1 : z.count + 2]
    tops, bottoms, edges, out_ref, profile_ref, sems = refs[z.count + 2 :]
    whole, part = shift_of(info_ref, 1)
    terms = [own_ref[...]] + [gets[d - 1][z.slots(d)] for d in range(1, z.count)]
    while len(terms) > 1:
        terms = [terms[k] + terms[k + 1] for k in range(0, len(terms), 2)]
    for k in range(2):
        profile_ref[k] = terms[0][:, k * z.planes : (k + 1) * z.planes]
    copies = []

    def send(source, target):
        copies.append(pltpu.make_async_copy(source, target, sems.at[len(copies)]))
        copies[-1].start()

    send(profile_ref, profile_hbm)
    left, right = fill_tables(z, g_ref, gets, tops, bottoms, edges)
    group = z.planes // CHUNKS

    def interior(k):
        for i in slanted:
            for y in range(k * group, (k + 1) * group):
                if 0 <= y - CY[i] < z.planes:
                    here = pl.ds(y * z.depth, z.depth)
                    out_ref[i, here, :] = moved_x(z, g_ref, i, y - CY[i], left, right)

    def finish(k):
        here = pl.ds(k * group * z.depth, group * z.depth)
        for first, last in SPANS:
            part = (pl.ds(first, last - first), here, slice(None))
            send(out_ref.at[part], out_hbm.at[part])

    for k in range(1, CHUNKS - 1):
        interior(k)
        finish(k)

    def put(i, value):
        here = pl.ds(0 if CY[i] == 1 else (z.planes - 1) * z.depth, z.depth)
        out_ref[i, here, :] = value
        if CX[i] == 0:
            send(out_ref.at[i, here, :], out_hbm.at[i, here, :])

    sliding(z, whole, part, tops, bottoms, edges, put)
    for k in (0, CHUNKS - 1):
        interior(k)
        finish(k)
    for copy in copies:
        copy.wait()


def local(count, ranks, pop_ratio, solid_blocks, shift_whole, shift_frac):
    _, planes, depth, width = pop_ratio.shape
    z = Sizes(planes, depth, width, count)
    assert ranks % 2 == 0
    f32 = lambda *shape: pltpu.VMEM(shape, jnp.float32)
    hbm = lambda ref: jax.ShapeDtypeStruct(ref.shape, ref.dtype)
    keep = lambda *values: [pltpu.with_memory_space_constraint(v, pltpu.VMEM) for v in values]
    vmem = pl.BlockSpec(memory_space=pltpu.VMEM)
    outside = pl.BlockSpec(memory_space=pl.ANY)
    cells = f32(Q, planes * depth, width)
    fields = f32(2, planes * depth, width)
    halo = f32(SLOTS, planes, width)
    shifts = [pltpu.VMEM((count, len(rising), depth, width), jnp.float32)] * 2
    shifts.append(pltpu.VMEM((count, depth, width), jnp.float32))
    pair = pltpu.SMEM(shift_whole.shape, jnp.int32)
    sems = lambda number: pltpu.SemaphoreType.DMA((number,))
    outer_keep = lambda *values: [pltpu.with_memory_space_constraint(v, pltpu.HBM) for v in values]
    shift_whole, shift_frac, solid_blocks = outer_keep(shift_whole, shift_frac, solid_blocks)

    def buffers(more):
        return [f32(z.slots(d) + more, depth, width) for d in range(1, count)]

    def call(body, ins, outs, scratch=(), direct=(), alias=None):
        specs = [outside if k in direct else vmem for k in range(len(outs))]
        return pl.pallas_call(
            functools.partial(body, z),
            out_shape=outs,
            in_specs=ins,
            out_specs=specs,
            scratch_shapes=list(scratch),
            input_output_aliases=alias or {},
            compiler_params=pltpu.CompilerParams(vmem_limit_bytes=8 << 20),
        )

    def swap_x(values):
        return [
            lax.ppermute(values[d - 1], "gx", [(i, i ^ d) for i in range(count)])
            for d in range(1, count)
        ]

    pairs = [(i, i ^ 1) for i in range(ranks)]
    across = [(i, (i - 1 if i % 2 == 0 else i + 1) % ranks) for i in range(ranks)]

    (pop,) = outer_keep(pop_ratio.reshape(cells.shape))
    post, old, mask, info, *sends = call(
        first_kernel,
        [outside] * 4,
        [cells, fields, f32(planes // BLOCK * z.deep, width), f32(2 * shift_whole.shape[0], width)] + buffers(0),
        [pair, pair, cells, pltpu.VMEM(solid_blocks.shape, jnp.int32), sems(CHUNKS + 3)],
    )(shift_whole, shift_frac, pop, solid_blocks)
    gets = swap_x(sends)
    walls, both = f32(2 * len(rising), depth, width), f32(2, depth, width)
    inner, outer, wall, side = call(
        second_kernel,
        [vmem] * (2 + count),
        [halo, halo, walls, both],
        shifts + [f32(2, Q, planes, width)],
    )(*keep(info, post, mask, *gets))
    outer = lax.ppermute(outer, "gz", across)
    inner = lax.ppermute(inner, "gz", pairs)
    (h,) = call(bulk_kernel, [vmem] * 3, [cells])(*keep(post, wall, side))
    g, acc, own, *sends = call(
        third_kernel,
        [vmem] * 6,
        [cells, fields, f32(depth, width)] + buffers(1),
        [
            pltpu.VMEM((2, SLOTS, planes, width), jnp.float32),
            pltpu.VMEM((2, len(upward), planes, width), jnp.float32),
        ],
    )(*keep(info, h, inner, outer, mask, old))
    gets = swap_x(sends)
    out, acc = call(
        direct_kernel, [vmem] * 2, [hbm(cells), hbm(fields)], [sems(len(straight) + 1)], [0, 1]
    )(*keep(g, acc))
    moves = 1 + len(SPANS) * CHUNKS + sum(CX[i] == 0 for i in rising + falling)
    out, profile = call(
        fourth_kernel,
        [vmem] * (2 + count) + [outside],
        [hbm(cells), hbm(f32(2, depth, planes))],
        shifts + [cells, f32(2, depth, planes), sems(moves)],
        [0, 1],
        {2 + count: 0},
    )(*keep(info, g, own, *gets), out)
    return (
        out.reshape(pop_ratio.shape),
        acc.reshape(2, planes, depth, width),
        jnp.swapaxes(profile, 1, 2),
    )


def solution(mesh):
    return jax.shard_map(
        functools.partial(local, mesh.shape["gx"], mesh.shape["gz"]),
        mesh=mesh,
        in_specs=(P(None, None, "gz", "gx"), P(None, "gz", "gx"), P(), P()),
        out_specs=(P(None, None, "gz", "gx"), P(None, None, "gz", "gx"), P(None, None, "gz")),
        check_vma=False,
    )
```

```python
import functools

import jax
import jax.numpy as jnp
import numpy as np
from jax import lax
from jax.experimental import pallas as pl
from jax.experimental.pallas import tpu as pltpu
from jax.sharding import PartitionSpec as P


BLOCK = 4
velocity_list = [
    (0, 0, 0),
    (1, 0, 0),
    (-1, 0, 0),
    (0, 1, 0),
    (0, -1, 0),
    (0, 0, 1),
    (0, 0, -1),
    (1, 1, 0),
    (-1, -1, 0),
    (1, -1, 0),
    (-1, 1, 0),
    (1, 0, 1),
    (-1, 0, -1),
    (1, 0, -1),
    (-1, 0, 1),
    (0, 1, 1),
    (0, -1, -1),
    (0, 1, -1),
    (0, -1, 1),
]
Q = len(velocity_list)
weights = [1.0 / 3.0] + [1.0 / 18.0] * 6 + [1.0 / 36.0] * 12
CX = [v[0] for v in velocity_list]
CY = [v[1] for v in velocity_list]
CZ = [v[2] for v in velocity_list]
opposite = [velocity_list.index((-x, -y, -z)) for x, y, z in velocity_list]
mirror = [velocity_list.index((x, y, -z)) for x, y, z in velocity_list]
rising = [i for i in range(Q) if CY[i] == 1]
falling = [i for i in range(Q) if CY[i] == -1]
eastward = [i for i in range(Q) if CX[i] == 1]
westward = [i for i in range(Q) if CX[i] == -1]
upward = [i for i in range(Q) if CZ[i] == 1]
level = [i for i in range(Q) if CZ[i] == 0]
downward = [mirror[i] for i in upward]
straight = [i for i in range(Q) if CX[i] == 0]
slanted = [i for i in range(Q) if CX[i] != 0]
SPANS = [(i, next(k for k in range(i, Q + 1) if k == Q or CX[k] == 0)) for i in slanted if CX[i - 1] == 0]
PART, SUMS = len(upward), 2 * len(upward)
MASK = SUMS + 4
SLOTS = MASK + 1
wall_speed = 0.08
visc_rate = 1.25
fraction_unit = 4096.0
relax_rates = [0.0, 1.19, 1.4, 0.0, 1.2, 0.0, 1.2, 0.0, 1.2, 1.25, 1.4, 1.25, 1.4]
relax_rates += [1.25, 1.25, 1.25, 1.98, 1.98, 1.98]


def row_norms():
    v = np.array(velocity_list, dtype=np.float64)
    x, y, z = v[:, 0], v[:, 1], v[:, 2]
    s = x * x + y * y + z * z
    rows = [
        np.ones(Q),
        19 * s - 30,
        (21 * s * s - 53 * s + 24) / 2,
        x,
        (5 * s - 9) * x,
        y,
        (5 * s - 9) * y,
        z,
        (5 * s - 9) * z,
        3 * x * x - s,
        (3 * s - 5) * (3 * x * x - s),
        y * y - z * z,
        (3 * s - 5) * (y * y - z * z),
        x * y,
        y * z,
        x * z,
        (y * y - z * z) * x,
        (z * z - x * x) * y,
        (x * x - y * y) * z,
    ]
    return [float(np.sum(row * row)) for row in rows]


RATE = [rate / norm for rate, norm in zip(relax_rates, row_norms())]


def plus(a, b):
    return b if a is None else a if b is None else a + b


def minus(a, b):
    return a if b is None else -b if a is None else a - b


def scaled(factor, a):
    return None if a is None else factor * a


def moments(f):
    sums = {i: plus(f[i], f[i + 1]) for i in range(1, Q, 2)}
    difs = {i: minus(f[i], f[i + 1]) for i in range(1, Q, 2)}
    p1, d1 = plus(sums[7], sums[9]), minus(sums[7], sums[9])
    p2, d2 = plus(sums[11], sums[13]), minus(sums[11], sums[13])
    p3, d3 = plus(sums[15], sums[17]), minus(sums[15], sums[17])
    s23 = plus(sums[3], sums[5])
    axis = plus(sums[1], s23)
    p12 = plus(p1, p2)
    diag = plus(p12, p3)
    a, c = plus(difs[7], difs[9]), minus(difs[7], difs[9])
    b, e = plus(difs[11], difs[13]), minus(difs[11], difs[13])
    d, g = plus(difs[15], difs[17]), minus(difs[15], difs[17])
    ab, cd, eg = plus(a, b), plus(c, d), plus(e, g)
    axis_x, diag_x = minus(scaled(2.0, sums[1]), s23), minus(p12, scaled(2.0, p3))
    axis_w, diag_w = minus(sums[3], sums[5]), minus(p1, p2)
    kept = [
        plus(f[0], plus(axis, diag)),
        plus(difs[1], ab),
        plus(difs[3], cd),
        plus(difs[5], eg),
    ]
    others = [
        minus(diag, f[0]),
        minus(plus(f[0], diag), scaled(2.0, axis)),
        minus(ab, scaled(2.0, difs[1])),
        minus(cd, scaled(2.0, difs[3])),
        minus(eg, scaled(2.0, difs[5])),
        plus(axis_x, diag_x),
        minus(diag_x, scaled(2.0, axis_x)),
        plus(axis_w, diag_w),
        minus(diag_w, scaled(2.0, axis_w)),
        d1,
        d3,
        d2,
        minus(a, b),
        minus(d, c),
        minus(e, g),
    ]
    return kept, others


def equilibrium(rho, jx, jy, jz):
    inverse = 1.0 / rho
    ux, uy, uz = jx * inverse, jy * inverse, jz * inverse
    xx, yy, zz = jx * ux, jy * uy, jz * uz
    yz_sum, yz_dif = yy + zz, yy - zz
    square = xx + yz_sum
    eq_x = 2.0 * xx - yz_sum
    eq = [square, None, None, None, None]
    eq += [eq_x, -0.5 * eq_x, yz_dif, -0.5 * yz_dif, jx * uy, jy * uz, jx * uz]
    return eq + [None] * 3


ORDER = [4, 6, 8, 9, 10, 11, 12, 13, 14, 15, 16, 17, 18]
FLOW = 5.0 / 3.0


def relax(moment):
    level_a, level_c = moment[:2]
    factors = [RATE[k] * (FLOW if k in (4, 6, 8) else 1.0) for k in ORDER]
    scaled_by = [scaled(k, m) for k, m in zip(factors, moment[2:])]
    flow_x, flow_y, flow_z, even_x, even_px, even_w, even_pw = scaled_by[:7]
    even_xy, even_yz, even_xz, twist_x, twist_y, twist_z = scaled_by[7:]

    def blend(by_e, by_s):
        rate_e, rate_s = by_e * RATE[1], by_s * RATE[2]
        return plus(scaled(19.0 * rate_e - 5.5 * rate_s, level_a), scaled(3.5 * rate_s, level_c))

    base_axis = blend(-11.0, -4.0)
    base_diag = blend(8.0, 1.0)
    lean = minus(even_x, scaled(2.0, even_px))
    tilt = minus(even_w, scaled(2.0, even_pw))
    side_x, side_w = plus(even_x, even_px), plus(even_w, even_pw)
    flat = plus(base_diag, side_x)
    diag_xy, diag_xz = plus(flat, side_w), minus(flat, side_w)
    diag_yz = minus(base_diag, scaled(2.0, side_x))
    low = minus(base_axis, lean)
    even = {
        1: plus(base_axis, scaled(2.0, lean)),
        3: plus(low, tilt),
        5: minus(low, tilt),
        7: plus(diag_xy, even_xy),
        9: minus(diag_xy, even_xy),
        11: plus(diag_xz, even_xz),
        13: minus(diag_xz, even_xz),
        15: plus(diag_yz, even_yz),
        17: minus(diag_yz, even_yz),
    }
    x_up, x_down = plus(flow_x, twist_x), minus(flow_x, twist_x)
    y_up, y_down = plus(flow_y, twist_y), minus(flow_y, twist_y)
    z_up, z_down = plus(flow_z, twist_z), minus(flow_z, twist_z)
    odd = {
        1: scaled(-4.0, flow_x),
        3: scaled(-4.0, flow_y),
        5: scaled(-4.0, flow_z),
        7: plus(x_up, y_down),
        9: minus(x_up, y_down),
        11: plus(x_down, z_up),
        13: minus(x_down, z_up),
        15: plus(y_up, z_down),
        17: minus(y_up, z_down),
    }
    out = [blend(-30.0, 12.0)]
    for i in range(1, Q, 2):
        out += [plus(even[i], odd[i]), minus(even[i], odd[i])]
    return out


def collide(f, solid):
    kept, others = moments(f)
    rest = [minus(m, e) for m, e in zip(others, equilibrium(*kept))]
    change = relax(rest)
    post = [jnp.where(solid, f[opposite[i]], f[i] - change[i]) for i in range(Q)]
    return post, kept[1], rest[9]


CHUNKS = 4


class Sizes:
    def __init__(self, planes, depth, width, count):
        self.planes, self.depth, self.width, self.count = planes, depth, width, count
        self.deep, self.wide = depth // BLOCK, width // BLOCK
        assert count >= 4 and count & (count - 1) == 0
        assert len(eastward) * planes + 4 <= width and 2 * planes <= width

    def slots(self, delta):
        return (2 if delta == self.count // 2 else 1) * len(rising) + 1

    def tile(self, ref, i, y):
        return ref[i, pl.ds(y * self.depth, self.depth), :]

    def lanes(self):
        return lax.broadcasted_iota(jnp.int32, (self.depth, self.width), 1)

    def rows(self):
        return lax.broadcasted_iota(jnp.int32, (self.depth, self.width), 0)

    def spread(self, row):
        return jnp.broadcast_to(row, (self.depth, self.width))

    def solid_tile(self, mask_ref, y):
        base = y // BLOCK * self.deep
        out = self.spread(mask_ref[base : base + 1, :])
        rows = self.rows()
        for step in range(1, self.deep):
            line = self.spread(mask_ref[base + step : base + step + 1, :])
            out = jnp.where(rows >= step * BLOCK, line, out)
        return out


def roll(value, shift, axis=1):
    shift = shift % value.shape[axis]
    return pltpu.roll(value, shift, axis) if shift else value


def edge_columns(z):
    return [
        (7, z.planes - 1, True),
        (10, z.planes - 1, False),
        (9, 0, True),
        (8, 0, False),
    ]


def wall_columns(z, ref, lanes):
    out = jnp.zeros((z.depth, z.width), jnp.float32)
    start = len(eastward) * z.planes
    for k, (i, y, right) in enumerate(edge_columns(z)):
        at = start + k
        moved = roll(z.tile(ref, i, y), at - (z.width - 1 if right else 0))
        out = jnp.where(lanes == at, moved, out)
    return out


def pack_x(z, whole, ref, sends, extra=None):
    me = lax.axis_index("gx")
    lanes = z.lanes()
    right_edge = wall_columns(z, ref, lanes)
    left_edge = right_edge
    for j in range(len(eastward)):
        for y in range(z.planes):
            at = j * z.planes + y
            hit = lanes == at
            moved = roll(z.tile(ref, eastward[j], y), at - (z.width - 1))
            right_edge = jnp.where(hit, moved, right_edge)
            moved = roll(z.tile(ref, westward[j], y), at)
            left_edge = jnp.where(hit, moved, left_edge)
    far = lax.div(whole, z.width)
    for delta in range(1, z.count):
        send = sends[delta - 1]
        partner = jnp.bitwise_xor(me, delta)
        ahead = lax.rem(me - partner + z.count, z.count)
        at_top = (ahead == far) | (ahead == lax.rem(far + 1, z.count))
        for s in range(len(rising)):
            top = z.tile(ref, rising[s], z.planes - 1)
            bottom = z.tile(ref, falling[s], 0)
            if delta == z.count // 2:
                send[s] = top
                send[len(rising) + s] = bottom
            else:
                send[s] = jnp.where(at_top, top, bottom)
        to_right = partner == lax.rem(me + 1, z.count)
        slots = z.slots(delta)
        send[slots - 1] = jnp.where(to_right, right_edge, left_edge)
        if extra is not None:
            send[slots] = extra


def fill_tables(z, ref, gets, tops, bottoms, edges):
    me = lax.axis_index("gx")
    for s in range(len(rising)):
        tops[me, s] = z.tile(ref, rising[s], z.planes - 1)
        bottoms[me, s] = z.tile(ref, falling[s], 0)
    edges[me] = wall_columns(z, ref, z.lanes())
    for delta in range(1, z.count):
        get = gets[delta - 1]
        partner = jnp.bitwise_xor(me, delta)
        for s in range(len(rising)):
            tops[partner, s] = get[s]
            second = len(rising) + s if delta == z.count // 2 else s
            bottoms[partner, s] = get[second]
        edges[partner] = get[z.slots(delta) - 1]
    left = edges[lax.rem(me + z.count - 1, z.count)]
    right = edges[lax.rem(me + 1, z.count)]
    return left, right


def mended(z, value, i, y, left, right):
    lanes, last = z.lanes(), z.width - 1
    if CX[i] == 1:
        at = eastward.index(i) * z.planes + y
        return jnp.where(lanes == 0, roll(left, -at), value)
    if CX[i] == -1:
        at = westward.index(i) * z.planes + y
        return jnp.where(lanes == last, roll(right, last - at), value)
    return value


def moved_x(z, ref, i, y, left, right):
    return mended(z, roll(z.tile(ref, i, y), CX[i]), i, y, left, right)


def sliding(z, whole, part, tops, bottoms, edges, put):
    me = lax.axis_index("gx")
    lanes, last = z.lanes(), z.width - 1
    weight = part.astype(jnp.float32) / fraction_unit
    far = lax.div(whole, z.width)
    rest = lax.rem(whole, z.width)
    start = len(eastward) * z.planes
    columns = {i: start + k for k, (i, _, _) in enumerate(edge_columns(z))}

    def window(i, planes, s, block, offset):
        pair = []
        for step in range(2):
            here = lax.rem(block + step, z.count)
            value = planes[here, s]
            if CX[i] == 1:
                side = edges[lax.rem(here + z.count - 1, z.count)]
                value = jnp.where(lanes == 0, roll(side, -columns[i]), roll(value, 1))
            elif CX[i] == -1:
                side = edges[lax.rem(here + 1, z.count)]
                value = jnp.where(lanes == last, roll(side, last - columns[i]), roll(value, -1))
            pair.append(value)
        first = jnp.where(lanes >= offset, pair[0], pair[1])
        second = jnp.where(lanes > offset, pair[0], pair[1])
        first = pltpu.roll(first, lax.rem(z.width - offset, z.width), 1)
        second = pltpu.roll(second, last - offset, 1)
        return first, second

    for s, i in enumerate(rising):
        near, next_one = window(i, tops, s, lax.rem(me + far, z.count), rest)
        fix = 6.0 * weights[i] * CX[i] * wall_speed
        value = (1.0 - weight) * near + weight * next_one
        put(i, value - fix if CX[i] else value)
    for s, i in enumerate(falling):
        block = lax.rem(me + 2 * z.count - far - 1, z.count)
        next_one, near = window(i, bottoms, s, block, last - rest)
        fix = 6.0 * weights[i] * CX[i] * wall_speed
        value = (1.0 - weight) * near + weight * next_one
        put(i, value + fix if CX[i] else value)


def wall_slot(i):
    return rising.index(i) if CY[i] == 1 else len(rising) + falling.index(i)


def first_kernel(z, whole_hbm, part_hbm, pop_hbm, solid_hbm, post_ref, acc_ref, mask_ref, info_ref, *refs):
    sends, (whole_ref, part_ref, pop_ref, solid_ref, sems) = refs[: z.count - 1], refs[z.count - 1 :]
    group = z.planes // CHUNKS * z.depth
    copies = [pltpu.make_async_copy(solid_hbm, solid_ref, sems.at[CHUNKS])]
    for k in range(CHUNKS):
        part = (slice(None), pl.ds(k * group, group), slice(None))
        copies.append(pltpu.make_async_copy(pop_hbm.at[part], pop_ref.at[part], sems.at[k]))
    copies.append(pltpu.make_async_copy(whole_hbm, whole_ref, sems.at[CHUNKS + 1]))
    copies.append(pltpu.make_async_copy(part_hbm, part_ref, sems.at[CHUNKS + 2]))
    for copy in copies:
        copy.start()
    copies[0].wait()
    grow = lax.broadcasted_iota(jnp.int32, (z.wide, z.width), 1) // BLOCK
    grow = grow == lax.broadcasted_iota(jnp.int32, (z.wide, z.width), 0)
    grow = grow.astype(jnp.float32)
    for k in range(solid_ref.shape[0]):
        flags = jnp.where(solid_ref[k] > 0, 1.0, 0.0)
        line = jnp.dot(flags, grow, preferred_element_type=jnp.float32)
        mask_ref[pl.ds(k * z.deep, z.deep), :] = line
    for y in range(z.planes):
        if y % (z.planes // CHUNKS) == 0:
            copies[1 + y // (z.planes // CHUNKS)].wait()
        solid = z.solid_tile(mask_ref, y) > 0.5
        f = [z.tile(pop_ref, i, y) * np.float32(weights[i]) for i in range(Q)]
        post, jx, moment_xy = collide(f, solid)
        here = pl.ds(y * z.depth, z.depth)
        for i in range(Q):
            post_ref[i, here, :] = post[i]
        acc_ref[0, here, :] = jnp.where(solid, 0.0, jx)
        acc_ref[1, here, :] = jnp.where(solid, 0.0, -(1.0 - 0.5 * visc_rate) * moment_xy)
    copies[-2].wait()
    copies[-1].wait()
    for step in range(whole_ref.shape[0]):
        for k, ref in enumerate((whole_ref, part_ref)):
            value = ref[step].astype(jnp.float32)
            info_ref[pl.ds(2 * step + k, 1), :] = jnp.full((1, z.width), value, jnp.float32)
    pack_x(z, whole_ref[0], post_ref, sends)


def shift_of(info_ref, step):
    values = [jnp.max(info_ref[2 * step + k : 2 * step + k + 1, :]) for k in range(2)]
    return [value.astype(jnp.int32) for value in values]


def second_kernel(z, info_ref, post_ref, mask_ref, *refs):
    gets, outs = refs[: z.count - 1], refs[z.count - 1 : z.count + 3]
    inner_ref, outer_ref, wall_ref, side_ref = outs
    tops, bottoms, edges, rows_ref = refs[z.count + 3 :]
    whole, part = shift_of(info_ref, 0)
    left, right = fill_tables(z, post_ref, gets, tops, bottoms, edges)
    side_ref[0], side_ref[1] = left, right
    columns = {1: left.T, -1: right.T}
    shape = (z.planes, z.width)
    lanes = lax.broadcasted_iota(jnp.int32, shape, 1)
    heights = lax.broadcasted_iota(jnp.int32, shape, 0)
    even = lax.rem(lax.axis_index("gz"), 2) == 0

    def line(i, row):
        value = post_ref[i, pl.ds(row, z.planes, stride=z.depth), :]
        if CX[i]:
            j = (eastward if CX[i] == 1 else westward).index(i)
            column = columns[CX[i]][j * z.planes : (j + 1) * z.planes, row : row + 1]
            edge = 0 if CX[i] == 1 else z.width - 1
            value = jnp.where(lanes == edge, jnp.broadcast_to(column, shape), roll(value, CX[i]))
        if CY[i]:
            enter = 0 if CY[i] == 1 else z.planes - 1
            wall = jnp.broadcast_to(wall_ref[wall_slot(i), row : row + 1, :], shape)
            value = jnp.where(heights == enter, wall, roll(value, CY[i], 0))
        return value

    jobs = []
    for side in range(2):
        near, far = (z.depth - 1, z.depth - 2) if side == 0 else (0, 1)
        for k in range(Q):
            row = near if CZ[k] >= 0 else far
            i = k if CZ[k] >= 0 else mirror[k]
            jobs.append((side, k, i if side == 0 else mirror[i], row))
    for still in (True, False):
        for side, k, i, row in jobs:
            if (CY[i] == 0) == still:
                rows_ref[side, k] = line(i, row)
        if still:

            def put(i, value):
                wall_ref[wall_slot(i)] = value

            sliding(z, whole, part, tops, bottoms, edges, put)

    chunk = min(8, z.planes)
    for start in range(0, z.planes, chunk):
        here = pl.ds(start, chunk)
        found = []
        for side in range(2):
            f = [None] * Q
            for i in level:
                f[i] = rows_ref[side, i, here, :]
            for i in upward:
                f[i] = rows_ref[side, mirror[i], here, :]
            kept, others = moments(f)
            change = relax(others)
            values = [rows_ref[side, i, here, :] for i in upward]
            values += [f[i] - change[i] for i in upward]
            found.append(values + kept)
        for slot in range(MASK):
            up, down = found[0][slot], found[1][slot]
            inner_ref[slot, here, :] = jnp.where(even, up, down)
            outer_ref[slot, here, :] = jnp.where(even, down, up)
    for k in range(z.planes // BLOCK):
        up = mask_ref[(k + 1) * z.deep - 1 : (k + 1) * z.deep, :]
        down = mask_ref[k * z.deep : k * z.deep + 1, :]
        here = pl.ds(k * BLOCK, BLOCK)
        block = (BLOCK, z.width)
        inner_ref[MASK, here, :] = jnp.broadcast_to(jnp.where(even, up, down), block)
        outer_ref[MASK, here, :] = jnp.broadcast_to(jnp.where(even, down, up), block)


def bulk_kernel(z, post_ref, wall_ref, side_ref, h_ref):
    left, right = side_ref[0], side_ref[1]
    for i in range(Q):
        for y in range(z.planes):
            here = pl.ds(y * z.depth, z.depth)
            if 0 <= y - CY[i] < z.planes:
                h_ref[i, here, :] = moved_x(z, post_ref, i, y - CY[i], left, right)
            else:
                h_ref[i, here, :] = wall_ref[wall_slot(i)]


def third_kernel(z, info_ref, h_ref, inner_ref, outer_ref, mask_ref, old_ref, *refs):
    (g_ref, acc_ref, part_ref), sends = refs[:3], refs[3 : 2 + z.count]
    sides, extra = refs[2 + z.count :]
    whole, _ = shift_of(info_ref, 1)
    even = lax.rem(lax.axis_index("gz"), 2) == 0
    sides[jnp.where(even, 1, 0)] = inner_ref[...]
    sides[jnp.where(even, 0, 1)] = outer_ref[...]
    chunk = min(8, z.planes)
    for side in range(2):
        for start in range(0, z.planes, chunk):
            here = pl.ds(start, chunk)
            row = start * z.depth + (0 if side == 0 else z.depth - 1)
            f = [None] * Q
            for i in downward:
                k = i if side == 0 else mirror[i]
                f[i] = h_ref[k, pl.ds(row, chunk, stride=z.depth), :]
            kept, others = moments(f)
            kept = [plus(kept[k], sides[side, SUMS + k, here, :]) for k in range(4)]
            change = relax([minus(m, e) for m, e in zip(others, equilibrium(*kept))])
            solid = sides[side, MASK, here, :] > 0.5
            for s, i in enumerate(upward):
                value = sides[side, PART + s, here, :] - change[i]
                extra[side, s, here, :] = jnp.where(solid, f[opposite[i]], value)
    rows, lanes = z.rows(), z.lanes()

    def moved(i, y, value, table, slot):
        if CZ[i] == 1:
            line = z.spread(table[0, slot(i), pl.ds(y, 1), :])
            return jnp.where(rows == 0, line, roll(value, 1, 0))
        if CZ[i] == -1:
            line = z.spread(table[1, slot(mirror[i]), pl.ds(y, 1), :])
            return jnp.where(rows == z.depth - 1, line, roll(value, -1, 0))
        return value

    sums = jnp.zeros((z.depth, z.width), jnp.float32)
    for y in range(z.planes):
        solid = z.solid_tile(mask_ref, y) > 0.5
        f = [moved(i, y, z.tile(h_ref, i, y), sides, upward.index) for i in range(Q)]
        post, jx, moment_xy = collide(f, solid)
        here = pl.ds(y * z.depth, z.depth)
        for i in range(Q):
            g_ref[i, here, :] = moved(i, y, post[i], extra, upward.index)
        fields = [jx, -(1.0 - 0.5 * visc_rate) * moment_xy]
        for k in range(2):
            value = old_ref[k, here, :] + jnp.where(solid, 0.0, fields[k])
            acc_ref[k, here, :] = value
            total = z.spread(jnp.sum(value, axis=1, keepdims=True))
            sums = jnp.where(lanes == k * z.planes + y, total, sums)
    part_ref[...] = sums
    pack_x(z, whole, g_ref, sends, sums)


def direct_kernel(z, g_ref, acc_ref, out_hbm, acc_hbm, turned_ref, sems):
    inner = (z.planes - 1) * z.depth
    copies = [pltpu.make_async_copy(acc_ref, acc_hbm, sems.at[len(straight)])]
    copies[0].start()
    for k, i in enumerate(straight):
        source, target = g_ref.at[i], out_hbm.at[i]
        if CY[i] == 1:
            source, target = source.at[pl.ds(0, inner), :], target.at[pl.ds(z.depth, inner), :]
        elif CY[i] == -1:
            source, target = source.at[pl.ds(z.depth, inner), :], target.at[pl.ds(0, inner), :]
        copies.append(pltpu.make_async_copy(source, target, sems.at[k]))
        copies[-1].start()
    for k, i in enumerate(slanted):
        for y in range(z.planes):
            if 0 <= y - CY[i] < z.planes:
                here = pl.ds(y * z.depth, z.depth)
                turned_ref[k, here, :] = roll(z.tile(g_ref, i, y - CY[i]), CX[i])
    for copy in copies:
        copy.wait()


def fourth_kernel(z, info_ref, g_ref, turned_ref, own_ref, *refs):
    gets, (_, out_hbm, profile_hbm) = refs[: z.count - 1], refs[z.count - 1 : z.count + 2]
    tops, bottoms, edges, out_ref, profile_ref, sems = refs[z.count + 2 :]
    whole, part = shift_of(info_ref, 1)
    terms = [own_ref[...]] + [gets[d - 1][z.slots(d)] for d in range(1, z.count)]
    while len(terms) > 1:
        terms = [terms[k] + terms[k + 1] for k in range(0, len(terms), 2)]
    for k in range(2):
        profile_ref[k] = terms[0][:, k * z.planes : (k + 1) * z.planes]
    copies = []

    def send(source, target):
        copies.append(pltpu.make_async_copy(source, target, sems.at[len(copies)]))
        copies[-1].start()

    send(profile_ref, profile_hbm)
    left, right = fill_tables(z, g_ref, gets, tops, bottoms, edges)
    group = z.planes // CHUNKS

    def interior(k):
        for i in slanted:
            for y in range(k * group, (k + 1) * group):
                if 0 <= y - CY[i] < z.planes:
                    here = pl.ds(y * z.depth, z.depth)
                    value = turned_ref[slanted.index(i), here, :]
                    out_ref[i, here, :] = mended(z, value, i, y - CY[i], left, right)

    def finish(k):
        here = pl.ds(k * group * z.depth, group * z.depth)
        for first, last in SPANS:
            part = (pl.ds(first, last - first), here, slice(None))
            send(out_ref.at[part], out_hbm.at[part])

    def put(i, value):
        here = pl.ds(0 if CY[i] == 1 else (z.planes - 1) * z.depth, z.depth)
        out_ref[i, here, :] = value
        if CX[i] == 0:
            send(out_ref.at[i, here, :], out_hbm.at[i, here, :])

    sliding(z, whole, part, tops, bottoms, edges, put)
    for k in range(CHUNKS):
        interior(k)
        finish(k)
    for copy in copies:
        copy.wait()


def local(count, ranks, pop_ratio, solid_blocks, shift_whole, shift_frac):
    _, planes, depth, width = pop_ratio.shape
    z = Sizes(planes, depth, width, count)
    assert ranks % 2 == 0
    f32 = lambda *shape: pltpu.VMEM(shape, jnp.float32)
    hbm = lambda ref: jax.ShapeDtypeStruct(ref.shape, ref.dtype)
    keep = lambda *values: [pltpu.with_memory_space_constraint(v, pltpu.VMEM) for v in values]
    vmem = pl.BlockSpec(memory_space=pltpu.VMEM)
    outside = pl.BlockSpec(memory_space=pl.ANY)
    cells = f32(Q, planes * depth, width)
    fields = f32(2, planes * depth, width)
    halo = f32(SLOTS, planes, width)
    shifts = [pltpu.VMEM((count, len(rising), depth, width), jnp.float32)] * 2
    shifts.append(pltpu.VMEM((count, depth, width), jnp.float32))
    pair = pltpu.SMEM(shift_whole.shape, jnp.int32)
    sems = lambda number: pltpu.SemaphoreType.DMA((number,))
    outer_keep = lambda *values: [pltpu.with_memory_space_constraint(v, pltpu.HBM) for v in values]
    shift_whole, shift_frac, solid_blocks = outer_keep(shift_whole, shift_frac, solid_blocks)

    def buffers(more):
        return [f32(z.slots(d) + more, depth, width) for d in range(1, count)]

    def call(body, ins, outs, scratch=(), direct=(), alias=None):
        specs = [outside if k in direct else vmem for k in range(len(outs))]
        return pl.pallas_call(
            functools.partial(body, z),
            out_shape=outs,
            in_specs=ins,
            out_specs=specs,
            scratch_shapes=list(scratch),
            input_output_aliases=alias or {},
            compiler_params=pltpu.CompilerParams(vmem_limit_bytes=8 << 20),
        )

    def swap_x(values):
        return [
            lax.ppermute(values[d - 1], "gx", [(i, i ^ d) for i in range(count)])
            for d in range(1, count)
        ]

    pairs = [(i, i ^ 1) for i in range(ranks)]
    across = [(i, (i - 1 if i % 2 == 0 else i + 1) % ranks) for i in range(ranks)]

    (pop,) = outer_keep(pop_ratio.reshape(cells.shape))
    post, old, mask, info, *sends = call(
        first_kernel,
        [outside] * 4,
        [cells, fields, f32(planes // BLOCK * z.deep, width), f32(2 * shift_whole.shape[0], width)] + buffers(0),
        [pair, pair, cells, pltpu.VMEM(solid_blocks.shape, jnp.int32), sems(CHUNKS + 3)],
    )(shift_whole, shift_frac, pop, solid_blocks)
    gets = swap_x(sends)
    walls, both = f32(2 * len(rising), depth, width), f32(2, depth, width)
    inner, outer, wall, side = call(
        second_kernel,
        [vmem] * (2 + count),
        [halo, halo, walls, both],
        shifts + [f32(2, Q, planes, width)],
    )(*keep(info, post, mask, *gets))
    outer = lax.ppermute(outer, "gz", across)
    inner = lax.ppermute(inner, "gz", pairs)
    (h,) = call(bulk_kernel, [vmem] * 3, [cells])(*keep(post, wall, side))
    g, acc, own, *sends = call(
        third_kernel,
        [vmem] * 6,
        [cells, fields, f32(depth, width)] + buffers(1),
        [
            pltpu.VMEM((2, SLOTS, planes, width), jnp.float32),
            pltpu.VMEM((2, len(upward), planes, width), jnp.float32),
        ],
    )(*keep(info, h, inner, outer, mask, old))
    gets = swap_x(sends)
    turned = f32(len(slanted), planes * depth, width)
    out, acc, turned = call(
        direct_kernel,
        [vmem] * 2,
        [hbm(cells), hbm(fields), turned],
        [sems(len(straight) + 1)],
        [0, 1],
    )(*keep(g, acc))
    moves = 1 + len(SPANS) * CHUNKS + sum(CX[i] == 0 for i in rising + falling)
    out, profile = call(
        fourth_kernel,
        [vmem] * (3 + count) + [outside],
        [hbm(cells), hbm(f32(2, depth, planes))],
        shifts + [cells, f32(2, depth, planes), sems(moves)],
        [0, 1],
        {3 + count: 0},
    )(*keep(info, g, turned, own, *gets), out)
    return (
        out.reshape(pop_ratio.shape),
        acc.reshape(2, planes, depth, width),
        jnp.swapaxes(profile, 1, 2),
    )


def solution(mesh):
    return jax.shard_map(
        functools.partial(local, mesh.shape["gx"], mesh.shape["gz"]),
        mesh=mesh,
        in_specs=(P(None, None, "gz", "gx"), P(None, "gz", "gx"), P(), P()),
        out_specs=(P(None, None, "gz", "gx"), P(None, None, "gz", "gx"), P(None, None, "gz")),
        check_vma=False,
    )
```

```python
import functools

import jax
import jax.numpy as jnp
import numpy as np
from jax import lax
from jax.experimental import pallas as pl
from jax.experimental.pallas import tpu as pltpu
from jax.sharding import PartitionSpec as P


BLOCK = 4
velocity_list = [
    (0, 0, 0),
    (1, 0, 0),
    (-1, 0, 0),
    (0, 1, 0),
    (0, -1, 0),
    (0, 0, 1),
    (0, 0, -1),
    (1, 1, 0),
    (-1, -1, 0),
    (1, -1, 0),
    (-1, 1, 0),
    (1, 0, 1),
    (-1, 0, -1),
    (1, 0, -1),
    (-1, 0, 1),
    (0, 1, 1),
    (0, -1, -1),
    (0, 1, -1),
    (0, -1, 1),
]
Q = len(velocity_list)
weights = [1.0 / 3.0] + [1.0 / 18.0] * 6 + [1.0 / 36.0] * 12
CX = [v[0] for v in velocity_list]
CY = [v[1] for v in velocity_list]
CZ = [v[2] for v in velocity_list]
opposite = [velocity_list.index((-x, -y, -z)) for x, y, z in velocity_list]
mirror = [velocity_list.index((x, y, -z)) for x, y, z in velocity_list]
rising = [i for i in range(Q) if CY[i] == 1]
falling = [i for i in range(Q) if CY[i] == -1]
eastward = [i for i in range(Q) if CX[i] == 1]
westward = [i for i in range(Q) if CX[i] == -1]
upward = [i for i in range(Q) if CZ[i] == 1]
level = [i for i in range(Q) if CZ[i] == 0]
downward = [mirror[i] for i in upward]
straight = [i for i in range(Q) if CX[i] == 0]
slanted = [i for i in range(Q) if CX[i] != 0]
SPANS = [(i, next(k for k in range(i, Q + 1) if k == Q or CX[k] == 0)) for i in slanted if CX[i - 1] == 0]
NEAR, PART, SUMS = 0, len(upward), 2 * len(upward)
MASK = SUMS + 4
SLOTS = MASK + 1
wall_speed = 0.08
visc_rate = 1.25
fraction_unit = 4096.0
relax_rates = [0.0, 1.19, 1.4, 0.0, 1.2, 0.0, 1.2, 0.0, 1.2, 1.25, 1.4, 1.25, 1.4]
relax_rates += [1.25, 1.25, 1.25, 1.98, 1.98, 1.98]


def row_norms():
    v = np.array(velocity_list, dtype=np.float64)
    x, y, z = v[:, 0], v[:, 1], v[:, 2]
    s = x * x + y * y + z * z
    rows = [
        np.ones(Q),
        19 * s - 30,
        (21 * s * s - 53 * s + 24) / 2,
        x,
        (5 * s - 9) * x,
        y,
        (5 * s - 9) * y,
        z,
        (5 * s - 9) * z,
        3 * x * x - s,
        (3 * s - 5) * (3 * x * x - s),
        y * y - z * z,
        (3 * s - 5) * (y * y - z * z),
        x * y,
        y * z,
        x * z,
        (y * y - z * z) * x,
        (z * z - x * x) * y,
        (x * x - y * y) * z,
    ]
    return [float(np.sum(row * row)) for row in rows]


RATE = [rate / norm for rate, norm in zip(relax_rates, row_norms())]


def plus(a, b):
    return b if a is None else a if b is None else a + b


def minus(a, b):
    return a if b is None else -b if a is None else a - b


def scaled(factor, a):
    return None if a is None else factor * a


def moments(f):
    sums = {i: plus(f[i], f[i + 1]) for i in range(1, Q, 2)}
    difs = {i: minus(f[i], f[i + 1]) for i in range(1, Q, 2)}
    p1, d1 = plus(sums[7], sums[9]), minus(sums[7], sums[9])
    p2, d2 = plus(sums[11], sums[13]), minus(sums[11], sums[13])
    p3, d3 = plus(sums[15], sums[17]), minus(sums[15], sums[17])
    s23 = plus(sums[3], sums[5])
    axis = plus(sums[1], s23)
    p12 = plus(p1, p2)
    diag = plus(p12, p3)
    a, c = plus(difs[7], difs[9]), minus(difs[7], difs[9])
    b, e = plus(difs[11], difs[13]), minus(difs[11], difs[13])
    d, g = plus(difs[15], difs[17]), minus(difs[15], difs[17])
    ab, cd, eg = plus(a, b), plus(c, d), plus(e, g)
    axis_x, diag_x = minus(scaled(2.0, sums[1]), s23), minus(p12, scaled(2.0, p3))
    axis_w, diag_w = minus(sums[3], sums[5]), minus(p1, p2)
    kept = [
        plus(f[0], plus(axis, diag)),
        plus(difs[1], ab),
        plus(difs[3], cd),
        plus(difs[5], eg),
    ]
    others = [
        minus(diag, f[0]),
        minus(plus(f[0], diag), scaled(2.0, axis)),
        minus(ab, scaled(2.0, difs[1])),
        minus(cd, scaled(2.0, difs[3])),
        minus(eg, scaled(2.0, difs[5])),
        plus(axis_x, diag_x),
        minus(diag_x, scaled(2.0, axis_x)),
        plus(axis_w, diag_w),
        minus(diag_w, scaled(2.0, axis_w)),
        d1,
        d3,
        d2,
        minus(a, b),
        minus(d, c),
        minus(e, g),
    ]
    return kept, others


def equilibrium(rho, jx, jy, jz):
    inverse = 1.0 / rho
    ux, uy, uz = jx * inverse, jy * inverse, jz * inverse
    xx, yy, zz = jx * ux, jy * uy, jz * uz
    yz_sum, yz_dif = yy + zz, yy - zz
    square = xx + yz_sum
    eq_x = 2.0 * xx - yz_sum
    eq = [square, None, None, None, None]
    eq += [eq_x, -0.5 * eq_x, yz_dif, -0.5 * yz_dif, jx * uy, jy * uz, jx * uz]
    return eq + [None] * 3


ORDER = [4, 6, 8, 9, 10, 11, 12, 13, 14, 15, 16, 17, 18]
FLOW = 5.0 / 3.0


def relax(moment):
    level_a, level_c = moment[:2]
    factors = [RATE[k] * (FLOW if k in (4, 6, 8) else 1.0) for k in ORDER]
    scaled_by = [scaled(k, m) for k, m in zip(factors, moment[2:])]
    flow_x, flow_y, flow_z, even_x, even_px, even_w, even_pw = scaled_by[:7]
    even_xy, even_yz, even_xz, twist_x, twist_y, twist_z = scaled_by[7:]

    def blend(by_e, by_s):
        rate_e, rate_s = by_e * RATE[1], by_s * RATE[2]
        return plus(scaled(19.0 * rate_e - 5.5 * rate_s, level_a), scaled(3.5 * rate_s, level_c))

    base_axis = blend(-11.0, -4.0)
    base_diag = blend(8.0, 1.0)
    lean = minus(even_x, scaled(2.0, even_px))
    tilt = minus(even_w, scaled(2.0, even_pw))
    side_x, side_w = plus(even_x, even_px), plus(even_w, even_pw)
    flat = plus(base_diag, side_x)
    diag_xy, diag_xz = plus(flat, side_w), minus(flat, side_w)
    diag_yz = minus(base_diag, scaled(2.0, side_x))
    low = minus(base_axis, lean)
    even = {
        1: plus(base_axis, scaled(2.0, lean)),
        3: plus(low, tilt),
        5: minus(low, tilt),
        7: plus(diag_xy, even_xy),
        9: minus(diag_xy, even_xy),
        11: plus(diag_xz, even_xz),
        13: minus(diag_xz, even_xz),
        15: plus(diag_yz, even_yz),
        17: minus(diag_yz, even_yz),
    }
    x_up, x_down = plus(flow_x, twist_x), minus(flow_x, twist_x)
    y_up, y_down = plus(flow_y, twist_y), minus(flow_y, twist_y)
    z_up, z_down = plus(flow_z, twist_z), minus(flow_z, twist_z)
    odd = {
        1: scaled(-4.0, flow_x),
        3: scaled(-4.0, flow_y),
        5: scaled(-4.0, flow_z),
        7: plus(x_up, y_down),
        9: minus(x_up, y_down),
        11: plus(x_down, z_up),
        13: minus(x_down, z_up),
        15: plus(y_up, z_down),
        17: minus(y_up, z_down),
    }
    out = [blend(-30.0, 12.0)]
    for i in range(1, Q, 2):
        out += [plus(even[i], odd[i]), minus(even[i], odd[i])]
    return out


def collide(f, solid):
    kept, others = moments(f)
    rest = [minus(m, e) for m, e in zip(others, equilibrium(*kept))]
    change = relax(rest)
    post = [jnp.where(solid, f[opposite[i]], f[i] - change[i]) for i in range(Q)]
    return post, kept[1], rest[9]


CHUNKS = 4


class Sizes:
    def __init__(self, planes, depth, width, count):
        self.planes, self.depth, self.width, self.count = planes, depth, width, count
        self.deep, self.wide = depth // BLOCK, width // BLOCK
        assert count >= 4 and count & (count - 1) == 0
        assert len(eastward) * planes + 4 <= width and 2 * planes <= width

    def slots(self, delta):
        return (2 if delta == self.count // 2 else 1) * len(rising) + 1

    def tile(self, ref, i, y):
        return ref[i, pl.ds(y * self.depth, self.depth), :]

    def lanes(self):
        return lax.broadcasted_iota(jnp.int32, (self.depth, self.width), 1)

    def rows(self):
        return lax.broadcasted_iota(jnp.int32, (self.depth, self.width), 0)

    def spread(self, row):
        return jnp.broadcast_to(row, (self.depth, self.width))

    def solid_tile(self, mask_ref, y):
        base = y // BLOCK * self.deep
        out = self.spread(mask_ref[base : base + 1, :])
        rows = self.rows()
        for step in range(1, self.deep):
            line = self.spread(mask_ref[base + step : base + step + 1, :])
            out = jnp.where(rows >= step * BLOCK, line, out)
        return out


def roll(value, shift, axis=1):
    shift = shift % value.shape[axis]
    return pltpu.roll(value, shift, axis) if shift else value


def edge_columns(z):
    return [
        (7, z.planes - 1, True),
        (10, z.planes - 1, False),
        (9, 0, True),
        (8, 0, False),
    ]


def wall_columns(z, ref, lanes):
    out = jnp.zeros((z.depth, z.width), jnp.float32)
    start = len(eastward) * z.planes
    for k, (i, y, right) in enumerate(edge_columns(z)):
        at = start + k
        moved = roll(z.tile(ref, i, y), at - (z.width - 1 if right else 0))
        out = jnp.where(lanes == at, moved, out)
    return out


def pack_x(z, whole, ref, sends, extra=None):
    me = lax.axis_index("gx")
    lanes = z.lanes()
    right_edge = wall_columns(z, ref, lanes)
    left_edge = right_edge
    for j in range(len(eastward)):
        for y in range(z.planes):
            at = j * z.planes + y
            hit = lanes == at
            moved = roll(z.tile(ref, eastward[j], y), at - (z.width - 1))
            right_edge = jnp.where(hit, moved, right_edge)
            moved = roll(z.tile(ref, westward[j], y), at)
            left_edge = jnp.where(hit, moved, left_edge)
    far = lax.div(whole, z.width)
    for delta in range(1, z.count):
        send = sends[delta - 1]
        partner = jnp.bitwise_xor(me, delta)
        ahead = lax.rem(me - partner + z.count, z.count)
        at_top = (ahead == far) | (ahead == lax.rem(far + 1, z.count))
        for s in range(len(rising)):
            top = z.tile(ref, rising[s], z.planes - 1)
            bottom = z.tile(ref, falling[s], 0)
            if delta == z.count // 2:
                send[s] = top
                send[len(rising) + s] = bottom
            else:
                send[s] = jnp.where(at_top, top, bottom)
        to_right = partner == lax.rem(me + 1, z.count)
        slots = z.slots(delta)
        send[slots - 1] = jnp.where(to_right, right_edge, left_edge)
        if extra is not None:
            send[slots] = extra


def fill_tables(z, ref, gets, tops, bottoms, edges):
    me = lax.axis_index("gx")
    for s in range(len(rising)):
        tops[me, s] = z.tile(ref, rising[s], z.planes - 1)
        bottoms[me, s] = z.tile(ref, falling[s], 0)
    edges[me] = wall_columns(z, ref, z.lanes())
    for delta in range(1, z.count):
        get = gets[delta - 1]
        partner = jnp.bitwise_xor(me, delta)
        for s in range(len(rising)):
            tops[partner, s] = get[s]
            second = len(rising) + s if delta == z.count // 2 else s
            bottoms[partner, s] = get[second]
        edges[partner] = get[z.slots(delta) - 1]
    left = edges[lax.rem(me + z.count - 1, z.count)]
    right = edges[lax.rem(me + 1, z.count)]
    return left, right


def mended(z, value, i, y, left, right):
    lanes, last = z.lanes(), z.width - 1
    if CX[i] == 1:
        at = eastward.index(i) * z.planes + y
        return jnp.where(lanes == 0, roll(left, -at), value)
    if CX[i] == -1:
        at = westward.index(i) * z.planes + y
        return jnp.where(lanes == last, roll(right, last - at), value)
    return value


def moved_x(z, ref, i, y, left, right):
    return mended(z, roll(z.tile(ref, i, y), CX[i]), i, y, left, right)


def sliding(z, whole, part, tops, bottoms, edges, put):
    me = lax.axis_index("gx")
    lanes, last = z.lanes(), z.width - 1
    weight = part.astype(jnp.float32) / fraction_unit
    far = lax.div(whole, z.width)
    rest = lax.rem(whole, z.width)
    start = len(eastward) * z.planes
    columns = {i: start + k for k, (i, _, _) in enumerate(edge_columns(z))}

    def window(i, planes, s, block, offset):
        pair = []
        for step in range(2):
            here = lax.rem(block + step, z.count)
            value = planes[here, s]
            if CX[i] == 1:
                side = edges[lax.rem(here + z.count - 1, z.count)]
                value = jnp.where(lanes == 0, roll(side, -columns[i]), roll(value, 1))
            elif CX[i] == -1:
                side = edges[lax.rem(here + 1, z.count)]
                value = jnp.where(lanes == last, roll(side, last - columns[i]), roll(value, -1))
            pair.append(value)
        first = jnp.where(lanes >= offset, pair[0], pair[1])
        second = jnp.where(lanes > offset, pair[0], pair[1])
        first = pltpu.roll(first, lax.rem(z.width - offset, z.width), 1)
        second = pltpu.roll(second, last - offset, 1)
        return first, second

    for s, i in enumerate(rising):
        near, next_one = window(i, tops, s, lax.rem(me + far, z.count), rest)
        fix = 6.0 * weights[i] * CX[i] * wall_speed
        value = (1.0 - weight) * near + weight * next_one
        put(i, value - fix if CX[i] else value)
    for s, i in enumerate(falling):
        block = lax.rem(me + 2 * z.count - far - 1, z.count)
        next_one, near = window(i, bottoms, s, block, last - rest)
        fix = 6.0 * weights[i] * CX[i] * wall_speed
        value = (1.0 - weight) * near + weight * next_one
        put(i, value + fix if CX[i] else value)


def wall_slot(i):
    return rising.index(i) if CY[i] == 1 else len(rising) + falling.index(i)


def first_kernel(z, whole_hbm, part_hbm, pop_hbm, solid_hbm, post_ref, acc_ref, mask_ref, info_ref, *refs):
    sends, (whole_ref, part_ref, pop_ref, solid_ref, sems) = refs[: z.count - 1], refs[z.count - 1 :]
    group = z.planes // CHUNKS * z.depth
    copies = [pltpu.make_async_copy(solid_hbm, solid_ref, sems.at[CHUNKS])]
    for k in range(CHUNKS):
        part = (slice(None), pl.ds(k * group, group), slice(None))
        copies.append(pltpu.make_async_copy(pop_hbm.at[part], pop_ref.at[part], sems.at[k]))
    copies.append(pltpu.make_async_copy(whole_hbm, whole_ref, sems.at[CHUNKS + 1]))
    copies.append(pltpu.make_async_copy(part_hbm, part_ref, sems.at[CHUNKS + 2]))
    for copy in copies:
        copy.start()
    copies[0].wait()
    grow = lax.broadcasted_iota(jnp.int32, (z.wide, z.width), 1) // BLOCK
    grow = grow == lax.broadcasted_iota(jnp.int32, (z.wide, z.width), 0)
    grow = grow.astype(jnp.float32)
    for k in range(solid_ref.shape[0]):
        flags = jnp.where(solid_ref[k] > 0, 1.0, 0.0)
        line = jnp.dot(flags, grow, preferred_element_type=jnp.float32)
        mask_ref[pl.ds(k * z.deep, z.deep), :] = line
    for y in range(z.planes):
        if y % (z.planes // CHUNKS) == 0:
            copies[1 + y // (z.planes // CHUNKS)].wait()
        solid = z.solid_tile(mask_ref, y) > 0.5
        f = [z.tile(pop_ref, i, y) * np.float32(weights[i]) for i in range(Q)]
        post, jx, moment_xy = collide(f, solid)
        here = pl.ds(y * z.depth, z.depth)
        for i in range(Q):
            post_ref[i, here, :] = post[i]
        acc_ref[0, here, :] = jnp.where(solid, 0.0, jx)
        acc_ref[1, here, :] = jnp.where(solid, 0.0, -(1.0 - 0.5 * visc_rate) * moment_xy)
    copies[-2].wait()
    copies[-1].wait()
    for step in range(whole_ref.shape[0]):
        for k, ref in enumerate((whole_ref, part_ref)):
            value = ref[step].astype(jnp.float32)
            info_ref[pl.ds(2 * step + k, 1), :] = jnp.full((1, z.width), value, jnp.float32)
    pack_x(z, whole_ref[0], post_ref, sends)


def shift_of(info_ref, step):
    values = [jnp.max(info_ref[2 * step + k : 2 * step + k + 1, :]) for k in range(2)]
    return [value.astype(jnp.int32) for value in values]


def second_kernel(z, info_ref, post_ref, mask_ref, *refs):
    gets, outs = refs[: z.count - 1], refs[z.count - 1 : z.count + 3]
    inner_ref, outer_ref, wall_ref, side_ref = outs
    tops, bottoms, edges, rows_ref = refs[z.count + 3 :]
    whole, part = shift_of(info_ref, 0)
    left, right = fill_tables(z, post_ref, gets, tops, bottoms, edges)
    side_ref[0], side_ref[1] = left, right
    columns = {1: left.T, -1: right.T}
    shape = (z.planes, z.width)
    lanes = lax.broadcasted_iota(jnp.int32, shape, 1)
    heights = lax.broadcasted_iota(jnp.int32, shape, 0)
    even = lax.rem(lax.axis_index("gz"), 2) == 0

    def line(i, row):
        value = post_ref[i, pl.ds(row, z.planes, stride=z.depth), :]
        if CX[i]:
            j = (eastward if CX[i] == 1 else westward).index(i)
            column = columns[CX[i]][j * z.planes : (j + 1) * z.planes, row : row + 1]
            edge = 0 if CX[i] == 1 else z.width - 1
            value = jnp.where(lanes == edge, jnp.broadcast_to(column, shape), roll(value, CX[i]))
        if CY[i]:
            enter = 0 if CY[i] == 1 else z.planes - 1
            wall = jnp.broadcast_to(wall_ref[wall_slot(i), row : row + 1, :], shape)
            value = jnp.where(heights == enter, wall, roll(value, CY[i], 0))
        return value

    jobs = []
    for side in range(2):
        near, far = (z.depth - 1, z.depth - 2) if side == 0 else (0, 1)
        for k in range(Q):
            row = near if CZ[k] >= 0 else far
            i = k if CZ[k] >= 0 else mirror[k]
            jobs.append((side, k, i if side == 0 else mirror[i], row))
    for still in (True, False):
        for side, k, i, row in jobs:
            if (CY[i] == 0) == still:
                rows_ref[side, k] = line(i, row)
        if still:

            def put(i, value):
                wall_ref[wall_slot(i)] = value

            sliding(z, whole, part, tops, bottoms, edges, put)

    chunk = min(8, z.planes)
    for start in range(0, z.planes, chunk):
        here = pl.ds(start, chunk)
        found = []
        for side in range(2):
            f = [None] * Q
            for i in level:
                f[i] = rows_ref[side, i, here, :]
            for i in upward:
                f[i] = rows_ref[side, mirror[i], here, :]
            kept, others = moments(f)
            change = relax(others)
            values = [rows_ref[side, i, here, :] for i in upward]
            values += [f[i] - change[i] for i in upward]
            found.append(values + kept)
        for slot in range(MASK):
            up, down = found[0][slot], found[1][slot]
            inner_ref[slot, here, :] = jnp.where(even, up, down)
            outer_ref[slot, here, :] = jnp.where(even, down, up)
    for k in range(z.planes // BLOCK):
        up = mask_ref[(k + 1) * z.deep - 1 : (k + 1) * z.deep, :]
        down = mask_ref[k * z.deep : k * z.deep + 1, :]
        here = pl.ds(k * BLOCK, BLOCK)
        block = (BLOCK, z.width)
        inner_ref[MASK, here, :] = jnp.broadcast_to(jnp.where(even, up, down), block)
        outer_ref[MASK, here, :] = jnp.broadcast_to(jnp.where(even, down, up), block)


def bulk_kernel(z, post_ref, wall_ref, side_ref, h_ref):
    left, right = side_ref[0], side_ref[1]
    for i in range(Q):
        for y in range(z.planes):
            here = pl.ds(y * z.depth, z.depth)
            if 0 <= y - CY[i] < z.planes:
                h_ref[i, here, :] = moved_x(z, post_ref, i, y - CY[i], left, right)
            else:
                h_ref[i, here, :] = wall_ref[wall_slot(i)]


def middle_kernel(z, h_ref, mask_ref, old_ref, g_ref, acc_ref):
    for y in range(z.planes):
        solid = z.solid_tile(mask_ref, y) > 0.5
        f = [roll(z.tile(h_ref, i, y), CZ[i], 0) for i in range(Q)]
        post, jx, moment_xy = collide(f, solid)
        here = pl.ds(y * z.depth, z.depth)
        for i in range(Q):
            g_ref[i, here, :] = roll(post[i], CZ[i], 0)
        fields = [jx, -(1.0 - 0.5 * visc_rate) * moment_xy]
        for k in range(2):
            acc_ref[k, here, :] = old_ref[k, here, :] + jnp.where(solid, 0.0, fields[k])


def third_kernel(z, info_ref, h_ref, inner_ref, outer_ref, mask_ref, old_ref, *refs):
    (g_ref, acc_ref, part_ref), sends = refs[2:5], refs[5 : 4 + z.count]
    (sides,) = refs[4 + z.count :]
    whole, _ = shift_of(info_ref, 1)
    even = lax.rem(lax.axis_index("gz"), 2) == 0
    sides[jnp.where(even, 1, 0)] = inner_ref[...]
    sides[jnp.where(even, 0, 1)] = outer_ref[...]
    chunk = min(2 * BLOCK, z.planes)
    shape = (chunk, z.width)
    heights = lax.broadcasted_iota(jnp.int32, shape, 0)
    for side in range(2):
        edge, next_row = (0, 1) if side == 0 else (z.depth - 1, z.depth - 2)
        actual = list(range(Q)) if side == 0 else mirror
        for start in range(0, z.planes, chunk):
            here = pl.ds(start, chunk)

            def rows(row):
                return pl.ds(start * z.depth + row, chunk, stride=z.depth)

            own = {i: h_ref[actual[i], rows(edge), :] for i in level + downward}
            f = [None] * Q
            for i in downward:
                f[i] = own[i]
            kept, others = moments(f)
            kept = [plus(kept[k], sides[side, SUMS + k, here, :]) for k in range(4)]
            change = relax([minus(m, e) for m, e in zip(others, equilibrium(*kept))])
            solid = sides[side, MASK, here, :] > 0.5
            for s, i in enumerate(upward):
                value = sides[side, PART + s, here, :] - change[i]
                g_ref[actual[i], rows(edge), :] = jnp.where(solid, f[opposite[i]], value)

            for i in level:
                f[i] = own[i]
            for s, i in enumerate(upward):
                f[i] = sides[side, NEAR + s, here, :]
            for i in downward:
                f[i] = h_ref[actual[i], rows(next_row), :]
            solid = jnp.zeros(shape, jnp.float32)
            for k in range(chunk // BLOCK):
                at = (start // BLOCK + k) * z.deep + (0 if side == 0 else z.deep - 1)
                line = jnp.broadcast_to(mask_ref[at : at + 1, :], shape)
                solid = jnp.where(heights >= k * BLOCK, line, solid)
            solid = solid > 0.5
            post, jx, moment_xy = collide(f, solid)
            for i in level:
                g_ref[actual[i], rows(edge), :] = post[i]
            for i in upward:
                g_ref[actual[i], rows(next_row), :] = post[i]
            fields = [jx, -(1.0 - 0.5 * visc_rate) * moment_xy]
            for k in range(2):
                value = old_ref[k, rows(edge), :] + jnp.where(solid, 0.0, fields[k])
                acc_ref[k, rows(edge), :] = value
    lanes = z.lanes()
    sums = jnp.zeros((z.depth, z.width), jnp.float32)
    for y in range(z.planes):
        for k in range(2):
            total = z.spread(jnp.sum(z.tile(acc_ref, k, y), axis=1, keepdims=True))
            sums = jnp.where(lanes == k * z.planes + y, total, sums)
    part_ref[...] = sums
    pack_x(z, whole, g_ref, sends, sums)


def direct_kernel(z, g_ref, acc_ref, out_hbm, acc_hbm, turned_ref, sems):
    inner = (z.planes - 1) * z.depth
    copies = [pltpu.make_async_copy(acc_ref, acc_hbm, sems.at[len(straight)])]
    copies[0].start()
    for k, i in enumerate(straight):
        source, target = g_ref.at[i], out_hbm.at[i]
        if CY[i] == 1:
            source, target = source.at[pl.ds(0, inner), :], target.at[pl.ds(z.depth, inner), :]
        elif CY[i] == -1:
            source, target = source.at[pl.ds(z.depth, inner), :], target.at[pl.ds(0, inner), :]
        copies.append(pltpu.make_async_copy(source, target, sems.at[k]))
        copies[-1].start()
    for k, i in enumerate(slanted):
        for y in range(z.planes):
            if 0 <= y - CY[i] < z.planes:
                here = pl.ds(y * z.depth, z.depth)
                turned_ref[k, here, :] = roll(z.tile(g_ref, i, y - CY[i]), CX[i])
    for copy in copies:
        copy.wait()


def fourth_kernel(z, info_ref, g_ref, turned_ref, own_ref, *refs):
    gets, (_, out_hbm, profile_hbm) = refs[: z.count - 1], refs[z.count - 1 : z.count + 2]
    tops, bottoms, edges, out_ref, profile_ref, sems = refs[z.count + 2 :]
    whole, part = shift_of(info_ref, 1)
    terms = [own_ref[...]] + [gets[d - 1][z.slots(d)] for d in range(1, z.count)]
    while len(terms) > 1:
        terms = [terms[k] + terms[k + 1] for k in range(0, len(terms), 2)]
    for k in range(2):
        profile_ref[k] = terms[0][:, k * z.planes : (k + 1) * z.planes]
    copies = []

    def send(source, target):
        copies.append(pltpu.make_async_copy(source, target, sems.at[len(copies)]))
        copies[-1].start()

    send(profile_ref, profile_hbm)
    left, right = fill_tables(z, g_ref, gets, tops, bottoms, edges)
    group = z.planes // CHUNKS

    def interior(k):
        for i in slanted:
            for y in range(k * group, (k + 1) * group):
                if 0 <= y - CY[i] < z.planes:
                    here = pl.ds(y * z.depth, z.depth)
                    value = turned_ref[slanted.index(i), here, :]
                    out_ref[i, here, :] = mended(z, value, i, y - CY[i], left, right)

    def finish(k):
        here = pl.ds(k * group * z.depth, group * z.depth)
        for first, last in SPANS:
            part = (pl.ds(first, last - first), here, slice(None))
            send(out_ref.at[part], out_hbm.at[part])

    def put(i, value):
        here = pl.ds(0 if CY[i] == 1 else (z.planes - 1) * z.depth, z.depth)
        out_ref[i, here, :] = value
        if CX[i] == 0:
            send(out_ref.at[i, here, :], out_hbm.at[i, here, :])

    sliding(z, whole, part, tops, bottoms, edges, put)
    for k in range(CHUNKS):
        interior(k)
        finish(k)
    for copy in copies:
        copy.wait()


def local(count, ranks, pop_ratio, solid_blocks, shift_whole, shift_frac):
    _, planes, depth, width = pop_ratio.shape
    z = Sizes(planes, depth, width, count)
    assert ranks % 2 == 0
    f32 = lambda *shape: pltpu.VMEM(shape, jnp.float32)
    hbm = lambda ref: jax.ShapeDtypeStruct(ref.shape, ref.dtype)
    keep = lambda *values: [pltpu.with_memory_space_constraint(v, pltpu.VMEM) for v in values]
    vmem = pl.BlockSpec(memory_space=pltpu.VMEM)
    outside = pl.BlockSpec(memory_space=pl.ANY)
    cells = f32(Q, planes * depth, width)
    fields = f32(2, planes * depth, width)
    halo = f32(SLOTS, planes, width)
    shifts = [pltpu.VMEM((count, len(rising), depth, width), jnp.float32)] * 2
    shifts.append(pltpu.VMEM((count, depth, width), jnp.float32))
    pair = pltpu.SMEM(shift_whole.shape, jnp.int32)
    sems = lambda number: pltpu.SemaphoreType.DMA((number,))
    outer_keep = lambda *values: [pltpu.with_memory_space_constraint(v, pltpu.HBM) for v in values]
    shift_whole, shift_frac, solid_blocks = outer_keep(shift_whole, shift_frac, solid_blocks)

    def buffers(more):
        return [f32(z.slots(d) + more, depth, width) for d in range(1, count)]

    def call(body, ins, outs, scratch=(), direct=(), alias=None):
        specs = [outside if k in direct else vmem for k in range(len(outs))]
        return pl.pallas_call(
            functools.partial(body, z),
            out_shape=outs,
            in_specs=ins,
            out_specs=specs,
            scratch_shapes=list(scratch),
            input_output_aliases=alias or {},
            compiler_params=pltpu.CompilerParams(vmem_limit_bytes=8 << 20),
        )

    def swap_x(values):
        return [
            lax.ppermute(values[d - 1], "gx", [(i, i ^ d) for i in range(count)])
            for d in range(1, count)
        ]

    pairs = [(i, i ^ 1) for i in range(ranks)]
    across = [(i, (i - 1 if i % 2 == 0 else i + 1) % ranks) for i in range(ranks)]

    (pop,) = outer_keep(pop_ratio.reshape(cells.shape))
    post, old, mask, info, *sends = call(
        first_kernel,
        [outside] * 4,
        [cells, fields, f32(planes // BLOCK * z.deep, width), f32(2 * shift_whole.shape[0], width)] + buffers(0),
        [pair, pair, cells, pltpu.VMEM(solid_blocks.shape, jnp.int32), sems(CHUNKS + 3)],
    )(shift_whole, shift_frac, pop, solid_blocks)
    gets = swap_x(sends)
    walls, both = f32(2 * len(rising), depth, width), f32(2, depth, width)
    inner, outer, wall, side = call(
        second_kernel,
        [vmem] * (2 + count),
        [halo, halo, walls, both],
        shifts + [f32(2, Q, planes, width)],
    )(*keep(info, post, mask, *gets))
    outer = lax.ppermute(outer, "gz", across)
    inner = lax.ppermute(inner, "gz", pairs)
    (h,) = call(bulk_kernel, [vmem] * 3, [cells])(*keep(post, wall, side))
    g, acc = call(middle_kernel, [vmem] * 3, [cells, fields])(*keep(h, mask, old))
    g, acc, own, *sends = call(
        third_kernel,
        [vmem] * 8,
        [cells, fields, f32(depth, width)] + buffers(1),
        [pltpu.VMEM((2, SLOTS, planes, width), jnp.float32)],
        alias={6: 0, 7: 1},
    )(*keep(info, h, inner, outer, mask, old, g, acc))
    gets = swap_x(sends)
    turned = f32(len(slanted), planes * depth, width)
    out, acc, turned = call(
        direct_kernel,
        [vmem] * 2,
        [hbm(cells), hbm(fields), turned],
        [sems(len(straight) + 1)],
        [0, 1],
    )(*keep(g, acc))
    moves = 1 + len(SPANS) * CHUNKS + sum(CX[i] == 0 for i in rising + falling)
    out, profile = call(
        fourth_kernel,
        [vmem] * (3 + count) + [outside],
        [hbm(cells), hbm(f32(2, depth, planes))],
        shifts + [cells, f32(2, depth, planes), sems(moves)],
        [0, 1],
        {3 + count: 0},
    )(*keep(info, g, turned, own, *gets), out)
    return (
        out.reshape(pop_ratio.shape),
        acc.reshape(2, planes, depth, width),
        jnp.swapaxes(profile, 1, 2),
    )


def solution(mesh):
    return jax.shard_map(
        functools.partial(local, mesh.shape["gx"], mesh.shape["gz"]),
        mesh=mesh,
        in_specs=(P(None, None, "gz", "gx"), P(None, "gz", "gx"), P(), P()),
        out_specs=(P(None, None, "gz", "gx"), P(None, None, "gz", "gx"), P(None, None, "gz")),
        check_vma=False,
    )
```

```python
import functools

import jax
import jax.numpy as jnp
import numpy as np
from jax import lax
from jax.experimental import pallas as pl
from jax.experimental.pallas import tpu as pltpu
from jax.sharding import PartitionSpec as P


BLOCK = 4
velocity_list = [
    (0, 0, 0),
    (1, 0, 0),
    (-1, 0, 0),
    (0, 1, 0),
    (0, -1, 0),
    (0, 0, 1),
    (0, 0, -1),
    (1, 1, 0),
    (-1, -1, 0),
    (1, -1, 0),
    (-1, 1, 0),
    (1, 0, 1),
    (-1, 0, -1),
    (1, 0, -1),
    (-1, 0, 1),
    (0, 1, 1),
    (0, -1, -1),
    (0, 1, -1),
    (0, -1, 1),
]
Q = len(velocity_list)
weights = [1.0 / 3.0] + [1.0 / 18.0] * 6 + [1.0 / 36.0] * 12
CX = [v[0] for v in velocity_list]
CY = [v[1] for v in velocity_list]
CZ = [v[2] for v in velocity_list]
opposite = [velocity_list.index((-x, -y, -z)) for x, y, z in velocity_list]
mirror = [velocity_list.index((x, y, -z)) for x, y, z in velocity_list]
rising = [i for i in range(Q) if CY[i] == 1]
falling = [i for i in range(Q) if CY[i] == -1]
eastward = [i for i in range(Q) if CX[i] == 1]
westward = [i for i in range(Q) if CX[i] == -1]
upward = [i for i in range(Q) if CZ[i] == 1]
level = [i for i in range(Q) if CZ[i] == 0]
downward = [mirror[i] for i in upward]
straight = [i for i in range(Q) if CX[i] == 0]
slanted = [i for i in range(Q) if CX[i] != 0]
SPANS = [(i, next(k for k in range(i, Q + 1) if k == Q or CX[k] == 0)) for i in slanted if CX[i - 1] == 0]
NEAR, PART, SUMS = 0, len(upward), 2 * len(upward)
MASK = SUMS + 4
SLOTS = MASK + 1
wall_speed = 0.08
visc_rate = 1.25
fraction_unit = 4096.0
relax_rates = [0.0, 1.19, 1.4, 0.0, 1.2, 0.0, 1.2, 0.0, 1.2, 1.25, 1.4, 1.25, 1.4]
relax_rates += [1.25, 1.25, 1.25, 1.98, 1.98, 1.98]


def row_norms():
    v = np.array(velocity_list, dtype=np.float64)
    x, y, z = v[:, 0], v[:, 1], v[:, 2]
    s = x * x + y * y + z * z
    rows = [
        np.ones(Q),
        19 * s - 30,
        (21 * s * s - 53 * s + 24) / 2,
        x,
        (5 * s - 9) * x,
        y,
        (5 * s - 9) * y,
        z,
        (5 * s - 9) * z,
        3 * x * x - s,
        (3 * s - 5) * (3 * x * x - s),
        y * y - z * z,
        (3 * s - 5) * (y * y - z * z),
        x * y,
        y * z,
        x * z,
        (y * y - z * z) * x,
        (z * z - x * x) * y,
        (x * x - y * y) * z,
    ]
    return [float(np.sum(row * row)) for row in rows]


RATE = [rate / norm for rate, norm in zip(relax_rates, row_norms())]


def plus(a, b):
    return b if a is None else a if b is None else a + b


def minus(a, b):
    return a if b is None else -b if a is None else a - b


def scaled(factor, a):
    return None if a is None else factor * a


def moments(f):
    sums = {i: plus(f[i], f[i + 1]) for i in range(1, Q, 2)}
    difs = {i: minus(f[i], f[i + 1]) for i in range(1, Q, 2)}
    p1, d1 = plus(sums[7], sums[9]), minus(sums[7], sums[9])
    p2, d2 = plus(sums[11], sums[13]), minus(sums[11], sums[13])
    p3, d3 = plus(sums[15], sums[17]), minus(sums[15], sums[17])
    s23 = plus(sums[3], sums[5])
    axis = plus(sums[1], s23)
    p12 = plus(p1, p2)
    diag = plus(p12, p3)
    a, c = plus(difs[7], difs[9]), minus(difs[7], difs[9])
    b, e = plus(difs[11], difs[13]), minus(difs[11], difs[13])
    d, g = plus(difs[15], difs[17]), minus(difs[15], difs[17])
    ab, cd, eg = plus(a, b), plus(c, d), plus(e, g)
    axis_x, diag_x = minus(scaled(2.0, sums[1]), s23), minus(p12, scaled(2.0, p3))
    axis_w, diag_w = minus(sums[3], sums[5]), minus(p1, p2)
    kept = [
        plus(f[0], plus(axis, diag)),
        plus(difs[1], ab),
        plus(difs[3], cd),
        plus(difs[5], eg),
    ]
    others = [
        minus(diag, f[0]),
        minus(plus(f[0], diag), scaled(2.0, axis)),
        minus(ab, scaled(2.0, difs[1])),
        minus(cd, scaled(2.0, difs[3])),
        minus(eg, scaled(2.0, difs[5])),
        plus(axis_x, diag_x),
        minus(diag_x, scaled(2.0, axis_x)),
        plus(axis_w, diag_w),
        minus(diag_w, scaled(2.0, axis_w)),
        d1,
        d3,
        d2,
        minus(a, b),
        minus(d, c),
        minus(e, g),
    ]
    return kept, others


def equilibrium(rho, jx, jy, jz):
    inverse = 1.0 / rho
    ux, uy, uz = jx * inverse, jy * inverse, jz * inverse
    xx, yy, zz = jx * ux, jy * uy, jz * uz
    yz_sum, yz_dif = yy + zz, yy - zz
    square = xx + yz_sum
    eq_x = 2.0 * xx - yz_sum
    eq = [square, None, None, None, None]
    eq += [eq_x, -0.5 * eq_x, yz_dif, -0.5 * yz_dif, jx * uy, jy * uz, jx * uz]
    return eq + [None] * 3


ORDER = [4, 6, 8, 9, 10, 11, 12, 13, 14, 15, 16, 17, 18]
FLOW = 5.0 / 3.0


def relax(moment):
    level_a, level_c = moment[:2]
    factors = [RATE[k] * (FLOW if k in (4, 6, 8) else 1.0) for k in ORDER]
    scaled_by = [scaled(k, m) for k, m in zip(factors, moment[2:])]
    flow_x, flow_y, flow_z, even_x, even_px, even_w, even_pw = scaled_by[:7]
    even_xy, even_yz, even_xz, twist_x, twist_y, twist_z = scaled_by[7:]

    def blend(by_e, by_s):
        rate_e, rate_s = by_e * RATE[1], by_s * RATE[2]
        return plus(scaled(19.0 * rate_e - 5.5 * rate_s, level_a), scaled(3.5 * rate_s, level_c))

    base_axis = blend(-11.0, -4.0)
    base_diag = blend(8.0, 1.0)
    lean = minus(even_x, scaled(2.0, even_px))
    tilt = minus(even_w, scaled(2.0, even_pw))
    side_x, side_w = plus(even_x, even_px), plus(even_w, even_pw)
    flat = plus(base_diag, side_x)
    diag_xy, diag_xz = plus(flat, side_w), minus(flat, side_w)
    diag_yz = minus(base_diag, scaled(2.0, side_x))
    low = minus(base_axis, lean)
    even = {
        1: plus(base_axis, scaled(2.0, lean)),
        3: plus(low, tilt),
        5: minus(low, tilt),
        7: plus(diag_xy, even_xy),
        9: minus(diag_xy, even_xy),
        11: plus(diag_xz, even_xz),
        13: minus(diag_xz, even_xz),
        15: plus(diag_yz, even_yz),
        17: minus(diag_yz, even_yz),
    }
    x_up, x_down = plus(flow_x, twist_x), minus(flow_x, twist_x)
    y_up, y_down = plus(flow_y, twist_y), minus(flow_y, twist_y)
    z_up, z_down = plus(flow_z, twist_z), minus(flow_z, twist_z)
    odd = {
        1: scaled(-4.0, flow_x),
        3: scaled(-4.0, flow_y),
        5: scaled(-4.0, flow_z),
        7: plus(x_up, y_down),
        9: minus(x_up, y_down),
        11: plus(x_down, z_up),
        13: minus(x_down, z_up),
        15: plus(y_up, z_down),
        17: minus(y_up, z_down),
    }
    out = [blend(-30.0, 12.0)]
    for i in range(1, Q, 2):
        out += [plus(even[i], odd[i]), minus(even[i], odd[i])]
    return out


def collide(f, solid):
    kept, others = moments(f)
    rest = [minus(m, e) for m, e in zip(others, equilibrium(*kept))]
    change = relax(rest)
    post = [jnp.where(solid, f[opposite[i]], f[i] - change[i]) for i in range(Q)]
    return post, kept[1], rest[9]


CHUNKS = 4


class Sizes:
    def __init__(self, planes, depth, width, count):
        self.planes, self.depth, self.width, self.count = planes, depth, width, count
        self.deep, self.wide = depth // BLOCK, width // BLOCK
        assert count >= 4 and count & (count - 1) == 0
        self.walls = 2 * planes * (len(eastward) + 1) // 2
        assert len(eastward) % 2 == 1 and self.walls + 4 <= width

    def slots(self, delta):
        return (2 if delta == self.count // 2 else 1) * len(rising) + 1

    def at(self, j, y):
        return 2 * self.planes * (j // 2) + 2 * y + j % 2

    def tile(self, ref, i, y):
        return ref[i, pl.ds(y * self.depth, self.depth), :]

    def lanes(self):
        return lax.broadcasted_iota(jnp.int32, (self.depth, self.width), 1)

    def rows(self):
        return lax.broadcasted_iota(jnp.int32, (self.depth, self.width), 0)

    def spread(self, row):
        return jnp.broadcast_to(row, (self.depth, self.width))

    def solid_tile(self, mask_ref, y):
        base = y // BLOCK * self.deep
        out = self.spread(mask_ref[base : base + 1, :])
        rows = self.rows()
        for step in range(1, self.deep):
            line = self.spread(mask_ref[base + step : base + step + 1, :])
            out = jnp.where(rows >= step * BLOCK, line, out)
        return out


def roll(value, shift, axis=1):
    shift = shift % value.shape[axis]
    return pltpu.roll(value, shift, axis) if shift else value


def edge_columns(z):
    return [
        (7, z.planes - 1, True),
        (10, z.planes - 1, False),
        (9, 0, True),
        (8, 0, False),
    ]


def wall_columns(z, get, lanes):
    out = jnp.zeros((z.depth, z.width), jnp.float32)
    for k, (i, y, right) in enumerate(edge_columns(z)):
        at = z.walls + k
        moved = roll(get(i, y), at - (z.width - 1 if right else 0))
        out = jnp.where(lanes == at, moved, out)
    return out


def edge_tiles(z, ref):
    lanes = z.lanes()
    right_edge = wall_columns(z, functools.partial(z.tile, ref), lanes)
    left_edge = right_edge
    for j in range(len(eastward)):
        for y in range(z.planes):
            at = z.at(j, y)
            hit = lanes == at
            moved = roll(z.tile(ref, eastward[j], y), at - (z.width - 1))
            right_edge = jnp.where(hit, moved, right_edge)
            moved = roll(z.tile(ref, westward[j], y), at)
            left_edge = jnp.where(hit, moved, left_edge)
    return right_edge, left_edge


def pack_x(z, whole, get, right_edge, left_edge, sends, extra=None):
    me = lax.axis_index("gx")
    far = lax.div(whole, z.width)
    for delta in range(1, z.count):
        send = sends[delta - 1]
        partner = jnp.bitwise_xor(me, delta)
        ahead = lax.rem(me - partner + z.count, z.count)
        at_top = (ahead == far) | (ahead == lax.rem(far + 1, z.count))
        for s in range(len(rising)):
            top = get(rising[s], z.planes - 1)
            bottom = get(falling[s], 0)
            if delta == z.count // 2:
                send[s] = top
                send[len(rising) + s] = bottom
            else:
                send[s] = jnp.where(at_top, top, bottom)
        to_right = partner == lax.rem(me + 1, z.count)
        slots = z.slots(delta)
        send[slots - 1] = jnp.where(to_right, right_edge, left_edge)
        if extra is not None:
            send[slots] = extra


def fill_tables(z, ref, gets, tops, bottoms, edges):
    me = lax.axis_index("gx")
    for s in range(len(rising)):
        tops[me, s] = z.tile(ref, rising[s], z.planes - 1)
        bottoms[me, s] = z.tile(ref, falling[s], 0)
    edges[me] = wall_columns(z, functools.partial(z.tile, ref), z.lanes())
    for delta in range(1, z.count):
        get = gets[delta - 1]
        partner = jnp.bitwise_xor(me, delta)
        for s in range(len(rising)):
            tops[partner, s] = get[s]
            second = len(rising) + s if delta == z.count // 2 else s
            bottoms[partner, s] = get[second]
        edges[partner] = get[z.slots(delta) - 1]
    left = edges[lax.rem(me + z.count - 1, z.count)]
    right = edges[lax.rem(me + 1, z.count)]
    return left, right


def mended(z, value, i, y, left, right):
    lanes, last = z.lanes(), z.width - 1
    if CX[i] == 1:
        at = z.at(eastward.index(i), y)
        return jnp.where(lanes == 0, roll(left, -at), value)
    if CX[i] == -1:
        at = z.at(westward.index(i), y)
        return jnp.where(lanes == last, roll(right, last - at), value)
    return value


def moved_x(z, ref, i, y, left, right):
    return mended(z, roll(z.tile(ref, i, y), CX[i]), i, y, left, right)


def sliding(z, whole, part, tops, bottoms, edges, put):
    me = lax.axis_index("gx")
    lanes, last = z.lanes(), z.width - 1
    weight = part.astype(jnp.float32) / fraction_unit
    far = lax.div(whole, z.width)
    rest = lax.rem(whole, z.width)
    columns = {i: z.walls + k for k, (i, _, _) in enumerate(edge_columns(z))}

    def window(i, planes, s, block, offset):
        pair = []
        for step in range(2):
            here = lax.rem(block + step, z.count)
            value = planes[here, s]
            if CX[i] == 1:
                side = edges[lax.rem(here + z.count - 1, z.count)]
                value = jnp.where(lanes == 0, roll(side, -columns[i]), roll(value, 1))
            elif CX[i] == -1:
                side = edges[lax.rem(here + 1, z.count)]
                value = jnp.where(lanes == last, roll(side, last - columns[i]), roll(value, -1))
            pair.append(value)
        first = jnp.where(lanes >= offset, pair[0], pair[1])
        second = jnp.where(lanes > offset, pair[0], pair[1])
        first = pltpu.roll(first, lax.rem(z.width - offset, z.width), 1)
        second = pltpu.roll(second, last - offset, 1)
        return first, second

    for s, i in enumerate(rising):
        near, next_one = window(i, tops, s, lax.rem(me + far, z.count), rest)
        fix = 6.0 * weights[i] * CX[i] * wall_speed
        value = (1.0 - weight) * near + weight * next_one
        put(i, value - fix if CX[i] else value)
    for s, i in enumerate(falling):
        block = lax.rem(me + 2 * z.count - far - 1, z.count)
        next_one, near = window(i, bottoms, s, block, last - rest)
        fix = 6.0 * weights[i] * CX[i] * wall_speed
        value = (1.0 - weight) * near + weight * next_one
        put(i, value + fix if CX[i] else value)


def wall_slot(i):
    return rising.index(i) if CY[i] == 1 else len(rising) + falling.index(i)


def first_kernel(z, whole_hbm, part_hbm, pop_hbm, solid_hbm, pop_ref, mask_ref, info_ref, *refs):
    sends, (whole_ref, part_ref, solid_ref, sems) = refs[: z.count - 1], refs[z.count - 1 :]
    group = z.planes // CHUNKS * z.depth
    copies = [pltpu.make_async_copy(solid_hbm, solid_ref, sems.at[CHUNKS])]
    for k in range(CHUNKS):
        part = (slice(None), pl.ds(k * group, group), slice(None))
        copies.append(pltpu.make_async_copy(pop_hbm.at[part], pop_ref.at[part], sems.at[k]))
    copies.append(pltpu.make_async_copy(whole_hbm, whole_ref, sems.at[CHUNKS + 1]))
    copies.append(pltpu.make_async_copy(part_hbm, part_ref, sems.at[CHUNKS + 2]))
    for copy in copies:
        copy.start()
    copies[0].wait()
    grow = lax.broadcasted_iota(jnp.int32, (z.wide, z.width), 1) // BLOCK
    grow = grow == lax.broadcasted_iota(jnp.int32, (z.wide, z.width), 0)
    grow = grow.astype(jnp.float32)
    for k in range(solid_ref.shape[0]):
        flags = jnp.where(solid_ref[k] > 0, 1.0, 0.0)
        line = jnp.dot(flags, grow, preferred_element_type=jnp.float32)
        mask_ref[pl.ds(k * z.deep, z.deep), :] = line

    lanes = z.lanes()
    couple = lanes // 2
    post, edge, solid_edge = {}, [None] * Q, None
    for y in range(z.planes):
        if y % (z.planes // CHUNKS) == 0:
            copies[1 + y // (z.planes // CHUNKS)].wait()
        flags = z.solid_tile(mask_ref, y)
        if y in (0, z.planes - 1):
            f = [z.tile(pop_ref, i, y) * np.float32(weights[i]) for i in range(Q)]
            values, _, _ = collide(f, flags > 0.5)
            for i in falling if y == 0 else rising:
                post[i, y] = values[i]

        def joined(value, old):
            value = roll(value, 2 * y + 1)
            return value if old is None else jnp.where(couple == y, value, old)

        edge = [joined(z.tile(pop_ref, i, y), edge[i]) for i in range(Q)]
        solid_edge = joined(flags, solid_edge)
    f = [edge[i] * np.float32(weights[i]) for i in range(Q)]
    values, _, _ = collide(f, solid_edge > 0.5)
    get = lambda i, y: post[i, y]
    right_edge = left_edge = wall_columns(z, get, lanes)
    for j in range(len(eastward)):
        hit = (lanes // (2 * z.planes) == j // 2) & (lanes % 2 == j % 2)
        right_edge = jnp.where(hit, roll(values[eastward[j]], z.at(j, 0)), right_edge)
        left_edge = jnp.where(hit, roll(values[westward[j]], z.at(j, 0) - 1), left_edge)
    copies[-2].wait()
    copies[-1].wait()
    for step in range(whole_ref.shape[0]):
        for k, ref in enumerate((whole_ref, part_ref)):
            value = ref[step].astype(jnp.float32)
            info_ref[pl.ds(2 * step + k, 1), :] = jnp.full((1, z.width), value, jnp.float32)
    pack_x(z, whole_ref[0], get, right_edge, left_edge, sends)


def collide_kernel(z, pop_ref, mask_ref, post_ref, acc_ref):
    for y in range(z.planes):
        solid = z.solid_tile(mask_ref, y) > 0.5
        f = [z.tile(pop_ref, i, y) * np.float32(weights[i]) for i in range(Q)]
        post, jx, moment_xy = collide(f, solid)
        here = pl.ds(y * z.depth, z.depth)
        for i in range(Q):
            post_ref[i, here, :] = post[i]
        acc_ref[0, here, :] = jnp.where(solid, 0.0, jx)
        acc_ref[1, here, :] = jnp.where(solid, 0.0, -(1.0 - 0.5 * visc_rate) * moment_xy)


def shift_of(info_ref, step):
    values = [jnp.max(info_ref[2 * step + k : 2 * step + k + 1, :]) for k in range(2)]
    return [value.astype(jnp.int32) for value in values]


def second_kernel(z, info_ref, post_ref, mask_ref, *refs):
    gets, outs = refs[: z.count - 1], refs[z.count - 1 : z.count + 3]
    inner_ref, outer_ref, wall_ref, side_ref = outs
    tops, bottoms, edges, rows_ref, columns_ref = refs[z.count + 3 :]
    whole, part = shift_of(info_ref, 0)
    left, right = fill_tables(z, post_ref, gets, tops, bottoms, edges)
    side_ref[0], side_ref[1] = left, right
    columns_ref[0], columns_ref[1] = left.T, right.T
    shape = (z.planes, z.width)
    lanes = lax.broadcasted_iota(jnp.int32, shape, 1)
    heights = lax.broadcasted_iota(jnp.int32, shape, 0)
    even = lax.rem(lax.axis_index("gz"), 2) == 0

    def line(i, row):
        value = post_ref[i, pl.ds(row, z.planes, stride=z.depth), :]
        if CX[i]:
            j = (eastward if CX[i] == 1 else westward).index(i)
            here = pl.ds(z.at(j, 0), z.planes, stride=2)
            column = columns_ref[0 if CX[i] == 1 else 1, here, :][:, row : row + 1]
            edge = 0 if CX[i] == 1 else z.width - 1
            value = jnp.where(lanes == edge, jnp.broadcast_to(column, shape), roll(value, CX[i]))
        if CY[i]:
            enter = 0 if CY[i] == 1 else z.planes - 1
            wall = jnp.broadcast_to(wall_ref[wall_slot(i), row : row + 1, :], shape)
            value = jnp.where(heights == enter, wall, roll(value, CY[i], 0))
        return value

    jobs = []
    for side in range(2):
        near, far = (z.depth - 1, z.depth - 2) if side == 0 else (0, 1)
        for k in range(Q):
            row = near if CZ[k] >= 0 else far
            i = k if CZ[k] >= 0 else mirror[k]
            jobs.append((side, k, i if side == 0 else mirror[i], row))
    for still in (True, False):
        for side, k, i, row in jobs:
            if (CY[i] == 0) == still:
                rows_ref[side, k] = line(i, row)
        if still:

            def put(i, value):
                wall_ref[wall_slot(i)] = value

            sliding(z, whole, part, tops, bottoms, edges, put)

    chunk = min(8, z.planes)
    for start in range(0, z.planes, chunk):
        here = pl.ds(start, chunk)
        found = []
        for side in range(2):
            f = [None] * Q
            for i in level:
                f[i] = rows_ref[side, i, here, :]
            for i in upward:
                f[i] = rows_ref[side, mirror[i], here, :]
            kept, others = moments(f)
            change = relax(others)
            values = [rows_ref[side, i, here, :] for i in upward]
            values += [f[i] - change[i] for i in upward]
            found.append(values + kept)
        for slot in range(MASK):
            up, down = found[0][slot], found[1][slot]
            inner_ref[slot, here, :] = jnp.where(even, up, down)
            outer_ref[slot, here, :] = jnp.where(even, down, up)
    for k in range(z.planes // BLOCK):
        up = mask_ref[(k + 1) * z.deep - 1 : (k + 1) * z.deep, :]
        down = mask_ref[k * z.deep : k * z.deep + 1, :]
        here = pl.ds(k * BLOCK, BLOCK)
        block = (BLOCK, z.width)
        inner_ref[MASK, here, :] = jnp.broadcast_to(jnp.where(even, up, down), block)
        outer_ref[MASK, here, :] = jnp.broadcast_to(jnp.where(even, down, up), block)


def bulk_kernel(z, post_ref, wall_ref, side_ref, h_ref):
    left, right = side_ref[0], side_ref[1]
    for i in range(Q):
        for y in range(z.planes):
            here = pl.ds(y * z.depth, z.depth)
            if 0 <= y - CY[i] < z.planes:
                h_ref[i, here, :] = moved_x(z, post_ref, i, y - CY[i], left, right)
            else:
                h_ref[i, here, :] = wall_ref[wall_slot(i)]


def middle_kernel(z, h_ref, mask_ref, old_ref, g_ref, acc_ref):
    for y in range(z.planes):
        solid = z.solid_tile(mask_ref, y) > 0.5
        f = [roll(z.tile(h_ref, i, y), CZ[i], 0) for i in range(Q)]
        post, jx, moment_xy = collide(f, solid)
        here = pl.ds(y * z.depth, z.depth)
        for i in range(Q):
            g_ref[i, here, :] = roll(post[i], CZ[i], 0)
        fields = [jx, -(1.0 - 0.5 * visc_rate) * moment_xy]
        for k in range(2):
            acc_ref[k, here, :] = old_ref[k, here, :] + jnp.where(solid, 0.0, fields[k])


def third_kernel(z, info_ref, h_ref, inner_ref, outer_ref, mask_ref, old_ref, *refs):
    (g_ref, acc_ref, part_ref), sends = refs[2:5], refs[5 : 4 + z.count]
    (sides,) = refs[4 + z.count :]
    whole, _ = shift_of(info_ref, 1)
    even = lax.rem(lax.axis_index("gz"), 2) == 0
    sides[jnp.where(even, 1, 0)] = inner_ref[...]
    sides[jnp.where(even, 0, 1)] = outer_ref[...]
    chunk = min(2 * BLOCK, z.planes)
    shape = (chunk, z.width)
    heights = lax.broadcasted_iota(jnp.int32, shape, 0)
    for side in range(2):
        edge, next_row = (0, 1) if side == 0 else (z.depth - 1, z.depth - 2)
        actual = list(range(Q)) if side == 0 else mirror
        for start in range(0, z.planes, chunk):
            here = pl.ds(start, chunk)

            def rows(row):
                return pl.ds(start * z.depth + row, chunk, stride=z.depth)

            own = {i: h_ref[actual[i], rows(edge), :] for i in level + downward}
            f = [None] * Q
            for i in downward:
                f[i] = own[i]
            kept, others = moments(f)
            kept = [plus(kept[k], sides[side, SUMS + k, here, :]) for k in range(4)]
            change = relax([minus(m, e) for m, e in zip(others, equilibrium(*kept))])
            solid = sides[side, MASK, here, :] > 0.5
            for s, i in enumerate(upward):
                value = sides[side, PART + s, here, :] - change[i]
                g_ref[actual[i], rows(edge), :] = jnp.where(solid, f[opposite[i]], value)

            for i in level:
                f[i] = own[i]
            for s, i in enumerate(upward):
                f[i] = sides[side, NEAR + s, here, :]
            for i in downward:
                f[i] = h_ref[actual[i], rows(next_row), :]
            solid = jnp.zeros(shape, jnp.float32)
            for k in range(chunk // BLOCK):
                at = (start // BLOCK + k) * z.deep + (0 if side == 0 else z.deep - 1)
                line = jnp.broadcast_to(mask_ref[at : at + 1, :], shape)
                solid = jnp.where(heights >= k * BLOCK, line, solid)
            solid = solid > 0.5
            post, jx, moment_xy = collide(f, solid)
            for i in level:
                g_ref[actual[i], rows(edge), :] = post[i]
            for i in upward:
                g_ref[actual[i], rows(next_row), :] = post[i]
            fields = [jx, -(1.0 - 0.5 * visc_rate) * moment_xy]
            for k in range(2):
                value = old_ref[k, rows(edge), :] + jnp.where(solid, 0.0, fields[k])
                acc_ref[k, rows(edge), :] = value
    lanes = z.lanes()
    sums = jnp.zeros((z.depth, z.width), jnp.float32)
    for y in range(z.planes):
        for k in range(2):
            total = z.spread(jnp.sum(z.tile(acc_ref, k, y), axis=1, keepdims=True))
            sums = jnp.where(lanes == k * z.planes + y, total, sums)
    part_ref[...] = sums
    pack_x(z, whole, functools.partial(z.tile, g_ref), *edge_tiles(z, g_ref), sends, sums)


def direct_kernel(z, g_ref, acc_ref, out_hbm, acc_hbm, turned_ref, sems):
    inner = (z.planes - 1) * z.depth
    copies = [pltpu.make_async_copy(acc_ref, acc_hbm, sems.at[len(straight)])]
    copies[0].start()
    for k, i in enumerate(straight):
        source, target = g_ref.at[i], out_hbm.at[i]
        if CY[i] == 1:
            source, target = source.at[pl.ds(0, inner), :], target.at[pl.ds(z.depth, inner), :]
        elif CY[i] == -1:
            source, target = source.at[pl.ds(z.depth, inner), :], target.at[pl.ds(0, inner), :]
        copies.append(pltpu.make_async_copy(source, target, sems.at[k]))
        copies[-1].start()
    for k, i in enumerate(slanted):
        for y in range(z.planes):
            if 0 <= y - CY[i] < z.planes:
                here = pl.ds(y * z.depth, z.depth)
                turned_ref[k, here, :] = roll(z.tile(g_ref, i, y - CY[i]), CX[i])
    for copy in copies:
        copy.wait()


def fourth_kernel(z, info_ref, g_ref, turned_ref, own_ref, *refs):
    gets, (_, out_hbm, profile_hbm) = refs[: z.count - 1], refs[z.count - 1 : z.count + 2]
    tops, bottoms, edges, out_ref, profile_ref, sems = refs[z.count + 2 :]
    whole, part = shift_of(info_ref, 1)
    terms = [own_ref[...]] + [gets[d - 1][z.slots(d)] for d in range(1, z.count)]
    while len(terms) > 1:
        terms = [terms[k] + terms[k + 1] for k in range(0, len(terms), 2)]
    for k in range(2):
        profile_ref[k] = terms[0][:, k * z.planes : (k + 1) * z.planes]
    copies = []

    def send(source, target):
        copies.append(pltpu.make_async_copy(source, target, sems.at[len(copies)]))
        copies[-1].start()

    send(profile_ref, profile_hbm)
    left, right = fill_tables(z, g_ref, gets, tops, bottoms, edges)
    group = z.planes // CHUNKS

    def interior(k):
        for i in slanted:
            for y in range(k * group, (k + 1) * group):
                if 0 <= y - CY[i] < z.planes:
                    here = pl.ds(y * z.depth, z.depth)
                    value = turned_ref[slanted.index(i), here, :]
                    out_ref[i, here, :] = mended(z, value, i, y - CY[i], left, right)

    def finish(k):
        here = pl.ds(k * group * z.depth, group * z.depth)
        for first, last in SPANS:
            part = (pl.ds(first, last - first), here, slice(None))
            send(out_ref.at[part], out_hbm.at[part])

    def put(i, value):
        here = pl.ds(0 if CY[i] == 1 else (z.planes - 1) * z.depth, z.depth)
        out_ref[i, here, :] = value
        if CX[i] == 0:
            send(out_ref.at[i, here, :], out_hbm.at[i, here, :])

    for k in range(1, CHUNKS - 1):
        interior(k)
        finish(k)
    for k in (0, CHUNKS - 1):
        interior(k)
    sliding(z, whole, part, tops, bottoms, edges, put)
    for k in (0, CHUNKS - 1):
        finish(k)
    for copy in copies:
        copy.wait()


def local(count, ranks, pop_ratio, solid_blocks, shift_whole, shift_frac):
    _, planes, depth, width = pop_ratio.shape
    z = Sizes(planes, depth, width, count)
    assert ranks % 2 == 0
    f32 = lambda *shape: pltpu.VMEM(shape, jnp.float32)
    hbm = lambda ref: jax.ShapeDtypeStruct(ref.shape, ref.dtype)
    keep = lambda *values: [pltpu.with_memory_space_constraint(v, pltpu.VMEM) for v in values]
    vmem = pl.BlockSpec(memory_space=pltpu.VMEM)
    outside = pl.BlockSpec(memory_space=pl.ANY)
    cells = f32(Q, planes * depth, width)
    fields = f32(2, planes * depth, width)
    halo = f32(SLOTS, planes, width)
    shifts = [pltpu.VMEM((count, len(rising), depth, width), jnp.float32)] * 2
    shifts.append(pltpu.VMEM((count, depth, width), jnp.float32))
    pair = pltpu.SMEM(shift_whole.shape, jnp.int32)
    sems = lambda number: pltpu.SemaphoreType.DMA((number,))
    outer_keep = lambda *values: [pltpu.with_memory_space_constraint(v, pltpu.HBM) for v in values]
    shift_whole, shift_frac, solid_blocks = outer_keep(shift_whole, shift_frac, solid_blocks)

    def buffers(more):
        return [f32(z.slots(d) + more, depth, width) for d in range(1, count)]

    def call(body, ins, outs, scratch=(), direct=(), alias=None):
        specs = [outside if k in direct else vmem for k in range(len(outs))]
        return pl.pallas_call(
            functools.partial(body, z),
            out_shape=outs,
            in_specs=ins,
            out_specs=specs,
            scratch_shapes=list(scratch),
            input_output_aliases=alias or {},
            compiler_params=pltpu.CompilerParams(vmem_limit_bytes=8 << 20),
        )

    def swap_x(values):
        return [
            lax.ppermute(values[d - 1], "gx", [(i, i ^ d) for i in range(count)])
            for d in range(1, count)
        ]

    pairs = [(i, i ^ 1) for i in range(ranks)]
    across = [(i, (i - 1 if i % 2 == 0 else i + 1) % ranks) for i in range(ranks)]

    (pop,) = outer_keep(pop_ratio.reshape(cells.shape))
    mask_shape = f32(planes // BLOCK * z.deep, width)
    loaded, mask, info, *sends = call(
        first_kernel,
        [outside] * 4,
        [cells, mask_shape, f32(2 * shift_whole.shape[0], width)] + buffers(0),
        [pair, pair, pltpu.VMEM(solid_blocks.shape, jnp.int32), sems(CHUNKS + 3)],
    )(shift_whole, shift_frac, pop, solid_blocks)
    post, old = call(collide_kernel, [vmem] * 2, [cells, fields])(*keep(loaded, mask))
    gets = swap_x(sends)
    walls, both = f32(2 * len(rising), depth, width), f32(2, depth, width)
    inner, outer, wall, side = call(
        second_kernel,
        [vmem] * (2 + count),
        [halo, halo, walls, both],
        shifts + [f32(2, Q, planes, width), f32(2, width, depth)],
    )(*keep(info, post, mask, *gets))
    outer = lax.ppermute(outer, "gz", across)
    inner = lax.ppermute(inner, "gz", pairs)
    (h,) = call(bulk_kernel, [vmem] * 3, [cells])(*keep(post, wall, side))
    g, acc = call(middle_kernel, [vmem] * 3, [cells, fields])(*keep(h, mask, old))
    g, acc, own, *sends = call(
        third_kernel,
        [vmem] * 8,
        [cells, fields, f32(depth, width)] + buffers(1),
        [pltpu.VMEM((2, SLOTS, planes, width), jnp.float32)],
        alias={6: 0, 7: 1},
    )(*keep(info, h, inner, outer, mask, old, g, acc))
    gets = swap_x(sends)
    turned = f32(len(slanted), planes * depth, width)
    out, acc, turned = call(
        direct_kernel,
        [vmem] * 2,
        [hbm(cells), hbm(fields), turned],
        [sems(len(straight) + 1)],
        [0, 1],
    )(*keep(g, acc))
    moves = 1 + len(SPANS) * CHUNKS + sum(CX[i] == 0 for i in rising + falling)
    out, profile = call(
        fourth_kernel,
        [vmem] * (3 + count) + [outside],
        [hbm(cells), hbm(f32(2, depth, planes))],
        shifts + [cells, f32(2, depth, planes), sems(moves)],
        [0, 1],
        {3 + count: 0},
    )(*keep(info, g, turned, own, *gets), out)
    return (
        out.reshape(pop_ratio.shape),
        acc.reshape(2, planes, depth, width),
        jnp.swapaxes(profile, 1, 2),
    )


def solution(mesh):
    return jax.shard_map(
        functools.partial(local, mesh.shape["gx"], mesh.shape["gz"]),
        mesh=mesh,
        in_specs=(P(None, None, "gz", "gx"), P(None, "gz", "gx"), P(), P()),
        out_specs=(P(None, None, "gz", "gx"), P(None, None, "gz", "gx"), P(None, None, "gz")),
        check_vma=False,
    )
```

```python
import functools

import jax
import jax.numpy as jnp
import numpy as np
from jax import lax
from jax.experimental import pallas as pl
from jax.experimental.pallas import tpu as pltpu
from jax.sharding import PartitionSpec as P


BLOCK = 4
velocity_list = [
    (0, 0, 0),
    (1, 0, 0),
    (-1, 0, 0),
    (0, 1, 0),
    (0, -1, 0),
    (0, 0, 1),
    (0, 0, -1),
    (1, 1, 0),
    (-1, -1, 0),
    (1, -1, 0),
    (-1, 1, 0),
    (1, 0, 1),
    (-1, 0, -1),
    (1, 0, -1),
    (-1, 0, 1),
    (0, 1, 1),
    (0, -1, -1),
    (0, 1, -1),
    (0, -1, 1),
]
Q = len(velocity_list)
weights = [1.0 / 3.0] + [1.0 / 18.0] * 6 + [1.0 / 36.0] * 12
CX = [v[0] for v in velocity_list]
CY = [v[1] for v in velocity_list]
CZ = [v[2] for v in velocity_list]
opposite = [velocity_list.index((-x, -y, -z)) for x, y, z in velocity_list]
mirror = [velocity_list.index((x, y, -z)) for x, y, z in velocity_list]
rising = [i for i in range(Q) if CY[i] == 1]
falling = [i for i in range(Q) if CY[i] == -1]
eastward = [i for i in range(Q) if CX[i] == 1]
westward = [i for i in range(Q) if CX[i] == -1]
upward = [i for i in range(Q) if CZ[i] == 1]
level = [i for i in range(Q) if CZ[i] == 0]
downward = [mirror[i] for i in upward]
straight = [i for i in range(Q) if CX[i] == 0]
slanted = [i for i in range(Q) if CX[i] != 0]
SPANS = [(i, next(k for k in range(i, Q + 1) if k == Q or CX[k] == 0)) for i in slanted if CX[i - 1] == 0]
NEAR, PART, SUMS = 0, len(upward), 2 * len(upward)
MASK = SUMS + 4
SLOTS = MASK + 1
wall_speed = 0.08
visc_rate = 1.25
fraction_unit = 4096.0
relax_rates = [0.0, 1.19, 1.4, 0.0, 1.2, 0.0, 1.2, 0.0, 1.2, 1.25, 1.4, 1.25, 1.4]
relax_rates += [1.25, 1.25, 1.25, 1.98, 1.98, 1.98]


def row_norms():
    v = np.array(velocity_list, dtype=np.float64)
    x, y, z = v[:, 0], v[:, 1], v[:, 2]
    s = x * x + y * y + z * z
    rows = [
        np.ones(Q),
        19 * s - 30,
        (21 * s * s - 53 * s + 24) / 2,
        x,
        (5 * s - 9) * x,
        y,
        (5 * s - 9) * y,
        z,
        (5 * s - 9) * z,
        3 * x * x - s,
        (3 * s - 5) * (3 * x * x - s),
        y * y - z * z,
        (3 * s - 5) * (y * y - z * z),
        x * y,
        y * z,
        x * z,
        (y * y - z * z) * x,
        (z * z - x * x) * y,
        (x * x - y * y) * z,
    ]
    return [float(np.sum(row * row)) for row in rows]


RATE = [rate / norm for rate, norm in zip(relax_rates, row_norms())]


def plus(a, b):
    return b if a is None else a if b is None else a + b


def minus(a, b):
    return a if b is None else -b if a is None else a - b


def scaled(factor, a):
    return None if a is None else factor * a


def moments(f):
    sums = {i: plus(f[i], f[i + 1]) for i in range(1, Q, 2)}
    difs = {i: minus(f[i], f[i + 1]) for i in range(1, Q, 2)}
    p1, d1 = plus(sums[7], sums[9]), minus(sums[7], sums[9])
    p2, d2 = plus(sums[11], sums[13]), minus(sums[11], sums[13])
    p3, d3 = plus(sums[15], sums[17]), minus(sums[15], sums[17])
    s23 = plus(sums[3], sums[5])
    axis = plus(sums[1], s23)
    p12 = plus(p1, p2)
    diag = plus(p12, p3)
    a, c = plus(difs[7], difs[9]), minus(difs[7], difs[9])
    b, e = plus(difs[11], difs[13]), minus(difs[11], difs[13])
    d, g = plus(difs[15], difs[17]), minus(difs[15], difs[17])
    ab, cd, eg = plus(a, b), plus(c, d), plus(e, g)
    axis_x, diag_x = minus(scaled(2.0, sums[1]), s23), minus(p12, scaled(2.0, p3))
    axis_w, diag_w = minus(sums[3], sums[5]), minus(p1, p2)
    kept = [
        plus(f[0], plus(axis, diag)),
        plus(difs[1], ab),
        plus(difs[3], cd),
        plus(difs[5], eg),
    ]
    others = [
        minus(diag, f[0]),
        minus(plus(f[0], diag), scaled(2.0, axis)),
        minus(ab, scaled(2.0, difs[1])),
        minus(cd, scaled(2.0, difs[3])),
        minus(eg, scaled(2.0, difs[5])),
        plus(axis_x, diag_x),
        minus(diag_x, scaled(2.0, axis_x)),
        plus(axis_w, diag_w),
        minus(diag_w, scaled(2.0, axis_w)),
        d1,
        d3,
        d2,
        minus(a, b),
        minus(d, c),
        minus(e, g),
    ]
    return kept, others


def equilibrium(rho, jx, jy, jz):
    inverse = 1.0 / rho
    ux, uy, uz = jx * inverse, jy * inverse, jz * inverse
    xx, yy, zz = jx * ux, jy * uy, jz * uz
    yz_sum, yz_dif = yy + zz, yy - zz
    square = xx + yz_sum
    eq_x = 2.0 * xx - yz_sum
    eq = [square, None, None, None, None]
    eq += [eq_x, -0.5 * eq_x, yz_dif, -0.5 * yz_dif, jx * uy, jy * uz, jx * uz]
    return eq + [None] * 3


ORDER = [4, 6, 8, 9, 10, 11, 12, 13, 14, 15, 16, 17, 18]
FLOW = 5.0 / 3.0


def relax(moment):
    level_a, level_c = moment[:2]
    factors = [RATE[k] * (FLOW if k in (4, 6, 8) else 1.0) for k in ORDER]
    scaled_by = [scaled(k, m) for k, m in zip(factors, moment[2:])]
    flow_x, flow_y, flow_z, even_x, even_px, even_w, even_pw = scaled_by[:7]
    even_xy, even_yz, even_xz, twist_x, twist_y, twist_z = scaled_by[7:]

    def blend(by_e, by_s):
        rate_e, rate_s = by_e * RATE[1], by_s * RATE[2]
        return plus(scaled(19.0 * rate_e - 5.5 * rate_s, level_a), scaled(3.5 * rate_s, level_c))

    base_axis = blend(-11.0, -4.0)
    base_diag = blend(8.0, 1.0)
    lean = minus(even_x, scaled(2.0, even_px))
    tilt = minus(even_w, scaled(2.0, even_pw))
    side_x, side_w = plus(even_x, even_px), plus(even_w, even_pw)
    flat = plus(base_diag, side_x)
    diag_xy, diag_xz = plus(flat, side_w), minus(flat, side_w)
    diag_yz = minus(base_diag, scaled(2.0, side_x))
    low = minus(base_axis, lean)
    even = {
        1: plus(base_axis, scaled(2.0, lean)),
        3: plus(low, tilt),
        5: minus(low, tilt),
        7: plus(diag_xy, even_xy),
        9: minus(diag_xy, even_xy),
        11: plus(diag_xz, even_xz),
        13: minus(diag_xz, even_xz),
        15: plus(diag_yz, even_yz),
        17: minus(diag_yz, even_yz),
    }
    x_up, x_down = plus(flow_x, twist_x), minus(flow_x, twist_x)
    y_up, y_down = plus(flow_y, twist_y), minus(flow_y, twist_y)
    z_up, z_down = plus(flow_z, twist_z), minus(flow_z, twist_z)
    odd = {
        1: scaled(-4.0, flow_x),
        3: scaled(-4.0, flow_y),
        5: scaled(-4.0, flow_z),
        7: plus(x_up, y_down),
        9: minus(x_up, y_down),
        11: plus(x_down, z_up),
        13: minus(x_down, z_up),
        15: plus(y_up, z_down),
        17: minus(y_up, z_down),
    }
    out = [blend(-30.0, 12.0)]
    for i in range(1, Q, 2):
        out += [plus(even[i], odd[i]), minus(even[i], odd[i])]
    return out


def collide(f, solid):
    kept, others = moments(f)
    rest = [minus(m, e) for m, e in zip(others, equilibrium(*kept))]
    change = relax(rest)
    post = [jnp.where(solid, f[opposite[i]], f[i] - change[i]) for i in range(Q)]
    return post, kept[1], rest[9]


CHUNKS = 4
LOADS = 2


class Sizes:
    def __init__(self, planes, depth, width, count):
        self.planes, self.depth, self.width, self.count = planes, depth, width, count
        self.deep, self.wide = depth // BLOCK, width // BLOCK
        assert count >= 4 and count & (count - 1) == 0
        self.walls = 2 * planes * (len(eastward) + 1) // 2
        assert len(eastward) % 2 == 1 and self.walls + 4 <= width

    def slots(self, delta):
        return (2 if delta == self.count // 2 else 1) * len(rising) + 1

    def at(self, j, y):
        return 2 * self.planes * (j // 2) + 2 * y + j % 2

    def tile(self, ref, i, y):
        return ref[i, pl.ds(y * self.depth, self.depth), :]

    def lanes(self):
        return lax.broadcasted_iota(jnp.int32, (self.depth, self.width), 1)

    def rows(self):
        return lax.broadcasted_iota(jnp.int32, (self.depth, self.width), 0)

    def spread(self, row):
        return jnp.broadcast_to(row, (self.depth, self.width))

    def solid_tile(self, mask_ref, y):
        base = y // BLOCK * self.deep
        out = self.spread(mask_ref[base : base + 1, :])
        rows = self.rows()
        for step in range(1, self.deep):
            line = self.spread(mask_ref[base + step : base + step + 1, :])
            out = jnp.where(rows >= step * BLOCK, line, out)
        return out


def roll(value, shift, axis=1):
    shift = shift % value.shape[axis]
    return pltpu.roll(value, shift, axis) if shift else value


def edge_columns(z):
    return [
        (7, z.planes - 1, True),
        (10, z.planes - 1, False),
        (9, 0, True),
        (8, 0, False),
    ]


def wall_columns(z, get, lanes):
    out = jnp.zeros((z.depth, z.width), jnp.float32)
    for k, (i, y, right) in enumerate(edge_columns(z)):
        at = z.walls + k
        moved = roll(get(i, y), at - (z.width - 1 if right else 0))
        out = jnp.where(lanes == at, moved, out)
    return out


def edge_tiles(z, ref):
    lanes = z.lanes()
    right_edge = wall_columns(z, functools.partial(z.tile, ref), lanes)
    left_edge = right_edge
    for j in range(len(eastward)):
        for y in range(z.planes):
            at = z.at(j, y)
            hit = lanes == at
            moved = roll(z.tile(ref, eastward[j], y), at - (z.width - 1))
            right_edge = jnp.where(hit, moved, right_edge)
            moved = roll(z.tile(ref, westward[j], y), at)
            left_edge = jnp.where(hit, moved, left_edge)
    return right_edge, left_edge


def pack_x(z, whole, get, right_edge, left_edge, sends, extra=None):
    me = lax.axis_index("gx")
    far = lax.div(whole, z.width)
    for delta in range(1, z.count):
        send = sends[delta - 1]
        partner = jnp.bitwise_xor(me, delta)
        ahead = lax.rem(me - partner + z.count, z.count)
        at_top = (ahead == far) | (ahead == lax.rem(far + 1, z.count))
        for s in range(len(rising)):
            top = get(rising[s], z.planes - 1)
            bottom = get(falling[s], 0)
            if delta == z.count // 2:
                send[s] = top
                send[len(rising) + s] = bottom
            else:
                send[s] = jnp.where(at_top, top, bottom)
        to_right = partner == lax.rem(me + 1, z.count)
        slots = z.slots(delta)
        send[slots - 1] = jnp.where(to_right, right_edge, left_edge)
        if extra is not None:
            send[slots] = extra


def fill_tables(z, ref, gets, tops, bottoms, edges):
    me = lax.axis_index("gx")
    for s in range(len(rising)):
        tops[me, s] = z.tile(ref, rising[s], z.planes - 1)
        bottoms[me, s] = z.tile(ref, falling[s], 0)
    edges[me] = wall_columns(z, functools.partial(z.tile, ref), z.lanes())
    for delta in range(1, z.count):
        get = gets[delta - 1]
        partner = jnp.bitwise_xor(me, delta)
        for s in range(len(rising)):
            tops[partner, s] = get[s]
            second = len(rising) + s if delta == z.count // 2 else s
            bottoms[partner, s] = get[second]
        edges[partner] = get[z.slots(delta) - 1]
    left = edges[lax.rem(me + z.count - 1, z.count)]
    right = edges[lax.rem(me + 1, z.count)]
    return left, right


def mended(z, value, i, y, left, right):
    lanes, last = z.lanes(), z.width - 1
    if CX[i] == 1:
        at = z.at(eastward.index(i), y)
        return jnp.where(lanes == 0, roll(left, -at), value)
    if CX[i] == -1:
        at = z.at(westward.index(i), y)
        return jnp.where(lanes == last, roll(right, last - at), value)
    return value


def moved_x(z, ref, i, y, left, right):
    return mended(z, roll(z.tile(ref, i, y), CX[i]), i, y, left, right)


def sliding(z, whole, part, tops, bottoms, edges, put):
    me = lax.axis_index("gx")
    lanes, last = z.lanes(), z.width - 1
    weight = part.astype(jnp.float32) / fraction_unit
    far = lax.div(whole, z.width)
    rest = lax.rem(whole, z.width)
    columns = {i: z.walls + k for k, (i, _, _) in enumerate(edge_columns(z))}

    def window(i, planes, s, block, offset):
        pair = []
        for step in range(2):
            here = lax.rem(block + step, z.count)
            value = planes[here, s]
            if CX[i] == 1:
                side = edges[lax.rem(here + z.count - 1, z.count)]
                value = jnp.where(lanes == 0, roll(side, -columns[i]), roll(value, 1))
            elif CX[i] == -1:
                side = edges[lax.rem(here + 1, z.count)]
                value = jnp.where(lanes == last, roll(side, last - columns[i]), roll(value, -1))
            pair.append(value)
        first = jnp.where(lanes >= offset, pair[0], pair[1])
        second = jnp.where(lanes > offset, pair[0], pair[1])
        first = pltpu.roll(first, lax.rem(z.width - offset, z.width), 1)
        second = pltpu.roll(second, last - offset, 1)
        return first, second

    for s, i in enumerate(rising):
        near, next_one = window(i, tops, s, lax.rem(me + far, z.count), rest)
        fix = 6.0 * weights[i] * CX[i] * wall_speed
        value = (1.0 - weight) * near + weight * next_one
        put(i, value - fix if CX[i] else value)
    for s, i in enumerate(falling):
        block = lax.rem(me + 2 * z.count - far - 1, z.count)
        next_one, near = window(i, bottoms, s, block, last - rest)
        fix = 6.0 * weights[i] * CX[i] * wall_speed
        value = (1.0 - weight) * near + weight * next_one
        put(i, value + fix if CX[i] else value)


def wall_slot(i):
    return rising.index(i) if CY[i] == 1 else len(rising) + falling.index(i)


def first_kernel(z, whole_hbm, part_hbm, pop_hbm, solid_hbm, pop_ref, mask_ref, info_ref, *refs):
    sends, (whole_ref, part_ref, solid_ref, sems) = refs[: z.count - 1], refs[z.count - 1 :]
    group = z.planes // LOADS * z.depth
    copies = [pltpu.make_async_copy(solid_hbm, solid_ref, sems.at[LOADS])]
    for k in range(LOADS):
        part = (slice(None), pl.ds(k * group, group), slice(None))
        copies.append(pltpu.make_async_copy(pop_hbm.at[part], pop_ref.at[part], sems.at[k]))
    copies.append(pltpu.make_async_copy(whole_hbm, whole_ref, sems.at[LOADS + 1]))
    copies.append(pltpu.make_async_copy(part_hbm, part_ref, sems.at[LOADS + 2]))
    for copy in copies:
        copy.start()
    copies[0].wait()
    grow = lax.broadcasted_iota(jnp.int32, (z.wide, z.width), 1) // BLOCK
    grow = grow == lax.broadcasted_iota(jnp.int32, (z.wide, z.width), 0)
    grow = grow.astype(jnp.float32)
    for k in range(solid_ref.shape[0]):
        flags = jnp.where(solid_ref[k] > 0, 1.0, 0.0)
        line = jnp.dot(flags, grow, preferred_element_type=jnp.float32)
        mask_ref[pl.ds(k * z.deep, z.deep), :] = line

    lanes = z.lanes()
    couple = lanes // 2
    post, edge, solid_edge = {}, [None] * Q, None
    for y in range(z.planes):
        if y % (z.planes // LOADS) == 0:
            copies[1 + y // (z.planes // LOADS)].wait()
        flags = z.solid_tile(mask_ref, y)
        if y in (0, z.planes - 1):
            f = [z.tile(pop_ref, i, y) * np.float32(weights[i]) for i in range(Q)]
            values, _, _ = collide(f, flags > 0.5)
            for i in falling if y == 0 else rising:
                post[i, y] = values[i]

        def joined(value, old):
            value = roll(value, 2 * y + 1)
            return value if old is None else jnp.where(couple == y, value, old)

        edge = [joined(z.tile(pop_ref, i, y), edge[i]) for i in range(Q)]
        solid_edge = joined(flags, solid_edge)
    f = [edge[i] * np.float32(weights[i]) for i in range(Q)]
    values, _, _ = collide(f, solid_edge > 0.5)
    get = lambda i, y: post[i, y]
    right_edge = left_edge = wall_columns(z, get, lanes)
    for j in range(len(eastward)):
        hit = (lanes // (2 * z.planes) == j // 2) & (lanes % 2 == j % 2)
        right_edge = jnp.where(hit, roll(values[eastward[j]], z.at(j, 0)), right_edge)
        left_edge = jnp.where(hit, roll(values[westward[j]], z.at(j, 0) - 1), left_edge)
    copies[-2].wait()
    copies[-1].wait()
    for step in range(whole_ref.shape[0]):
        for k, ref in enumerate((whole_ref, part_ref)):
            value = ref[step].astype(jnp.float32)
            info_ref[pl.ds(2 * step + k, 1), :] = jnp.full((1, z.width), value, jnp.float32)
    pack_x(z, whole_ref[0], get, right_edge, left_edge, sends)


def collide_kernel(z, pop_ref, mask_ref, post_ref, acc_ref):
    for y in range(z.planes):
        solid = z.solid_tile(mask_ref, y) > 0.5
        f = [z.tile(pop_ref, i, y) * np.float32(weights[i]) for i in range(Q)]
        post, jx, moment_xy = collide(f, solid)
        here = pl.ds(y * z.depth, z.depth)
        for i in range(Q):
            post_ref[i, here, :] = post[i]
        acc_ref[0, here, :] = jnp.where(solid, 0.0, jx)
        acc_ref[1, here, :] = jnp.where(solid, 0.0, -(1.0 - 0.5 * visc_rate) * moment_xy)


def shift_of(info_ref, step):
    values = [info_ref[2 * step + k : 2 * step + k + 1, :][0, 0] for k in range(2)]
    return [value.astype(jnp.int32) for value in values]


def second_kernel(z, info_ref, post_ref, mask_ref, *refs):
    gets, outs = refs[: z.count - 1], refs[z.count - 1 : z.count + 3]
    inner_ref, outer_ref, wall_ref, side_ref = outs
    tops, bottoms, edges, rows_ref, columns_ref = refs[z.count + 3 :]
    whole, part = shift_of(info_ref, 0)
    left, right = fill_tables(z, post_ref, gets, tops, bottoms, edges)
    side_ref[0], side_ref[1] = left, right
    columns_ref[0], columns_ref[1] = left.T, right.T
    shape = (z.planes, z.width)
    lanes = lax.broadcasted_iota(jnp.int32, shape, 1)
    heights = lax.broadcasted_iota(jnp.int32, shape, 0)
    even = lax.rem(lax.axis_index("gz"), 2) == 0

    def line(i, row):
        value = post_ref[i, pl.ds(row, z.planes, stride=z.depth), :]
        if CX[i]:
            j = (eastward if CX[i] == 1 else westward).index(i)
            here = pl.ds(z.at(j, 0), z.planes, stride=2)
            column = columns_ref[0 if CX[i] == 1 else 1, here, :][:, row : row + 1]
            edge = 0 if CX[i] == 1 else z.width - 1
            value = jnp.where(lanes == edge, jnp.broadcast_to(column, shape), roll(value, CX[i]))
        if CY[i]:
            enter = 0 if CY[i] == 1 else z.planes - 1
            wall = jnp.broadcast_to(wall_ref[wall_slot(i), row : row + 1, :], shape)
            value = jnp.where(heights == enter, wall, roll(value, CY[i], 0))
        return value

    jobs = []
    for side in range(2):
        near, far = (z.depth - 1, z.depth - 2) if side == 0 else (0, 1)
        for k in range(Q):
            row = near if CZ[k] >= 0 else far
            i = k if CZ[k] >= 0 else mirror[k]
            jobs.append((side, k, i if side == 0 else mirror[i], row))
    for still in (True, False):
        for side, k, i, row in jobs:
            if (CY[i] == 0) == still:
                rows_ref[side, k] = line(i, row)
        if still:

            def put(i, value):
                wall_ref[wall_slot(i)] = value

            sliding(z, whole, part, tops, bottoms, edges, put)

    chunk = min(8, z.planes)
    for start in range(0, z.planes, chunk):
        here = pl.ds(start, chunk)
        found = []
        for side in range(2):
            f = [None] * Q
            for i in level:
                f[i] = rows_ref[side, i, here, :]
            for i in upward:
                f[i] = rows_ref[side, mirror[i], here, :]
            kept, others = moments(f)
            change = relax(others)
            values = [rows_ref[side, i, here, :] for i in upward]
            values += [f[i] - change[i] for i in upward]
            found.append(values + kept)
        for slot in range(MASK):
            up, down = found[0][slot], found[1][slot]
            inner_ref[slot, here, :] = jnp.where(even, up, down)
            outer_ref[slot, here, :] = jnp.where(even, down, up)
    for k in range(z.planes // BLOCK):
        up = mask_ref[(k + 1) * z.deep - 1 : (k + 1) * z.deep, :]
        down = mask_ref[k * z.deep : k * z.deep + 1, :]
        here = pl.ds(k * BLOCK, BLOCK)
        block = (BLOCK, z.width)
        inner_ref[MASK, here, :] = jnp.broadcast_to(jnp.where(even, up, down), block)
        outer_ref[MASK, here, :] = jnp.broadcast_to(jnp.where(even, down, up), block)


def bulk_kernel(z, post_ref, wall_ref, side_ref, h_ref):
    left, right = side_ref[0], side_ref[1]
    for i in range(Q):
        for y in range(z.planes):
            here = pl.ds(y * z.depth, z.depth)
            if 0 <= y - CY[i] < z.planes:
                h_ref[i, here, :] = moved_x(z, post_ref, i, y - CY[i], left, right)
            else:
                h_ref[i, here, :] = wall_ref[wall_slot(i)]


def middle_kernel(z, h_ref, mask_ref, old_ref, g_ref, acc_ref):
    for y in range(z.planes):
        solid = z.solid_tile(mask_ref, y) > 0.5
        f = [roll(z.tile(h_ref, i, y), CZ[i], 0) for i in range(Q)]
        post, jx, moment_xy = collide(f, solid)
        here = pl.ds(y * z.depth, z.depth)
        for i in range(Q):
            g_ref[i, here, :] = roll(post[i], CZ[i], 0)
        fields = [jx, -(1.0 - 0.5 * visc_rate) * moment_xy]
        for k in range(2):
            acc_ref[k, here, :] = old_ref[k, here, :] + jnp.where(solid, 0.0, fields[k])


def third_kernel(z, info_ref, h_ref, inner_ref, outer_ref, mask_ref, old_ref, *refs):
    (g_ref, acc_ref, part_ref), sends = refs[2:5], refs[5 : 4 + z.count]
    (sides,) = refs[4 + z.count :]
    whole, _ = shift_of(info_ref, 1)
    even = lax.rem(lax.axis_index("gz"), 2) == 0
    sides[jnp.where(even, 1, 0)] = inner_ref[...]
    sides[jnp.where(even, 0, 1)] = outer_ref[...]
    chunk = min(2 * BLOCK, z.planes)
    shape = (chunk, z.width)
    heights = lax.broadcasted_iota(jnp.int32, shape, 0)
    for side in range(2):
        edge, next_row = (0, 1) if side == 0 else (z.depth - 1, z.depth - 2)
        actual = list(range(Q)) if side == 0 else mirror
        for start in range(0, z.planes, chunk):
            here = pl.ds(start, chunk)

            def rows(row):
                return pl.ds(start * z.depth + row, chunk, stride=z.depth)

            own = {i: h_ref[actual[i], rows(edge), :] for i in level + downward}
            f = [None] * Q
            for i in downward:
                f[i] = own[i]
            kept, others = moments(f)
            kept = [plus(kept[k], sides[side, SUMS + k, here, :]) for k in range(4)]
            change = relax([minus(m, e) for m, e in zip(others, equilibrium(*kept))])
            solid = sides[side, MASK, here, :] > 0.5
            for s, i in enumerate(upward):
                value = sides[side, PART + s, here, :] - change[i]
                g_ref[actual[i], rows(edge), :] = jnp.where(solid, f[opposite[i]], value)

            for i in level:
                f[i] = own[i]
            for s, i in enumerate(upward):
                f[i] = sides[side, NEAR + s, here, :]
            for i in downward:
                f[i] = h_ref[actual[i], rows(next_row), :]
            solid = jnp.zeros(shape, jnp.float32)
            for k in range(chunk // BLOCK):
                at = (start // BLOCK + k) * z.deep + (0 if side == 0 else z.deep - 1)
                line = jnp.broadcast_to(mask_ref[at : at + 1, :], shape)
                solid = jnp.where(heights >= k * BLOCK, line, solid)
            solid = solid > 0.5
            post, jx, moment_xy = collide(f, solid)
            for i in level:
                g_ref[actual[i], rows(edge), :] = post[i]
            for i in upward:
                g_ref[actual[i], rows(next_row), :] = post[i]
            fields = [jx, -(1.0 - 0.5 * visc_rate) * moment_xy]
            for k in range(2):
                value = old_ref[k, rows(edge), :] + jnp.where(solid, 0.0, fields[k])
                acc_ref[k, rows(edge), :] = value
    lanes = z.lanes()
    sums = jnp.zeros((z.depth, z.width), jnp.float32)
    for y in range(z.planes):
        for k in range(2):
            total = z.spread(jnp.sum(z.tile(acc_ref, k, y), axis=1, keepdims=True))
            sums = jnp.where(lanes == k * z.planes + y, total, sums)
    part_ref[...] = sums
    pack_x(z, whole, functools.partial(z.tile, g_ref), *edge_tiles(z, g_ref), sends, sums)


def direct_kernel(z, g_ref, acc_ref, out_hbm, acc_hbm, turned_ref, sems):
    inner = (z.planes - 1) * z.depth
    copies = [pltpu.make_async_copy(acc_ref, acc_hbm, sems.at[len(straight)])]
    copies[0].start()
    for k, i in enumerate(straight):
        source, target = g_ref.at[i], out_hbm.at[i]
        if CY[i] == 1:
            source, target = source.at[pl.ds(0, inner), :], target.at[pl.ds(z.depth, inner), :]
        elif CY[i] == -1:
            source, target = source.at[pl.ds(z.depth, inner), :], target.at[pl.ds(0, inner), :]
        copies.append(pltpu.make_async_copy(source, target, sems.at[k]))
        copies[-1].start()
    for k, i in enumerate(slanted):
        for y in range(z.planes):
            if 0 <= y - CY[i] < z.planes:
                here = pl.ds(y * z.depth, z.depth)
                turned_ref[k, here, :] = roll(z.tile(g_ref, i, y - CY[i]), CX[i])
    for copy in copies:
        copy.wait()


def fourth_kernel(z, info_ref, g_ref, turned_ref, own_ref, *refs):
    gets, (_, out_hbm, profile_hbm) = refs[: z.count - 1], refs[z.count - 1 : z.count + 2]
    tops, bottoms, edges, out_ref, profile_ref, sems = refs[z.count + 2 :]
    whole, part = shift_of(info_ref, 1)
    terms = [own_ref[...]] + [gets[d - 1][z.slots(d)] for d in range(1, z.count)]
    while len(terms) > 1:
        terms = [terms[k] + terms[k + 1] for k in range(0, len(terms), 2)]
    for k in range(2):
        profile_ref[k] = terms[0][:, k * z.planes : (k + 1) * z.planes]
    copies = []

    def send(source, target):
        copies.append(pltpu.make_async_copy(source, target, sems.at[len(copies)]))
        copies[-1].start()

    send(profile_ref, profile_hbm)
    left, right = fill_tables(z, g_ref, gets, tops, bottoms, edges)
    group = z.planes // CHUNKS

    def interior(k):
        for i in slanted:
            for y in range(k * group, (k + 1) * group):
                if 0 <= y - CY[i] < z.planes:
                    here = pl.ds(y * z.depth, z.depth)
                    value = turned_ref[slanted.index(i), here, :]
                    out_ref[i, here, :] = mended(z, value, i, y - CY[i], left, right)

    def finish(k):
        here = pl.ds(k * group * z.depth, group * z.depth)
        for first, last in SPANS:
            part = (pl.ds(first, last - first), here, slice(None))
            send(out_ref.at[part], out_hbm.at[part])

    def put(i, value):
        here = pl.ds(0 if CY[i] == 1 else (z.planes - 1) * z.depth, z.depth)
        out_ref[i, here, :] = value
        if CX[i] == 0:
            send(out_ref.at[i, here, :], out_hbm.at[i, here, :])

    for k in range(1, CHUNKS - 1):
        interior(k)
        finish(k)
    for k in (0, CHUNKS - 1):
        interior(k)
    sliding(z, whole, part, tops, bottoms, edges, put)
    for k in (0, CHUNKS - 1):
        finish(k)
    for copy in copies:
        copy.wait()


def local(count, ranks, pop_ratio, solid_blocks, shift_whole, shift_frac):
    _, planes, depth, width = pop_ratio.shape
    z = Sizes(planes, depth, width, count)
    assert ranks % 2 == 0
    f32 = lambda *shape: pltpu.VMEM(shape, jnp.float32)
    hbm = lambda ref: jax.ShapeDtypeStruct(ref.shape, ref.dtype)
    keep = lambda *values: [pltpu.with_memory_space_constraint(v, pltpu.VMEM) for v in values]
    vmem = pl.BlockSpec(memory_space=pltpu.VMEM)
    outside = pl.BlockSpec(memory_space=pl.ANY)
    cells = f32(Q, planes * depth, width)
    fields = f32(2, planes * depth, width)
    halo = f32(SLOTS, planes, width)
    shifts = [pltpu.VMEM((count, len(rising), depth, width), jnp.float32)] * 2
    shifts.append(pltpu.VMEM((count, depth, width), jnp.float32))
    pair = pltpu.SMEM(shift_whole.shape, jnp.int32)
    sems = lambda number: pltpu.SemaphoreType.DMA((number,))
    outer_keep = lambda *values: [pltpu.with_memory_space_constraint(v, pltpu.HBM) for v in values]
    shift_whole, shift_frac, solid_blocks = outer_keep(shift_whole, shift_frac, solid_blocks)

    def buffers(more):
        return [f32(z.slots(d) + more, depth, width) for d in range(1, count)]

    def call(body, ins, outs, scratch=(), direct=(), alias=None):
        specs = [outside if k in direct else vmem for k in range(len(outs))]
        return pl.pallas_call(
            functools.partial(body, z),
            out_shape=outs,
            in_specs=ins,
            out_specs=specs,
            scratch_shapes=list(scratch),
            input_output_aliases=alias or {},
            compiler_params=pltpu.CompilerParams(vmem_limit_bytes=8 << 20),
        )

    def swap_x(values):
        return [
            lax.ppermute(values[d - 1], "gx", [(i, i ^ d) for i in range(count)])
            for d in range(1, count)
        ]

    pairs = [(i, i ^ 1) for i in range(ranks)]
    across = [(i, (i - 1 if i % 2 == 0 else i + 1) % ranks) for i in range(ranks)]

    (pop,) = outer_keep(pop_ratio.reshape(cells.shape))
    mask_shape = f32(planes // BLOCK * z.deep, width)
    loaded, mask, info, *sends = call(
        first_kernel,
        [outside] * 4,
        [cells, mask_shape, f32(2 * shift_whole.shape[0], width)] + buffers(0),
        [pair, pair, pltpu.VMEM(solid_blocks.shape, jnp.int32), sems(LOADS + 3)],
    )(shift_whole, shift_frac, pop, solid_blocks)
    post, old = call(collide_kernel, [vmem] * 2, [cells, fields])(*keep(loaded, mask))
    gets = swap_x(sends)
    walls, both = f32(2 * len(rising), depth, width), f32(2, depth, width)
    inner, outer, wall, side = call(
        second_kernel,
        [vmem] * (2 + count),
        [halo, halo, walls, both],
        shifts + [f32(2, Q, planes, width), f32(2, width, depth)],
    )(*keep(info, post, mask, *gets))
    outer = lax.ppermute(outer, "gz", across)
    inner = lax.ppermute(inner, "gz", pairs)
    (h,) = call(bulk_kernel, [vmem] * 3, [cells])(*keep(post, wall, side))
    g, acc = call(middle_kernel, [vmem] * 3, [cells, fields])(*keep(h, mask, old))
    g, acc, own, *sends = call(
        third_kernel,
        [vmem] * 8,
        [cells, fields, f32(depth, width)] + buffers(1),
        [pltpu.VMEM((2, SLOTS, planes, width), jnp.float32)],
        alias={6: 0, 7: 1},
    )(*keep(info, h, inner, outer, mask, old, g, acc))
    gets = swap_x(sends)
    turned = f32(len(slanted), planes * depth, width)
    out, acc, turned = call(
        direct_kernel,
        [vmem] * 2,
        [hbm(cells), hbm(fields), turned],
        [sems(len(straight) + 1)],
        [0, 1],
    )(*keep(g, acc))
    moves = 1 + len(SPANS) * CHUNKS + sum(CX[i] == 0 for i in rising + falling)
    out, profile = call(
        fourth_kernel,
        [vmem] * (3 + count) + [outside],
        [hbm(cells), hbm(f32(2, depth, planes))],
        shifts + [cells, f32(2, depth, planes), sems(moves)],
        [0, 1],
        {3 + count: 0},
    )(*keep(info, g, turned, own, *gets), out)
    return (
        out.reshape(pop_ratio.shape),
        acc.reshape(2, planes, depth, width),
        jnp.swapaxes(profile, 1, 2),
    )


def solution(mesh):
    return jax.shard_map(
        functools.partial(local, mesh.shape["gx"], mesh.shape["gz"]),
        mesh=mesh,
        in_specs=(P(None, None, "gz", "gx"), P(None, "gz", "gx"), P(), P()),
        out_specs=(P(None, None, "gz", "gx"), P(None, None, "gz", "gx"), P(None, None, "gz")),
        check_vma=False,
    )
```
